32 devices in a mesh: groups: 2 (over y), ctx: 4 (over z), tp: 2 (over x), sub: 2 (over core).
Axes of the slice: x: 2, y: 2, z: 4, core: 2. Of those that a mesh axis runs over, the one named last changes fastest.
Arguments:
- x_input: bfloat16 [4096, 8192], P(('groups', 'ctx', 'sub'), 'tp'), parts along dimension 0, may hold values from -48 to 48
- gate_input: bfloat16 [4096, 8192], P(('groups', 'ctx', 'sub'), 'tp'), parts along dimension 0, may hold values from -6 to 6
- state_proj: bfloat16 [4096, 8, 2, 128], P(('groups', 'ctx', 'sub'), 'tp'), parts along dimension 0, may hold values from -2.5 to 2.5
- mix_weight: bfloat16 [4, 8192], P(None, 'tp'), may hold values from -3 to 3
- mix_bias: float32 [8192], P('tp'), may hold values from -3 to 3
- state_weight: bfloat16 [4, 8, 2, 128], P(None, 'tp'), may hold values from -3 to 3
- state_bias: float32 [8, 2, 128], P('tp'), may hold values from -2.5 to 2.5
- step_raw: float32 [4096, 128], P(('groups', 'ctx', 'sub'), 'tp'), parts along dimension 0, may hold values from -4.5 to 50
- decay_log: float32 [128], P('tp'), may hold values from -5.3 to 0.41
- skip_gain: float32 [128], P('tp'), may hold values from 0.5 to 1.5
- norm_gain: float32 [8192], P('tp'), may hold values from 0.5 to 1.5
- out_weight: bfloat16 [8192, 4096], P(('tp', 'sub')), may hold values from -0.0625 to 0.0625
- doc_lengths: int32 [16], P('groups'), parts along dimension 0, may hold values from 1 to 1024, 2048 in all
Outputs:
- output: bfloat16 [4096, 4096], P(('groups', 'ctx', 'sub'), 'tp'), parts along dimension 0
The draws below stay inside these ranges and needn't reach their ends.
There are 2 independent parts, one for each index of `groups`. The reference program is written for one: setup_inputs(seed, part) draws one part's arguments, and reference() takes and returns one part's arrays. A program takes and returns all parts, laid end to end along the dimension named above; an argument that names none is the same for every part. Nothing has to cross between parts.
Inputs may be any that keep to these rules, and one draw needn't show every extreme that they name: `doc_lengths`: documents lie end to end from position 0 in the given order; the largest has exactly 1024 positions.
All inputs are finite; a program needn't handle non-finite values.
Results may differ from the reference program's by a relative error of at most 0.0095.
Values may be sent and summed in bfloat16 or wider, within the bound.
No kernel may reach another device: no remote copies, remote signals or barrier semaphores. Data moves between devices by JAX's collectives and lax.ppermute only.
A program may use at most 192 MiB of HBM per device.

```python
import math
from functools import partial
import jax
import jax.numpy as jnp
import numpy as np
from jax import lax

HEADS = 128
HEAD_DIM = 64
STATE = 128
GROUPS = 8
KERNEL = 4
FEATURES = 4096
BLOCK = 128
INNER = 8192
PACKED_TOKENS = 2048
DOCS = 8


def draw_x_input(key, part):
    random_subkeys = jax.random.split(key, 4)
    head_ids = jnp.arange(HEADS)
    per_group = HEADS // GROUPS
    head_trend = (head_ids % per_group).astype(jnp.float32) / max(per_group - 1, 1) - 0.5
    head_scale = jnp.exp(math.log(3.0) * head_trend + 1.2 * (jax.random.uniform(random_subkeys[0], (HEADS,)) - 0.5))
    columns = jnp.repeat(head_scale, HEAD_DIM)
    row_scale = jnp.exp(jax.random.uniform(random_subkeys[1], (PACKED_TOKENS, 1), minval=0.0, maxval=math.log(10.0))) / math.sqrt(10.0)
    values = jnp.clip(jax.random.normal(random_subkeys[3], (PACKED_TOKENS, INNER)), -4.0, 4.0)
    return (values * row_scale * columns[None, :]).astype(jnp.bfloat16)


def draw_step_raw(key, part):
    random_subkeys = jax.random.split(key, 4)
    base_size = jnp.exp(jax.random.uniform(random_subkeys[0], (PACKED_TOKENS, HEADS), minval=math.log(0.02), maxval=math.log(0.1)))
    block_count = PACKED_TOKENS // BLOCK
    block_factor = jnp.exp(jax.random.uniform(random_subkeys[1], (block_count, 1, HEADS), minval=-0.5, maxval=0.5))
    delta_stride = (base_size.reshape(block_count, BLOCK, HEADS) * block_factor).reshape(PACKED_TOKENS, HEADS)
    surge_positions = jax.random.randint(random_subkeys[2], (3,), 0, PACKED_TOKENS)
    surge_marker = jnp.any(jnp.arange(PACKED_TOKENS)[:, None] == surge_positions[None, :], axis=1)
    surge_magnitude = jax.random.uniform(random_subkeys[3], (PACKED_TOKENS, 1), minval=20.0, maxval=50.0)
    delta_stride = jnp.where(surge_marker[:, None], surge_magnitude, delta_stride)
    return (delta_stride + jnp.log(-jnp.expm1(-delta_stride))).astype(jnp.float32)


def draw_decay_log(key, part):
    random_subkeys = jax.random.split(key, 3)
    slow_share = 0.5
    slow_flag = jax.random.uniform(random_subkeys[0], (HEADS,)) < slow_share
    slow_rate = jax.random.uniform(random_subkeys[1], (HEADS,), minval=math.log(0.005), maxval=math.log(0.015))
    fast_rate = jax.random.uniform(random_subkeys[2], (HEADS,), minval=math.log(0.5), maxval=math.log(1.5))
    return jnp.where(slow_flag, slow_rate, fast_rate).astype(jnp.float32)


def shard_levels(rng, shape, cuts, least, high):
    loudness, own = 1.0, jax.random.fold_in(rng, 6)
    for axis_at, parts in cuts:
        heights = jnp.exp(jax.random.uniform(jax.random.fold_in(own, axis_at), (parts,), jnp.float32, least / len(cuts), high / len(cuts)))
        loudness = loudness * jnp.repeat(heights, shape[axis_at] // parts).reshape([-1 if axis == axis_at else 1 for axis in range(len(shape))])
    return loudness


def length_profile(amount, total, reach, skew):
    portions = [(1 << 20) // math.isqrt(standing ** skew) + 1 for standing in range(2, amount + 1)]
    rest, holding = total - reach - (amount - 1), [1] * (amount - 1)
    while rest > 0:
        free = [i for i in range(amount - 1) if holding[i] < reach]
        mass, budget = sum([portions[i] for i in free]), rest
        for i in free:
            extra = min(reach - holding[i], max(1, budget * portions[i] // mass), rest)
            holding[i] = holding[i] + extra
            rest = rest - extra
    return np.array([reach] + holding)


def ragged_sizes(own_key, number_of, total, reach, lean):
    if number_of == 2:
        one = jax.random.randint(own_key, (), max(1, total - reach), min(reach, total - 1) + 1)
        return jnp.stack([one, total - one])
    lengths = jnp.asarray(length_profile(number_of, total, reach, lean), jnp.int32)
    pairs = (number_of - 1) // 2
    donor, taker = lengths[1:1 + 2 * pairs:2], lengths[2:2 + 2 * pairs:2]
    slack = jnp.minimum(donor - 1, reach - taker)
    shifted = jax.random.randint(jax.random.fold_in(own_key, 1), (pairs,), 0, 1 << 20) % (slack + 1)
    lengths = lengths.at[1:1 + 2 * pairs:2].set(donor - shifted).at[2:2 + 2 * pairs:2].set(taker + shifted)
    return lengths[jax.random.permutation(jax.random.fold_in(own_key, 2), number_of)]


def noise(rng, extent, scale, reach, shards=(), kind=jnp.bfloat16):
    factor_of = shard_levels(rng, extent, shards, -0.22, 0.18) if shards else 1.0
    result = jax.random.normal(rng, extent, jnp.float32) * scale * factor_of
    return jnp.minimum(jnp.maximum(result, -reach), reach).astype(kind)


def setup_inputs(seed: int = 0, part: int = 0) -> dict:
    splits = jax.random.split(jax.random.key(seed), 14)
    part_splits = jax.random.split(jax.random.fold_in(splits[13], part), 14)
    return {
        "x_input": draw_x_input(jax.random.fold_in(jax.random.fold_in(splits[13], part), 71), part),
        "gate_input": noise(part_splits[1], (PACKED_TOKENS, INNER), 1.0, 6.0, ((0, 8), (1, 2))),
        "state_proj": noise(part_splits[2], (PACKED_TOKENS, GROUPS, 2, STATE), 0.3, 2.5, ((0, 8), (1, 2))),
        "mix_weight": noise(splits[3], (KERNEL, INNER), KERNEL ** -0.5, 3.0, ((1, 2),)),
        "mix_bias": noise(splits[4], (INNER,), 0.5, 3.0, ((0, 2),), jnp.float32),
        "state_weight": noise(splits[5], (KERNEL, GROUPS, 2, STATE), KERNEL ** -0.5, 3.0, ((1, 2),)),
        "state_bias": noise(splits[6], (GROUPS, 2, STATE), 0.3, 2.5, ((0, 2),), jnp.float32),
        "step_raw": draw_step_raw(jax.random.fold_in(jax.random.fold_in(splits[13], part), 71), part),
        "decay_log": draw_decay_log(jax.random.fold_in(splits[13], 71), part),
        "skip_gain": jnp.clip(0.5 + 1.0 * jax.random.uniform(splits[9], (HEADS,), jnp.float32) ** shard_levels(splits[9], (HEADS,), ((0, 2),), -0.2, 0.2), 0.5, 1.5),
        "norm_gain": jnp.clip(0.5 + 1.0 * jax.random.uniform(splits[10], (INNER,), jnp.float32) ** shard_levels(splits[10], (INNER,), ((0, 2),), -0.2, 0.2), 0.5, 1.5),
        "out_weight": noise(splits[11], (INNER, FEATURES), INNER ** -0.5, 0.0625, ((0, 4),)),
        "doc_lengths": ragged_sizes(part_splits[12], DOCS, PACKED_TOKENS, PACKED_TOKENS // 2, 2).astype(jnp.int32),
    }


highest = lax.Precision.HIGHEST
epsilon = 1e-05

def doc_index(positions, doc_lengths):
    starts = (jnp.cumsum(doc_lengths) - doc_lengths).astype(jnp.int32)
    counted = lax.optimization_barrier(jnp.sum((starts[None, :] <= positions[:, None]).astype(jnp.int32), axis=1))
    return (counted - 1).astype(jnp.int32)

def causal_mix(padded, padded_ids, doc_ids, weight, bias_term):
    length = doc_ids.shape[0]
    tap_count = weight.shape[0]
    summed = jnp.broadcast_to(bias_term.astype(jnp.float32), padded[tap_count - 1:].shape)
    for offset in range(tap_count):
        window = padded[offset:offset + length].astype(jnp.float32)
        matches = (padded_ids[offset:offset + length] == doc_ids).reshape((length,) + (1,) * (window.ndim - 1))
        summed = summed + jnp.where(matches, window * weight[offset].astype(jnp.float32), 0.0)
    return jax.nn.silu(summed).astype(jnp.bfloat16)

def block_step(state_in, pieces, head_group):
    values, b_group, c_group, log_decay, doc_ids, doc_prior = pieces
    length = doc_ids.shape[0]
    cumulative = jnp.cumsum(log_decay, axis=0)
    places = jnp.arange(length)
    causal = (doc_ids[:, None] == doc_ids[None, :]) & (places[:, None] >= places[None, :])
    spread = jnp.minimum(cumulative[:, None, :] - cumulative[None, :, :], 0.0)
    weights = jnp.where(causal[:, :, None], jnp.exp(spread), 0.0)
    scores = jnp.einsum('ign,jgn->gij', c_group, b_group, precision=highest)
    scores = jnp.einsum('hg,gij->ijh', head_group, scores, precision=highest) * weights
    within = jnp.einsum('ijh,jhp->ihp', scores, values, precision=highest)
    output_coefficient_heads = jnp.einsum('hg,ign->ihn', head_group, c_group, precision=highest)
    b_heads = jnp.einsum('hg,jgn->jhn', head_group, b_group, precision=highest)
    reach_decay = jnp.where((doc_ids == doc_prior)[:, None], jnp.exp(cumulative), 0.0)
    carried = jnp.einsum('ihn,hpn->ihp', output_coefficient_heads, state_in, precision=highest) * reach_decay[:, :, None]
    tail_decay = jnp.where((doc_ids == doc_ids[-1])[:, None], jnp.exp(cumulative[-1][None, :] - cumulative), 0.0)
    fresh_part = jnp.einsum('jhp,jhn->hpn', values * tail_decay[:, :, None], b_heads, precision=highest)
    kept_part = jnp.where(doc_ids[-1] == doc_prior, jnp.exp(cumulative[-1]), 0.0)
    state_out = kept_part[:, None, None] * state_in + fresh_part
    return (state_out, within + carried)

def reference(x_input, gate_input, state_proj, mix_weight, mix_bias, state_weight, state_bias, step_raw, decay_log, skip_gain, norm_gain, out_weight, doc_lengths):
    tokens = x_input.shape[0]
    positions = jnp.arange(tokens, dtype=jnp.int32)
    doc_ids = doc_index(positions, doc_lengths)
    prior_ids = doc_index(jnp.arange(1 - KERNEL, 0, dtype=jnp.int32), doc_lengths)
    padded_ids = jnp.concatenate([prior_ids, doc_ids])
    x_padded = jnp.concatenate([jnp.zeros((KERNEL - 1, INNER), jnp.bfloat16), x_input])
    x_mixed = causal_mix(x_padded, padded_ids, doc_ids, mix_weight, mix_bias)
    sequence_padded = jnp.concatenate([jnp.zeros((KERNEL - 1,) + state_proj.shape[1:], jnp.bfloat16), state_proj])
    state_mixed = causal_mix(sequence_padded, padded_ids, doc_ids, state_weight, state_bias)
    step_sizes = jax.nn.softplus(step_raw)
    log_decay = -jnp.exp(decay_log)[None, :] * step_sizes
    x_heads = x_mixed.astype(jnp.float32).reshape(tokens, HEADS, HEAD_DIM)
    values = x_heads * step_sizes[:, :, None]
    b_all = state_mixed[:, :, 0].astype(jnp.float32)
    c_all = state_mixed[:, :, 1].astype(jnp.float32)
    head_group = (jnp.arange(HEADS)[:, None] // (HEADS // GROUPS) == jnp.arange(GROUPS)[None, :]).astype(jnp.float32)
    block_count = tokens // BLOCK
    block_priors = jnp.concatenate([jnp.array([-1], jnp.int32), doc_ids[BLOCK - 1:tokens - 1:BLOCK]])
    pieces = (values.reshape(block_count, BLOCK, HEADS, HEAD_DIM), b_all.reshape(block_count, BLOCK, GROUPS, STATE), c_all.reshape(block_count, BLOCK, GROUPS, STATE), log_decay.reshape(block_count, BLOCK, HEADS), doc_ids.reshape(block_count, BLOCK), block_priors)
    zero_state = jnp.zeros((HEADS, HEAD_DIM, STATE), jnp.float32)
    final_state, scan_blocks = lax.scan(partial(block_step, head_group=head_group), zero_state, pieces)
    scan_out = scan_blocks.reshape(tokens, HEADS, HEAD_DIM)
    gate_act = jax.nn.silu(gate_input.astype(jnp.float32)).reshape(tokens, HEADS, HEAD_DIM)
    gated_out = (scan_out + skip_gain[None, :, None] * x_heads) * gate_act
    grouped = gated_out.reshape(tokens, GROUPS, INNER // GROUPS)
    mean_square = lax.optimization_barrier(jnp.mean(grouped * grouped, axis=2, keepdims=True))
    hidden = ((grouped * lax.rsqrt(mean_square + epsilon)).reshape(tokens, INNER) * norm_gain[None, :]).astype(jnp.bfloat16)
    return jnp.dot(hidden, out_weight, preferred_element_type=jnp.float32).astype(jnp.bfloat16)
```

```python
import functools

import jax
import jax.numpy as jnp
from jax import lax
from jax.experimental import pallas as pl
from jax.experimental.pallas import tpu as pltpu
from jax.sharding import PartitionSpec as P

HEADS = 128
GROUPS = 8
CHUNK = 128
EPSILON = 1e-05
LOG2E = 1.4426950408889634
MASKED = -1e30
F32 = jnp.float32
BF16 = jnp.bfloat16


def shifted(shard, axis, by):
    peers = lax.axis_size(axis)
    pairs = [(i, i + by) for i in range(peers) if 0 <= i + by < peers]
    return lax.ppermute(shard, axis, pairs)


def swapped(shard, axis):
    return lax.ppermute(shard, axis, [(i, i ^ 1) for i in range(lax.axis_size(axis))])


def doc_start(positions, docs_ref):
    start = jnp.zeros_like(positions)
    total = jnp.int32(0)
    for doc in range(docs_ref.shape[0]):
        start = jnp.where(positions >= total, total, start)
        total = total + docs_ref[doc]
    return start


def rows_of(count, first):
    return first + lax.broadcasted_iota(jnp.int32, (count, 1), 0)


def split2(value):
    high = value.astype(BF16)
    return high, (value - high.astype(F32)).astype(BF16)


def split3(value):
    high = value.astype(BF16)
    rest = value - high.astype(F32)
    mid = rest.astype(BF16)
    return high, mid, (rest - mid.astype(F32)).astype(BF16)


def mm(a, b):
    return jnp.dot(a, b, preferred_element_type=F32)


def contract_rows(a, b):
    return lax.dot_general(a, b, (((0,), (0,)), ((), ())), preferred_element_type=F32)


def contract_lanes(a, b):
    return lax.dot_general(a, b, (((1,), (1,)), ((), ())), preferred_element_type=F32)


def silu(value):
    half = 0.5 * value
    return half + half * jnp.tanh(half)


def head_lanes(heads, head_width, lanes, first_lane):
    head = lax.broadcasted_iota(jnp.int32, (heads, lanes), 0)
    lane = first_lane + lax.broadcasted_iota(jnp.int32, (heads, lanes), 1)
    low = head * head_width
    return jnp.where((lane >= low) & (lane < low + head_width), 1.0, 0.0).astype(BF16)


def conv_kernel(meta, docs, x, x_rim, w, bias, s, s_rim, sw, sbias, out, shift, rim_shift, *, taps):
    step, last = pl.program_id(0), pl.num_programs(0) - 1
    count = x.shape[0]
    rims = x_rim.shape[0]

    @pl.when(step == 0)
    def _():
        start = doc_start(rows_of(count, meta[0]), docs) - meta[0]
        row = lax.broadcasted_iota(jnp.int32, (count, count), 0)
        col = lax.broadcasted_iota(jnp.int32, (count, count), 1)
        rim_row = lax.broadcasted_iota(jnp.int32, (rims, rims), 0)
        rim_col = lax.broadcasted_iota(jnp.int32, (rims, rims), 1) - rims
        for back in range(1, taps):
            hit = (col == row - back) & (col >= start)
            shift[back - 1] = jnp.where(hit, 1.0, 0.0).astype(BF16)
            rim_hit = (rim_col == rim_row - back) & (rim_col >= start[:rims])
            rim_shift[back - 1] = jnp.where(rim_hit, 1.0, 0.0).astype(BF16)

    def mix(x_part, rim_part, w_part, bias_part):
        value = x_part[...]
        rim = rim_part[...]
        weight = w_part[...].astype(F32)
        summed = bias_part[...] + value.astype(F32) * weight[taps - 1 : taps]
        top = jnp.zeros((rims, value.shape[1]), F32)
        for back in range(1, taps):
            row = weight[taps - 1 - back : taps - back]
            summed = summed + mm(shift[back - 1], value) * row
            top = top + mm(rim_shift[back - 1], rim) * row
        out[:rims, :] = silu(summed[:rims] + top).astype(BF16)
        out[rims:, :] = silu(summed[rims:]).astype(BF16)

    @pl.when(step < last)
    def _():
        mix(x, x_rim, w, bias)

    @pl.when(step == last)
    def _():
        mix(s, s_rim, sw, sbias)


def conv_half(meta, docs, x, x_rim, w, bias, s, s_rim, sw, sbias, width, block):
    count = x.shape[0]
    taps = w.shape[0]
    rims = x_rim.shape[0]
    steps = width // block
    x_at = lambda i, m, d: (0, m[1] * steps + jnp.minimum(i, steps - 1))
    s_at = lambda i, m, d: (0, m[2])
    specs = []
    for at in (x_at, s_at):
        for rows in (count, rims, taps, 1):
            specs.append(pl.BlockSpec((rows, block), at))
    return pl.pallas_call(
        functools.partial(conv_kernel, taps=taps),
        grid_spec=pltpu.PrefetchScalarGridSpec(
            num_scalar_prefetch=2,
            grid=(steps + 1,),
            in_specs=specs,
            out_specs=pl.BlockSpec((count, block), lambda i, m, d: (0, i)),
            scratch_shapes=[
                pltpu.VMEM((taps - 1, count, count), BF16),
                pltpu.VMEM((taps - 1, rims, rims), BF16),
            ],
        ),
        out_shape=jax.ShapeDtypeStruct((count, width + block), BF16),
        compiler_params=pltpu.CompilerParams(vmem_limit_bytes=32 << 20),
        cost_estimate=pl.CostEstimate(
            flops=8 * count * width, bytes_accessed=4 * count * (width + block), transcendentals=count * width
        ),
        name="conv",
    )(meta, docs, x, x_rim, w, bias, s, s_rim, sw, sbias)


def state_kernel(
    meta, docs, own, got, own_bc, got_bc, own_raw, got_raw, rate,
    x_out, bc_out, s_out, d_out, cum_out, dlt_out, raw, weight,
    *, head_width, group_width, state_width,
):
    step = pl.program_id(0)
    half = own.shape[0]
    count = 2 * half
    heads = raw.shape[1]
    width = own.shape[1]
    own_at = pl.ds(pl.multiple_of(meta[0] * half, half), half)
    got_at = pl.ds(pl.multiple_of((1 - meta[0]) * half, half), half)
    first = meta[1]
    last_start = doc_start(first + count - 1, docs)

    @pl.when(step == 0)
    def _():
        bc_out[own_at, :] = own_bc[...]
        bc_out[got_at, :] = got_bc[...]
        raw[own_at, :] = own_raw[...]
        raw[got_at, :] = got_raw[...]
        value = raw[...]
        size = jnp.maximum(value, 0.0) + jnp.log(1.0 + jnp.exp(-jnp.abs(value)))
        decay = (-LOG2E * jnp.exp(rate[...])) * size
        row = lax.broadcasted_iota(jnp.int32, (count, count), 0)
        col = lax.broadcasted_iota(jnp.int32, (count, count), 1)
        below = jnp.where(col <= row, 1.0, 0.0).astype(BF16)
        high, mid, low = split3(decay)
        cum = mm(below, high) + (mm(below, mid) + mm(below, low))
        cum_out[...] = cum
        dlt_out[...] = (cum - jnp.log2(size)).T
        end = cum[count - 1 :]
        tail = jnp.where(rows_of(count, first) >= last_start, size * jnp.exp2(end - cum), 0.0)
        high, low = split2(tail)
        weight[0] = high
        weight[1] = low

    x_out[own_at, :] = own[...]
    x_out[got_at, :] = got[...]
    spread = head_lanes(heads, head_width, width, step * width)
    group = (step * width) // group_width
    b = bc_out[:, pl.ds(pl.multiple_of(group * 2 * state_width, state_width), state_width)]
    tails = mm(weight[0], spread) + mm(weight[1], spread)
    weighted = (x_out[...].astype(F32) * tails).astype(BF16)
    s_out[...] = contract_rows(b, weighted).astype(BF16)
    kept = jnp.exp2(jnp.broadcast_to(cum_out[count - 1 :, :], (8, heads)))
    high, mid, low = split3(jnp.where(last_start < first, kept, 0.0))
    d_out[...] = mm(high, spread) + (mm(mid, spread) + mm(low, spread))


def intra_kernel(
    meta, docs, x, bc, cum, dlt, gate_own, gate_got, skip,
    a_out, f_out, state, base, spread, reach, into, tail,
    *, head_width, group_heads, state_width,
):
    step = pl.program_id(0)
    count, width = x.shape
    heads = cum.shape[1]
    first = meta[1] + step * count

    @pl.when(step == 0)
    def _():
        state[...] = jnp.zeros_like(state)
        base[...] = jnp.zeros_like(base)
        spread[...] = head_lanes(heads, head_width, width, 0)

    starts = doc_start(rows_of(count, first), docs)
    last_start = doc_start(first + count - 1, docs)
    here = cum[...]
    before = base[:1, :]
    end = here[count - 1 :]
    lanes = spread[...]

    def spread_over(value):
        high, low = split2(value)
        return mm(high, lanes) + mm(low, lanes)

    reach[...] = spread_over(jnp.where(starts < first, jnp.exp2(here - before), 0.0))
    into[...] = spread_over(jnp.where(starts < meta[1], jnp.exp2(here), 0.0))
    to_end = jnp.exp2(end - dlt[...].T)
    tail[...] = spread_over(jnp.where(rows_of(count, first) >= last_start, to_end, 0.0))
    kept = jnp.broadcast_to(jnp.where(last_start < first, jnp.exp2(end - before), 0.0), (8, heads))
    high, mid, low = split3(kept)
    kept = (mm(high, lanes) + (mm(mid, lanes) + mm(low, lanes)))[:1]
    row = lax.broadcasted_iota(jnp.int32, (count, count), 0)
    col = lax.broadcasted_iota(jnp.int32, (count, count), 1)
    mask = jnp.where((col <= row) & (col >= starts - first), 0.0, MASKED)
    is_own = (step * count) // (count * (pl.num_programs(0) // 2)) == meta[0]
    low_lanes = lax.broadcasted_iota(jnp.int32, (count, 2 * head_width), 1) < head_width
    zero = jnp.zeros((count, 2 * head_width), BF16)
    for group in range(heads // group_heads):
        b = bc[:, group * 2 * state_width : (group * 2 + 1) * state_width]
        c = bc[:, (group * 2 + 1) * state_width : (group * 2 + 2) * state_width]
        scores = contract_lanes(c, b)
        for head in range(group * group_heads, (group + 1) * group_heads, 2):
            at = slice(head * head_width, (head + 2) * head_width)
            pair = []
            for k in (head, head + 1):
                exponent = (here[:, k : k + 1] - dlt[k : k + 1, :]) + mask
                pair.append((jnp.exp2(exponent) * scores).astype(BF16))
            value = x[:, at]
            stacked = jnp.concatenate([jnp.where(low_lanes, value, zero), jnp.where(low_lanes, zero, value)], axis=0)
            within = mm(jnp.concatenate(pair, axis=1), stacked)
            old = state[:, at]
            carried = mm(c, old.astype(BF16)) * reach[:, at]
            x_part = value.astype(F32)
            y = within + carried + x_part * skip[:, at]
            gate = silu(jnp.where(is_own, gate_own[:, at], gate_got[:, at]).astype(F32))
            a_out[:, at] = y * gate
            f_out[:, at] = gate * into[:, at]
            fresh = contract_rows(b, (x_part * tail[:, at]).astype(BF16))
            state[:, at] = old * kept[:, at] + fresh
    base[...] = jnp.broadcast_to(end, base.shape)


def project_kernel(
    meta, a, f, bc, incoming, gain, squares, w, hidden, send, keep,
    *, row_steps, group_width, state_width, divisor,
):
    step = pl.program_id(0)
    count = a.shape[0]
    width = a.shape[1]
    half = send.shape[0]

    @pl.when(step < row_steps)
    def _():
        at = pl.ds(pl.multiple_of(step * count, count), count)
        for group in range(width // group_width):
            lanes = slice(group * group_width, (group + 1) * group_width)
            c = bc[:, (group * 2 + 1) * state_width : (group * 2 + 2) * state_width]
            gated = a[:, lanes] + mm(c, incoming[:, lanes]) * f[:, lanes]
            if squares is None:
                total = jnp.sum(gated * gated, axis=1, keepdims=True)
            else:
                total = squares[...]
            scale = lax.rsqrt(total / divisor + EPSILON)
            hidden[at, lanes] = (gated * scale * gain[:, lanes]).astype(BF16)

    @pl.when(step >= row_steps)
    def _():
        there = pl.ds(pl.multiple_of((1 - meta[0]) * half, half), half)
        here = pl.ds(pl.multiple_of(meta[0] * half, half), half)
        send[...] = mm(hidden[there, :], w[...]).astype(BF16)
        keep[...] = mm(hidden[here, :], w[...])


def product_kernel(meta, hidden, w, send, keep):
    half = send.shape[0]
    there = pl.ds(pl.multiple_of((1 - meta[0]) * half, half), half)
    here = pl.ds(pl.multiple_of(meta[0] * half, half), half)
    send[...] = mm(hidden[there, :], w[...]).astype(BF16)
    keep[...] = mm(hidden[here, :], w[...])


def padded_rim(shard, rims):
    return jnp.concatenate([jnp.zeros((rims - shard.shape[0],) + shard.shape[1:], shard.dtype), shard])


def local(
    x_input, gate_input, state_proj, mix_weight, mix_bias, state_weight, state_bias,
    step_raw, decay_log, skip_gain, norm_gain, out_weight, doc_lengths,
):
    half, channels = x_input.shape
    all_heads = step_raw.shape[1]
    groups, _, state_width = state_proj.shape[1:]
    taps = mix_weight.shape[0]
    features = out_weight.shape[1]
    head_width = channels // all_heads
    heads = all_heads // 2
    width = channels // 2
    count = 2 * half
    whole_groups = groups % 2 == 0
    my_groups = groups // 2 if whole_groups else groups
    group_heads = heads // my_groups
    group_width = group_heads * head_width
    block = my_groups * 2 * state_width
    sub = lax.axis_index("sub").astype(jnp.int32)
    ctx = lax.axis_index("ctx").astype(jnp.int32)
    tp = lax.axis_index("tp").astype(jnp.int32)
    tp_size = lax.axis_size("tp")
    ctx_size = lax.axis_size("ctx")
    block_first = ctx * count
    docs = doc_lengths.astype(jnp.int32)
    zero = jnp.int32(0)

    s_input = state_proj.reshape(half, groups * 2 * state_width)
    s_weight = state_weight.reshape(taps, groups * 2 * state_width)
    s_bias = state_bias.reshape(1, groups * 2 * state_width)
    rims = 16
    x_rim, s_rim = shifted(
        (padded_rim(x_input[half - taps + 1 :], rims), padded_rim(s_input[half - taps + 1 :], rims)),
        ("ctx", "sub"),
        1,
    )
    own_raw = lax.dynamic_slice_in_dim(step_raw, sub * heads, heads, 1)
    got_raw = swapped(lax.dynamic_slice_in_dim(step_raw, (1 - sub) * heads, heads, 1), "sub")
    conv = functools.partial(
        conv_half, docs=docs, x=x_input, x_rim=x_rim, w=mix_weight, bias=mix_bias.reshape(1, channels),
        s=s_input, s_rim=s_rim, sw=s_weight, sbias=s_bias, width=width, block=block,
    )
    first = block_first + sub * half
    other = conv(jnp.stack([first, 1 - sub, 1 - sub if whole_groups else zero]))
    got = swapped(other, "sub")
    own = conv(jnp.stack([first, sub, sub if whole_groups else zero]))
    got_gate = swapped(lax.dynamic_slice_in_dim(gate_input, (1 - sub) * width, width, 1), "sub")

    meta = jnp.stack([sub, block_first, tp])
    cols = min(512, group_width)
    steps = width // cols
    rate = lax.dynamic_slice_in_dim(decay_log, sub * heads, heads, 0).reshape(1, heads)
    fixed = lambda *shape: pl.BlockSpec(shape, lambda i, *m: (0,) * len(shape))
    x_cat, bc, state, kept, cum, dlt = pl.pallas_call(
        functools.partial(
            state_kernel, head_width=head_width, group_width=group_width, state_width=state_width
        ),
        grid_spec=pltpu.PrefetchScalarGridSpec(
            num_scalar_prefetch=2,
            grid=(steps,),
            in_specs=[
                pl.BlockSpec((half, cols), lambda i, *m: (0, i)),
                pl.BlockSpec((half, cols), lambda i, *m: (0, i)),
                pl.BlockSpec((half, block), lambda i, *m: (0, width // block)),
                pl.BlockSpec((half, block), lambda i, *m: (0, width // block)),
                fixed(half, heads),
                fixed(half, heads),
                fixed(1, heads),
            ],
            out_specs=[
                pl.BlockSpec((count, cols), lambda i, *m: (0, i)),
                fixed(count, block),
                pl.BlockSpec((state_width, cols), lambda i, *m: (0, i)),
                pl.BlockSpec((8, cols), lambda i, *m: (0, i)),
                fixed(count, heads),
                fixed(heads, count),
            ],
            scratch_shapes=[pltpu.VMEM((count, heads), F32), pltpu.VMEM((2, count, heads), BF16)],
        ),
        out_shape=[
            jax.ShapeDtypeStruct((count, width), BF16),
            jax.ShapeDtypeStruct((count, block), BF16),
            jax.ShapeDtypeStruct((state_width, width), BF16),
            jax.ShapeDtypeStruct((8, width), F32),
            jax.ShapeDtypeStruct((count, heads), F32),
            jax.ShapeDtypeStruct((heads, count), F32),
        ],
        compiler_params=pltpu.CompilerParams(vmem_limit_bytes=32 << 20),
        cost_estimate=pl.CostEstimate(
            flops=4 * count * width * state_width, bytes_accessed=5 * count * width, transcendentals=count * heads
        ),
        name="state",
    )(meta, docs, own, got, own, got, own_raw, got_raw, rate)

    arriving = jnp.zeros_like(state)
    for hop in range(ctx_size // 2):
        leaving = state
        if hop:
            leaving = (state.astype(F32) + kept[:1] * arriving.astype(F32)).astype(BF16)
        arriving = shifted(leaving, "ctx", 1)

    chunks = count // CHUNK
    skip = jnp.repeat(lax.dynamic_slice_in_dim(skip_gain, sub * heads, heads, 0), head_width).reshape(1, width)
    by_row = lambda n: pl.BlockSpec((CHUNK, n), lambda i, *m: (i, 0))
    gated, carry_gate = pl.pallas_call(
        functools.partial(
            intra_kernel, head_width=head_width, group_heads=group_heads, state_width=state_width
        ),
        grid_spec=pltpu.PrefetchScalarGridSpec(
            num_scalar_prefetch=2,
            grid=(chunks,),
            in_specs=[
                by_row(width),
                by_row(block),
                by_row(heads),
                pl.BlockSpec((heads, CHUNK), lambda i, *m: (0, i)),
                pl.BlockSpec((CHUNK, width), lambda i, m, d: (lax.rem(i, chunks // 2), m[0])),
                pl.BlockSpec((CHUNK, width), lambda i, m, d: (lax.rem(i, chunks // 2), 0)),
                fixed(1, width),
            ],
            out_specs=[by_row(width), by_row(width)],
            scratch_shapes=[
                pltpu.VMEM((state_width, width), F32),
                pltpu.VMEM((8, heads), F32),
                pltpu.VMEM((heads, width), BF16),
                pltpu.VMEM((CHUNK, width), F32),
                pltpu.VMEM((CHUNK, width), F32),
                pltpu.VMEM((CHUNK, width), F32),
            ],
        ),
        out_shape=[jax.ShapeDtypeStruct((count, width), F32), jax.ShapeDtypeStruct((count, width), F32)],
        compiler_params=pltpu.CompilerParams(vmem_limit_bytes=32 << 20),
        cost_estimate=pl.CostEstimate(
            flops=8 * count * width * CHUNK, bytes_accessed=14 * count * width,
            transcendentals=count * CHUNK * heads,
        ),
        name="intra",
    )(meta, docs, x_cat, bc, cum, dlt, gate_input, got_gate, skip)

    divisor = HEADS // GROUPS * head_width
    squares = None
    if not whole_groups:
        c = bc[:, state_width:]
        total = gated + jnp.dot(c, arriving, preferred_element_type=F32) * carry_gate
        mine = jnp.sum(total * total, axis=1, keepdims=True)
        squares = mine + swapped(mine, "sub")

    row_steps = chunks
    out_cols = features // tp_size
    mm_cols = min(512, out_cols)
    pair = tp_size == 2
    part = out_cols // mm_cols
    blocks = part if pair else features // mm_cols
    w_first = (lambda m: (1 - m[2]) * part) if pair else (lambda m: 0)
    project = functools.partial(
        project_kernel, row_steps=row_steps, group_width=group_width, state_width=state_width, divisor=divisor
    )
    clamp = lambda i: jnp.minimum(i, row_steps - 1)
    column = lambda i: jnp.maximum(i - row_steps, 0)
    in_specs = [
        pl.BlockSpec((CHUNK, width), lambda i, m: (clamp(i), 0)),
        pl.BlockSpec((CHUNK, width), lambda i, m: (clamp(i), 0)),
        pl.BlockSpec((CHUNK, block), lambda i, m: (clamp(i), 0)),
        fixed(state_width, width),
        pl.BlockSpec((1, width), lambda i, m: (0, m[0])),
    ]
    operands = [gated, carry_gate, bc, arriving, norm_gain.reshape(1, channels)]
    if squares is None:
        body = lambda m, a, f, b, n, g, *rest: project(m, a, f, b, n, g, None, *rest)
    else:
        body = project
        in_specs.append(pl.BlockSpec((CHUNK, 1), lambda i, m: (clamp(i), 0)))
        operands.append(squares)
    in_specs.append(pl.BlockSpec((width, mm_cols), lambda i, m: (0, w_first(m) + column(i))))
    operands.append(out_weight)
    columns = blocks * mm_cols
    hidden, send, keep = pl.pallas_call(
        body,
        grid_spec=pltpu.PrefetchScalarGridSpec(
            num_scalar_prefetch=1,
            grid=(row_steps + blocks,),
            in_specs=in_specs,
            out_specs=[
                fixed(count, width),
                pl.BlockSpec((half, mm_cols), lambda i, m: (0, column(i))),
                pl.BlockSpec((half, mm_cols), lambda i, m: (0, column(i))),
            ],
        ),
        out_shape=[
            jax.ShapeDtypeStruct((count, width), BF16),
            jax.ShapeDtypeStruct((half, columns), BF16),
            jax.ShapeDtypeStruct((half, columns), F32),
        ],
        compiler_params=pltpu.CompilerParams(vmem_limit_bytes=40 << 20),
        cost_estimate=pl.CostEstimate(
            flops=2 * count * width * columns, bytes_accessed=10 * count * width + 2 * width * columns,
            transcendentals=0,
        ),
        name="project",
    )(meta, *operands)
    got_send = swapped(send, "sub")
    far = (keep + got_send.astype(F32)).astype(BF16)
    if not pair:
        return lax.psum_scatter(far, "tp", scatter_dimension=1, tiled=True)
    got_far = swapped(far, "tp")
    near_send, near_keep = pl.pallas_call(
        product_kernel,
        grid_spec=pltpu.PrefetchScalarGridSpec(
            num_scalar_prefetch=1,
            grid=(part,),
            in_specs=[
                fixed(count, width),
                pl.BlockSpec((width, mm_cols), lambda i, m: (0, m[2] * part + i)),
            ],
            out_specs=[
                pl.BlockSpec((half, mm_cols), lambda i, m: (0, i)),
                pl.BlockSpec((half, mm_cols), lambda i, m: (0, i)),
            ],
        ),
        out_shape=[
            jax.ShapeDtypeStruct((half, out_cols), BF16),
            jax.ShapeDtypeStruct((half, out_cols), F32),
        ],
        compiler_params=pltpu.CompilerParams(vmem_limit_bytes=32 << 20),
        cost_estimate=pl.CostEstimate(
            flops=2 * count * width * out_cols, bytes_accessed=2 * count * width + 2 * width * out_cols,
            transcendentals=0,
        ),
        name="product",
    )(meta, hidden, out_weight)
    near = near_keep + swapped(near_send, "sub").astype(F32)
    return (near + got_far.astype(F32)).astype(BF16)


def solution(mesh):
    in_specs = (
        P(("groups", "ctx", "sub"), "tp"),
        P(("groups", "ctx", "sub"), "tp"),
        P(("groups", "ctx", "sub"), "tp", None, None),
        P(None, "tp"),
        P("tp"),
        P(None, "tp", None, None),
        P("tp", None, None),
        P(("groups", "ctx", "sub"), "tp"),
        P("tp"),
        P("tp"),
        P("tp"),
        P(("tp", "sub"), None),
        P("groups"),
    )
    out_specs = P(("groups", "ctx", "sub"), "tp")
    return jax.shard_map(local, mesh=mesh, in_specs=in_specs, out_specs=out_specs, check_vma=False)
```

```python
import functools

import jax
import jax.numpy as jnp
from jax import lax
from jax.experimental import pallas as pl
from jax.experimental.pallas import tpu as pltpu
from jax.sharding import PartitionSpec as P

HEADS = 128
GROUPS = 8
CHUNK = 128
EPSILON = 1e-05
LOG2E = 1.4426950408889634
MASKED = -1e30
VMEM = 60 << 20
F32 = jnp.float32
BF16 = jnp.bfloat16


def shifted(shard, axis, by):
    peers = lax.axis_size(axis)
    pairs = [(i, i + by) for i in range(peers) if 0 <= i + by < peers]
    return lax.ppermute(shard, axis, pairs)


def swapped(shard, axis):
    return lax.ppermute(shard, axis, [(i, i ^ 1) for i in range(lax.axis_size(axis))])


def doc_start(positions, docs_ref):
    start = jnp.zeros_like(positions)
    total = jnp.int32(0)
    for doc in range(docs_ref.shape[0]):
        start = jnp.where(positions >= total, total, start)
        total = total + docs_ref[doc]
    return start


def rows_of(count, first):
    return first + lax.broadcasted_iota(jnp.int32, (count, 1), 0)


def split2(value):
    high = value.astype(BF16)
    return high, (value - high.astype(F32)).astype(BF16)


def split3(value):
    high = value.astype(BF16)
    rest = value - high.astype(F32)
    mid = rest.astype(BF16)
    return high, mid, (rest - mid.astype(F32)).astype(BF16)


def mm(a, b):
    return jnp.dot(a, b, preferred_element_type=F32)


def contract_rows(a, b):
    return lax.dot_general(a, b, (((0,), (0,)), ((), ())), preferred_element_type=F32)


def contract_lanes(a, b):
    return lax.dot_general(a, b, (((1,), (1,)), ((), ())), preferred_element_type=F32)


def silu(value):
    half = 0.5 * value
    return half + half * jnp.tanh(half)


def head_lanes(heads, head_width, lanes, first_lane):
    head = lax.broadcasted_iota(jnp.int32, (heads, lanes), 0)
    lane = first_lane + lax.broadcasted_iota(jnp.int32, (heads, lanes), 1)
    low = head * head_width
    return jnp.where((lane >= low) & (lane < low + head_width), 1.0, 0.0).astype(BF16)


def conv_kernel(meta, docs, x, x_rim, w, bias, s, s_rim, sw, sbias, out, shift, rim_shift, *, taps):
    step, last = pl.program_id(0), pl.num_programs(0) - 1
    count = x.shape[0]
    rims = x_rim.shape[0]

    @pl.when(step == 0)
    def _():
        first = meta[1] + meta[0] * count
        start = doc_start(rows_of(count, first), docs) - first
        row = lax.broadcasted_iota(jnp.int32, (count, count), 0)
        col = lax.broadcasted_iota(jnp.int32, (count, count), 1)
        rim_row = lax.broadcasted_iota(jnp.int32, (rims, rims), 0)
        rim_col = lax.broadcasted_iota(jnp.int32, (rims, rims), 1) - rims
        for back in range(1, taps):
            hit = (col == row - back) & (col >= start)
            shift[back - 1] = jnp.where(hit, 1.0, 0.0).astype(BF16)
            rim_hit = (rim_col == rim_row - back) & (rim_col >= start[:rims])
            rim_shift[back - 1] = jnp.where(rim_hit, 1.0, 0.0).astype(BF16)

    def mix(x_part, rim_part, w_part, bias_part):
        value = x_part[...]
        rim = rim_part[...]
        weight = w_part[...].astype(F32)
        summed = bias_part[...] + value.astype(F32) * weight[taps - 1 : taps]
        top = jnp.zeros((rims, value.shape[1]), F32)
        for back in range(1, taps):
            row = weight[taps - 1 - back : taps - back]
            summed = summed + mm(shift[back - 1], value) * row
            top = top + mm(rim_shift[back - 1], rim) * row
        out[:rims, :] = silu(summed[:rims] + top).astype(BF16)
        out[rims:, :] = silu(summed[rims:]).astype(BF16)

    @pl.when(step < last)
    def _():
        mix(x, x_rim, w, bias)

    @pl.when(step == last)
    def _():
        mix(s, s_rim, sw, sbias)


def conv_half(other, meta, docs, x, w, bias, s, sw, sbias, rim, rims, width, block, whole_groups):
    count, channels = x.shape
    taps = w.shape[0]
    steps = width // block
    half = lambda m: 1 - m[0] if other else m[0]
    x_at = lambda i, m, d: half(m) * steps + jnp.minimum(i, steps - 1)
    s_at = lambda i, m, d: half(m) if whole_groups else 0
    rim_at = lambda i, m, d: channels // block + s_at(i, m, d)
    specs = []
    for at, rim_col in ((x_at, x_at), (s_at, rim_at)):
        for rows in (count, rims, taps, 1):
            col = rim_col if rows == rims else at
            specs.append(pl.BlockSpec((rows, block), lambda i, m, d, col=col: (0, col(i, m, d))))
    return pl.pallas_call(
        functools.partial(conv_kernel, taps=taps),
        grid_spec=pltpu.PrefetchScalarGridSpec(
            num_scalar_prefetch=2,
            grid=(steps + 1,),
            in_specs=specs,
            out_specs=pl.BlockSpec((count, block), lambda i, m, d: (0, i)),
            scratch_shapes=[
                pltpu.VMEM((taps - 1, count, count), BF16),
                pltpu.VMEM((taps - 1, rims, rims), BF16),
            ],
        ),
        out_shape=jax.ShapeDtypeStruct((count, width + block), BF16),
        compiler_params=pltpu.CompilerParams(vmem_limit_bytes=VMEM),
        cost_estimate=pl.CostEstimate(
            flops=8 * count * width, bytes_accessed=4 * count * (width + block), transcendentals=count * width
        ),
        name="conv",
    )(meta, docs, x, rim, w, bias, s, rim, sw, sbias)


def state_kernel(
    meta, docs, own, got, own_bc, got_bc, own_raw, got_raw, rate,
    x_out, bc_out, s_out, d_out, cum_out, dlt_out, raw, weight,
    *, head_width, group_width, state_width,
):
    step = pl.program_id(0)
    half = own.shape[0]
    count = 2 * half
    heads = raw.shape[1]
    width = own.shape[1]
    own_at = pl.ds(pl.multiple_of(meta[0] * half, half), half)
    got_at = pl.ds(pl.multiple_of((1 - meta[0]) * half, half), half)
    first = meta[1]
    last_start = doc_start(first + count - 1, docs)

    @pl.when(step == 0)
    def _():
        bc_out[own_at, :] = own_bc[...]
        bc_out[got_at, :] = got_bc[...]
        mine = meta[0] == 0
        raw[own_at, :] = jnp.where(mine, own_raw[:, :heads], own_raw[:, heads:])
        raw[got_at, :] = jnp.where(mine, got_raw[:, :heads], got_raw[:, heads:])
        value = raw[...]
        rates = jnp.where(mine, rate[:, :heads], rate[:, heads:])
        size = jnp.maximum(value, 0.0) + jnp.log(1.0 + jnp.exp(-jnp.abs(value)))
        decay = (-LOG2E * jnp.exp(rates)) * size
        row = lax.broadcasted_iota(jnp.int32, (count, count), 0)
        col = lax.broadcasted_iota(jnp.int32, (count, count), 1)
        below = jnp.where(col <= row, 1.0, 0.0).astype(BF16)
        high, mid, low = split3(decay)
        cum = mm(below, high) + (mm(below, mid) + mm(below, low))
        cum_out[...] = cum
        dlt_out[...] = (cum - jnp.log2(size)).T
        end = cum[count - 1 :]
        tail = jnp.where(rows_of(count, first) >= last_start, size * jnp.exp2(end - cum), 0.0)
        high, low = split2(tail)
        weight[0] = high
        weight[1] = low

    x_out[own_at, :] = own[...]
    x_out[got_at, :] = got[...]
    spread = head_lanes(heads, head_width, width, step * width)
    group = (step * width) // group_width
    b = bc_out[:, pl.ds(pl.multiple_of(group * 2 * state_width, state_width), state_width)]
    tails = mm(weight[0], spread) + mm(weight[1], spread)
    weighted = (x_out[...].astype(F32) * tails).astype(BF16)
    s_out[...] = contract_rows(b, weighted).astype(BF16)
    kept = jnp.exp2(jnp.broadcast_to(cum_out[count - 1 :, :], (8, heads)))
    high, mid, low = split3(jnp.where(last_start < first, kept, 0.0))
    d_out[...] = mm(high, spread) + (mm(mid, spread) + mm(low, spread))


def intra_kernel(
    meta, docs, x, bc, cum, dlt, gate_own, gate_got, gain,
    a_out, f_out, state, base, spread, skip, reach, into, tail,
    *, head_width, group_heads, state_width,
):
    step = pl.program_id(0)
    count, width = x.shape
    heads = cum.shape[1]
    first = meta[1] + step * count

    @pl.when(step == 0)
    def _():
        state[...] = jnp.zeros_like(state)
        base[...] = jnp.zeros_like(base)
        spread[...] = head_lanes(heads, head_width, width, 0)
        mine = jnp.where(meta[0] == 0, gain[:, :heads], gain[:, heads:])
        high, mid, low = split3(jnp.broadcast_to(mine, (8, heads)))
        skip[...] = mm(high, spread[...]) + (mm(mid, spread[...]) + mm(low, spread[...]))

    starts = doc_start(rows_of(count, first), docs)
    last_start = doc_start(first + count - 1, docs)
    here = cum[...]
    before = base[:1, :]
    end = here[count - 1 :]
    lanes = spread[...]

    def spread_over(value):
        high, low = split2(value)
        return mm(high, lanes) + mm(low, lanes)

    reach[...] = spread_over(jnp.where(starts < first, jnp.exp2(here - before), 0.0))
    into[...] = spread_over(jnp.where(starts < meta[1], jnp.exp2(here), 0.0))
    to_end = jnp.exp2(end - dlt[...].T)
    tail[...] = spread_over(jnp.where(rows_of(count, first) >= last_start, to_end, 0.0))
    kept = jnp.broadcast_to(jnp.where(last_start < first, jnp.exp2(end - before), 0.0), (8, heads))
    high, mid, low = split3(kept)
    kept = (mm(high, lanes) + (mm(mid, lanes) + mm(low, lanes)))[:1]
    row = lax.broadcasted_iota(jnp.int32, (count, count), 0)
    col = lax.broadcasted_iota(jnp.int32, (count, count), 1)
    mask = jnp.where((col <= row) & (col >= starts - first), 0.0, MASKED)
    is_own = (step * count) // (count * (pl.num_programs(0) // 2)) == meta[0]
    low_lanes = lax.broadcasted_iota(jnp.int32, (count, 2 * head_width), 1) < head_width
    zero = jnp.zeros((count, 2 * head_width), BF16)
    for group in range(heads // group_heads):
        b = bc[:, group * 2 * state_width : (group * 2 + 1) * state_width]
        c = bc[:, (group * 2 + 1) * state_width : (group * 2 + 2) * state_width]
        scores = contract_lanes(c, b)
        for head in range(group * group_heads, (group + 1) * group_heads, 2):
            at = slice(head * head_width, (head + 2) * head_width)
            pair = []
            for k in (head, head + 1):
                exponent = (here[:, k : k + 1] - dlt[k : k + 1, :]) + mask
                pair.append((jnp.exp2(exponent) * scores).astype(BF16))
            value = x[:, at]
            stacked = jnp.concatenate([jnp.where(low_lanes, value, zero), jnp.where(low_lanes, zero, value)], axis=0)
            within = mm(jnp.concatenate(pair, axis=1), stacked)
            old = state[:, at]
            carried = mm(c, old.astype(BF16)) * reach[:, at]
            x_part = value.astype(F32)
            y = within + carried + x_part * skip[:1, at]
            gate = silu(jnp.where(is_own, gate_own[:, at], gate_got[:, at]).astype(F32))
            a_out[:, at] = y * gate
            f_out[:, at] = gate * into[:, at]
            fresh = contract_rows(b, (x_part * tail[:, at]).astype(BF16))
            state[:, at] = old * kept[:, at] + fresh
    base[...] = jnp.broadcast_to(end, base.shape)


def project_kernel(
    meta, a, f, bc, incoming, gain, squares, w, hidden, send, keep,
    *, row_steps, group_width, state_width, divisor,
):
    step = pl.program_id(0)
    count = a.shape[0]
    width = a.shape[1]
    half = send.shape[0]

    @pl.when(step < row_steps)
    def _():
        at = pl.ds(pl.multiple_of(step * count, count), count)
        for group in range(width // group_width):
            lanes = slice(group * group_width, (group + 1) * group_width)
            c = bc[:, (group * 2 + 1) * state_width : (group * 2 + 2) * state_width]
            gated = a[:, lanes] + mm(c, incoming[:, lanes]) * f[:, lanes]
            if squares is None:
                total = jnp.sum(gated * gated, axis=1, keepdims=True)
            else:
                total = squares[...]
            scale = lax.rsqrt(total / divisor + EPSILON)
            hidden[at, lanes] = (gated * scale * gain[:, lanes]).astype(BF16)

    @pl.when(step >= row_steps)
    def _():
        there = pl.ds(pl.multiple_of((1 - meta[0]) * half, half), half)
        here = pl.ds(pl.multiple_of(meta[0] * half, half), half)
        send[...] = mm(hidden[there, :], w[...]).astype(BF16)
        keep[...] = mm(hidden[here, :], w[...])


def product_kernel(meta, hidden, w, send, keep):
    half = send.shape[0]
    there = pl.ds(pl.multiple_of((1 - meta[0]) * half, half), half)
    here = pl.ds(pl.multiple_of(meta[0] * half, half), half)
    send[...] = mm(hidden[there, :], w[...]).astype(BF16)
    keep[...] = mm(hidden[here, :], w[...])


def local(
    x_input, gate_input, state_proj, mix_weight, mix_bias, state_weight, state_bias,
    step_raw, decay_log, skip_gain, norm_gain, out_weight, doc_lengths,
):
    half, channels = x_input.shape
    all_heads = step_raw.shape[1]
    groups, _, state_width = state_proj.shape[1:]
    taps = mix_weight.shape[0]
    features = out_weight.shape[1]
    head_width = channels // all_heads
    heads = all_heads // 2
    width = channels // 2
    count = 2 * half
    whole_groups = groups % 2 == 0
    my_groups = groups // 2 if whole_groups else groups
    group_heads = heads // my_groups
    group_width = group_heads * head_width
    block = my_groups * 2 * state_width
    sub = lax.axis_index("sub").astype(jnp.int32)
    ctx = lax.axis_index("ctx").astype(jnp.int32)
    tp = lax.axis_index("tp").astype(jnp.int32)
    tp_size = lax.axis_size("tp")
    ctx_size = lax.axis_size("ctx")
    block_first = ctx * count
    docs = doc_lengths.astype(jnp.int32)

    s_input = state_proj.reshape(half, groups * 2 * state_width)
    s_weight = state_weight.reshape(taps, groups * 2 * state_width)
    s_bias = state_bias.reshape(1, groups * 2 * state_width)
    rims = 16
    meta = jnp.stack([sub, block_first, tp])
    rim = shifted(jnp.concatenate([x_input[half - rims :], s_input[half - rims :]], axis=1), ("ctx", "sub"), 1)
    got_raw = swapped(step_raw, "sub")
    conv = functools.partial(
        conv_half, meta=meta, docs=docs, x=x_input, w=mix_weight, bias=mix_bias.reshape(1, channels), s=s_input,
        sw=s_weight, sbias=s_bias, rim=rim, rims=rims, width=width, block=block, whole_groups=whole_groups,
    )
    other = conv(True)
    got = swapped(other, "sub")
    own = conv(False)
    got_gate = swapped(lax.dynamic_slice_in_dim(gate_input, (1 - sub) * width, width, 1), "sub")

    cols = min(512, group_width)
    steps = width // cols
    fixed = lambda *shape: pl.BlockSpec(shape, lambda i, *m: (0,) * len(shape))
    x_cat, bc, state, kept, cum, dlt = pl.pallas_call(
        functools.partial(
            state_kernel, head_width=head_width, group_width=group_width, state_width=state_width
        ),
        grid_spec=pltpu.PrefetchScalarGridSpec(
            num_scalar_prefetch=2,
            grid=(steps,),
            in_specs=[
                pl.BlockSpec((half, cols), lambda i, *m: (0, i)),
                pl.BlockSpec((half, cols), lambda i, *m: (0, i)),
                pl.BlockSpec((half, block), lambda i, *m: (0, width // block)),
                pl.BlockSpec((half, block), lambda i, *m: (0, width // block)),
                fixed(half, all_heads),
                fixed(half, all_heads),
                fixed(1, all_heads),
            ],
            out_specs=[
                pl.BlockSpec((count, cols), lambda i, *m: (0, i)),
                fixed(count, block),
                pl.BlockSpec((state_width, cols), lambda i, *m: (0, i)),
                pl.BlockSpec((8, cols), lambda i, *m: (0, i)),
                fixed(count, heads),
                fixed(heads, count),
            ],
            scratch_shapes=[pltpu.VMEM((count, heads), F32), pltpu.VMEM((2, count, heads), BF16)],
        ),
        out_shape=[
            jax.ShapeDtypeStruct((count, width), BF16),
            jax.ShapeDtypeStruct((count, block), BF16),
            jax.ShapeDtypeStruct((state_width, width), BF16),
            jax.ShapeDtypeStruct((8, width), F32),
            jax.ShapeDtypeStruct((count, heads), F32),
            jax.ShapeDtypeStruct((heads, count), F32),
        ],
        compiler_params=pltpu.CompilerParams(vmem_limit_bytes=VMEM),
        cost_estimate=pl.CostEstimate(
            flops=4 * count * width * state_width, bytes_accessed=5 * count * width, transcendentals=count * heads
        ),
        name="state",
    )(meta, docs, own, got, own, got, step_raw, got_raw, decay_log.reshape(1, all_heads))

    arriving = jnp.zeros_like(state)
    for hop in range(ctx_size // 2):
        leaving = state
        if hop:
            leaving = (state.astype(F32) + kept[:1] * arriving.astype(F32)).astype(BF16)
        arriving = shifted(leaving, "ctx", 1)

    chunks = count // CHUNK
    by_row = lambda n: pl.BlockSpec((CHUNK, n), lambda i, *m: (i, 0))
    gated, carry_gate = pl.pallas_call(
        functools.partial(
            intra_kernel, head_width=head_width, group_heads=group_heads, state_width=state_width
        ),
        grid_spec=pltpu.PrefetchScalarGridSpec(
            num_scalar_prefetch=2,
            grid=(chunks,),
            in_specs=[
                by_row(width),
                by_row(block),
                by_row(heads),
                pl.BlockSpec((heads, CHUNK), lambda i, *m: (0, i)),
                pl.BlockSpec((CHUNK, width), lambda i, m, d: (lax.rem(i, chunks // 2), m[0])),
                pl.BlockSpec((CHUNK, width), lambda i, m, d: (lax.rem(i, chunks // 2), 0)),
                fixed(1, all_heads),
            ],
            out_specs=[by_row(width), by_row(width)],
            scratch_shapes=[
                pltpu.VMEM((state_width, width), F32),
                pltpu.VMEM((8, heads), F32),
                pltpu.VMEM((heads, width), BF16),
                pltpu.VMEM((8, width), F32),
                pltpu.VMEM((CHUNK, width), F32),
                pltpu.VMEM((CHUNK, width), F32),
                pltpu.VMEM((CHUNK, width), F32),
            ],
        ),
        out_shape=[jax.ShapeDtypeStruct((count, width), F32), jax.ShapeDtypeStruct((count, width), F32)],
        compiler_params=pltpu.CompilerParams(vmem_limit_bytes=VMEM),
        cost_estimate=pl.CostEstimate(
            flops=8 * count * width * CHUNK, bytes_accessed=14 * count * width,
            transcendentals=count * CHUNK * heads,
        ),
        name="intra",
    )(meta, docs, x_cat, bc, cum, dlt, gate_input, got_gate, skip_gain.reshape(1, all_heads))

    divisor = HEADS // GROUPS * head_width
    squares = None
    if not whole_groups:
        c = bc[:, state_width:]
        total = gated + jnp.dot(c, arriving, preferred_element_type=F32) * carry_gate
        mine = jnp.sum(total * total, axis=1, keepdims=True)
        squares = mine + swapped(mine, "sub")

    row_steps = chunks
    out_cols = features // tp_size
    mm_cols = min(512, out_cols)
    pair = tp_size == 2
    part = out_cols // mm_cols
    blocks = part if pair else features // mm_cols
    w_first = (lambda m: (1 - m[2]) * part) if pair else (lambda m: 0)
    project = functools.partial(
        project_kernel, row_steps=row_steps, group_width=group_width, state_width=state_width, divisor=divisor
    )
    clamp = lambda i: jnp.minimum(i, row_steps - 1)
    column = lambda i: jnp.maximum(i - row_steps, 0)
    in_specs = [
        pl.BlockSpec((CHUNK, width), lambda i, m: (clamp(i), 0)),
        pl.BlockSpec((CHUNK, width), lambda i, m: (clamp(i), 0)),
        pl.BlockSpec((CHUNK, block), lambda i, m: (clamp(i), 0)),
        fixed(state_width, width),
        pl.BlockSpec((1, width), lambda i, m: (0, m[0])),
    ]
    operands = [gated, carry_gate, bc, arriving, norm_gain.reshape(1, channels)]
    if squares is None:
        body = lambda m, a, f, b, n, g, *rest: project(m, a, f, b, n, g, None, *rest)
    else:
        body = project
        in_specs.append(pl.BlockSpec((CHUNK, 1), lambda i, m: (clamp(i), 0)))
        operands.append(squares)
    in_specs.append(pl.BlockSpec((width, mm_cols), lambda i, m: (0, w_first(m) + column(i))))
    operands.append(out_weight)
    columns = blocks * mm_cols
    hidden, send, keep = pl.pallas_call(
        body,
        grid_spec=pltpu.PrefetchScalarGridSpec(
            num_scalar_prefetch=1,
            grid=(row_steps + blocks,),
            in_specs=in_specs,
            out_specs=[
                fixed(count, width),
                pl.BlockSpec((half, mm_cols), lambda i, m: (0, column(i))),
                pl.BlockSpec((half, mm_cols), lambda i, m: (0, column(i))),
            ],
        ),
        out_shape=[
            jax.ShapeDtypeStruct((count, width), BF16),
            jax.ShapeDtypeStruct((half, columns), BF16),
            jax.ShapeDtypeStruct((half, columns), F32),
        ],
        compiler_params=pltpu.CompilerParams(vmem_limit_bytes=VMEM),
        cost_estimate=pl.CostEstimate(
            flops=2 * count * width * columns, bytes_accessed=10 * count * width + 2 * width * columns,
            transcendentals=0,
        ),
        name="project",
    )(meta, *operands)
    got_send = swapped(send, "sub")
    far = (keep + got_send.astype(F32)).astype(BF16)
    if not pair:
        return lax.psum_scatter(far, "tp", scatter_dimension=1, tiled=True)
    got_far = swapped(far, "tp")
    near_send, near_keep = pl.pallas_call(
        product_kernel,
        grid_spec=pltpu.PrefetchScalarGridSpec(
            num_scalar_prefetch=1,
            grid=(part,),
            in_specs=[
                fixed(count, width),
                pl.BlockSpec((width, mm_cols), lambda i, m: (0, m[2] * part + i)),
            ],
            out_specs=[
                pl.BlockSpec((half, mm_cols), lambda i, m: (0, i)),
                pl.BlockSpec((half, mm_cols), lambda i, m: (0, i)),
            ],
        ),
        out_shape=[
            jax.ShapeDtypeStruct((half, out_cols), BF16),
            jax.ShapeDtypeStruct((half, out_cols), F32),
        ],
        compiler_params=pltpu.CompilerParams(vmem_limit_bytes=VMEM),
        cost_estimate=pl.CostEstimate(
            flops=2 * count * width * out_cols, bytes_accessed=2 * count * width + 2 * width * out_cols,
            transcendentals=0,
        ),
        name="product",
    )(meta, hidden, out_weight)
    near = near_keep + swapped(near_send, "sub").astype(F32)
    return (near + got_far.astype(F32)).astype(BF16)


def solution(mesh):
    in_specs = (
        P(("groups", "ctx", "sub"), "tp"),
        P(("groups", "ctx", "sub"), "tp"),
        P(("groups", "ctx", "sub"), "tp", None, None),
        P(None, "tp"),
        P("tp"),
        P(None, "tp", None, None),
        P("tp", None, None),
        P(("groups", "ctx", "sub"), "tp"),
        P("tp"),
        P("tp"),
        P("tp"),
        P(("tp", "sub"), None),
        P("groups"),
    )
    out_specs = P(("groups", "ctx", "sub"), "tp")
    return jax.shard_map(local, mesh=mesh, in_specs=in_specs, out_specs=out_specs, check_vma=False)
```

```python
import functools

import jax
import jax.numpy as jnp
from jax import lax
from jax.experimental import pallas as pl
from jax.experimental.pallas import tpu as pltpu
from jax.sharding import PartitionSpec as P

HEADS = 128
GROUPS = 8
CHUNK = 128
EPSILON = 1e-05
LOG2E = 1.4426950408889634
CEILING = 126.0
VMEM = 60 << 20
F32 = jnp.float32
BF16 = jnp.bfloat16


def shifted(shard, axis, by):
    peers = lax.axis_size(axis)
    pairs = [(i, i + by) for i in range(peers) if 0 <= i + by < peers]
    return lax.ppermute(shard, axis, pairs)


def swapped(shard, axis):
    return lax.ppermute(shard, axis, [(i, i ^ 1) for i in range(lax.axis_size(axis))])


def doc_start(positions, docs_ref):
    start = jnp.zeros_like(positions)
    total = jnp.int32(0)
    for doc in range(docs_ref.shape[0]):
        start = jnp.where(positions >= total, total, start)
        total = total + docs_ref[doc]
    return start


def rows_of(count, first):
    return first + lax.broadcasted_iota(jnp.int32, (count, 1), 0)


def split2(value):
    high = value.astype(BF16)
    return high, (value - high.astype(F32)).astype(BF16)


def split3(value):
    high = value.astype(BF16)
    rest = value - high.astype(F32)
    mid = rest.astype(BF16)
    return high, mid, (rest - mid.astype(F32)).astype(BF16)


def mm(a, b):
    return jnp.dot(a, b, preferred_element_type=F32)


def contract_lanes(a, b):
    return lax.dot_general(a, b, (((1,), (1,)), ((), ())), preferred_element_type=F32)


def silu(value):
    half = 0.5 * value
    return half + half * jnp.tanh(half)


def head_lanes(copies, heads, head_width, lanes, first_lane):
    shape = (copies * heads, lanes)
    head = lax.rem(lax.broadcasted_iota(jnp.int32, shape, 0), heads)
    lane = first_lane + lax.broadcasted_iota(jnp.int32, shape, 1)
    low = head * head_width
    return jnp.where((lane >= low) & (lane < low + head_width), 1.0, 0.0).astype(BF16)


def convolved(first, docs, pieces, store, taps):
    count = pieces[0][0].shape[0]
    rims = pieces[0][1].shape[0]
    start = doc_start(rows_of(count, first), docs) - first
    row = lax.broadcasted_iota(jnp.int32, (count, count), 0)
    col = lax.broadcasted_iota(jnp.int32, (count, count), 1)
    rim_row = lax.broadcasted_iota(jnp.int32, (rims, rims), 0)
    rim_col = lax.broadcasted_iota(jnp.int32, (rims, rims), 1) - rims
    shifts = []
    for back in range(1, taps):
        hit = (col == row - back) & (col >= start)
        rim_hit = (rim_col == rim_row - back) & (rim_col >= start[:rims])
        shifts.append((jnp.where(hit, 1.0, 0.0).astype(BF16), jnp.where(rim_hit, 1.0, 0.0).astype(BF16)))
    for index, (x, rim, w, bias) in enumerate(pieces):
        span = min(256, x.shape[1])
        for low in range(0, x.shape[1], span):
            at = slice(low, low + span)
            value = x[:, at]
            weight = w[:, at].astype(F32)
            summed = bias[:, at] + value.astype(F32) * weight[taps - 1 : taps]
            top = jnp.zeros((rims, span), F32)
            for back in range(1, taps):
                line = weight[taps - 1 - back : taps - back]
                shift, rim_shift = shifts[back - 1]
                summed = summed + mm(shift, value) * line
                top = top + mm(rim_shift, rim[:, at]) * line
            store(index, at, slice(0, rims), silu(summed[:rims] + top).astype(BF16))
            store(index, at, slice(rims, count), silu(summed[rims:]).astype(BF16))


def conv_kernel(meta, docs, x, x_rim, w, bias, s, s_rim, sw, sbias, out, *, taps):
    width = x.shape[1]

    def store(index, at, rows, value):
        out[rows, slice(at.start + index * width, at.stop + index * width)] = value

    first = meta[1] + meta[0] * x.shape[0]
    convolved(first, docs, [(x, x_rim, w, bias), (s, s_rim, sw, sbias)], store, taps)


def decay_kernel(
    meta, docs, own_raw, got_raw, rate, cum_out, dlt_out, tail_out, kept_out, raw,
):
    half = own_raw.shape[1]
    heads, count = raw.shape
    mine = meta[0] == 0
    first = meta[1]
    own_at = pl.ds(pl.multiple_of(meta[0] * half, half), half)
    got_at = pl.ds(pl.multiple_of((1 - meta[0]) * half, half), half)
    last_start = doc_start(first + count - 1, docs)
    raw[:, own_at] = jnp.where(mine, own_raw[:heads], own_raw[heads:])
    raw[:, got_at] = jnp.where(mine, got_raw[:heads], got_raw[heads:])
    value = raw[...]
    size = jnp.maximum(value, 0.0) + jnp.log(1.0 + jnp.exp(-jnp.abs(value)))
    decay = (-LOG2E * jnp.exp(jnp.where(mine, rate[:heads], rate[heads:]))) * size
    row = lax.broadcasted_iota(jnp.int32, (count, count), 0)
    col = lax.broadcasted_iota(jnp.int32, (count, count), 1)
    above = jnp.where(row <= col, 1.0, 0.0).astype(BF16)
    high, mid, low = split3(decay)
    cum = mm(high, above) + (mm(mid, above) + mm(low, above))
    dlt_out[...] = cum - jnp.log2(size)
    end = cum[:, count - 1 :]
    places = first + lax.broadcasted_iota(jnp.int32, (1, count), 1)
    tail = jnp.where(places >= last_start, size * jnp.exp2(end - cum), 0.0)
    high, low = split2(tail.T)
    tail_out[:, :heads] = high
    tail_out[:, heads:] = low
    cum = cum.T
    cum_out[...] = cum
    kept = jnp.exp2(jnp.broadcast_to(cum[count - 1 :], (8, heads)))
    high, mid, low = split3(jnp.where(last_start < first, kept, 0.0))
    kept_out[:, :heads] = high
    kept_out[:, heads : 2 * heads] = mid
    kept_out[:, 2 * heads :] = low


def state_kernel(
    meta, docs, x, x_rim, w, bias, s, s_rim, sw, sbias, got, tail, kept,
    x_out, bc_out, s_out, d_out, *, taps, heads, head_width, first_lane,
):
    half, width = x.shape
    state_width = bc_out.shape[1] // 2
    own_row = pl.multiple_of(meta[0] * half, half)
    got_at = pl.ds(pl.multiple_of((1 - meta[0]) * half, half), half)

    def store(index, at, rows, value):
        place = pl.ds(pl.multiple_of(own_row + rows.start, 16), rows.stop - rows.start)
        if index:
            bc_out[place, at] = value
        else:
            x_out[place, at] = value

    convolved(meta[1] + meta[0] * half, docs, [(x, x_rim, w, bias), (s, s_rim, sw, sbias)], store, taps)
    x_out[got_at, :] = got[:, :width]
    bc_out[got_at, :] = got[:, width:]
    b = bc_out[:, :state_width].T
    span = min(256, width)
    for low in range(0, width, span):
        at = slice(low, low + span)
        tails = mm(tail[...], head_lanes(2, heads, head_width, span, first_lane + low))
        weighted = (x_out[:, at].astype(F32) * tails).astype(BF16)
        s_out[:, at] = mm(b, weighted).astype(BF16)
        d_out[:, at] = mm(kept[...], head_lanes(3, heads, head_width, span, first_lane + low))


def intra_kernel(
    meta, docs, x, bc, cum, dlt, gate_own, gate_got, gain,
    a_out, f_out, state, base, spread, skip, reach, into, tail,
    *, head_width, first_head, group_heads,
):
    step = pl.program_id(0)
    count, width = x.shape
    heads = cum.shape[1]
    state_width = bc.shape[1] // 2
    first = meta[1] + step * count

    @pl.when(step == 0)
    def _():
        state[...] = jnp.zeros_like(state)
        base[...] = jnp.zeros_like(base)
        spread[...] = head_lanes(3, heads, head_width, width, first_head * head_width)
        mine = jnp.where(meta[0] == 0, gain[:, :heads], gain[:, heads:])
        skip[...] = mm(jnp.concatenate(split3(jnp.broadcast_to(mine, (8, heads))), axis=1), spread[...])

    starts = doc_start(rows_of(count, first), docs)
    last_start = doc_start(first + count - 1, docs)
    here = cum[...]
    before = base[:1, :]
    end = here[count - 1 :]

    def spread_over(value):
        return mm(jnp.concatenate(split2(value), axis=1), spread[: 2 * heads])

    reach[...] = spread_over(jnp.where(starts < first, jnp.exp2(here - before), 0.0))
    into[...] = spread_over(jnp.where(starts < meta[1], jnp.exp2(here), 0.0))
    to_end = jnp.exp2(end - dlt[...].T)
    tail[...] = spread_over(jnp.where(rows_of(count, first) >= last_start, to_end, 0.0))
    kept = jnp.broadcast_to(jnp.where(last_start < first, jnp.exp2(end - before), 0.0), (8, heads))
    kept = mm(jnp.concatenate(split3(kept), axis=1), spread[...])[:1]
    row = lax.broadcasted_iota(jnp.int32, (count, count), 0)
    col = lax.broadcasted_iota(jnp.int32, (count, count), 1)
    is_own = (step * count) // (count * (pl.num_programs(0) // 2)) == meta[0]
    low_lanes = lax.broadcasted_iota(jnp.int32, (count, 2 * head_width), 1) < head_width
    zero = jnp.zeros((count, 2 * head_width), BF16)
    b = bc[:, :state_width]
    c = bc[:, state_width:]
    b_turned = b.T
    scores = jnp.where((col <= row) & (col >= starts - first), contract_lanes(c, b), 0.0)
    for head in range(0, group_heads, 2):
        at = slice(head * head_width, (head + 2) * head_width)
        pair = []
        for k in (first_head + head, first_head + head + 1):
            exponent = jnp.minimum(here[:, k : k + 1] - dlt[k : k + 1, :], CEILING)
            pair.append((jnp.exp2(exponent) * scores).astype(BF16))
        value = x[:, at]
        stacked = jnp.concatenate([jnp.where(low_lanes, value, zero), jnp.where(low_lanes, zero, value)], axis=0)
        within = mm(jnp.concatenate(pair, axis=1), stacked)
        old = state[:, at]
        carried = mm(c, old.astype(BF16)) * reach[:, at]
        x_part = value.astype(F32)
        y = within + carried + x_part * skip[:1, at]
        gate = silu(jnp.where(is_own, gate_own[:, at], gate_got[:, at]).astype(F32))
        a_out[:, at] = y * gate
        f_out[:, at] = gate * into[:, at]
        fresh = mm(b_turned, (x_part * tail[:, at]).astype(BF16))
        state[:, at] = old * kept[:, at] + fresh
    base[...] = jnp.broadcast_to(end, base.shape)


def normed(a, f, bc, incoming, gain, squares, divisor):
    state_width = bc.shape[1] // 2
    gated = a[...] + mm(bc[:, state_width:], incoming[...]) * f[...]
    total = jnp.sum(gated * gated, axis=1, keepdims=True) if squares is None else squares[...]
    return (gated * lax.rsqrt(total / divisor + EPSILON) * gain[...]).astype(BF16)


def norm_kernel(meta, a, f, bc, incoming, gain, hidden, *, divisor):
    hidden[...] = normed(a, f, bc, incoming, gain, None, divisor)


def project_kernel(meta, *refs, ready, squared, divisor):
    refs = list(refs)
    rows = []
    for _ in range(2):
        rows.append((refs[:ready], refs[ready : ready + 3], refs[ready + 3] if squared else None))
        refs = refs[ready + 3 + squared :]
    incoming, gain, w, hidden, send, keep = refs
    count = send.shape[0]

    @pl.when(pl.program_id(0) == 0)
    def _():
        for index, (done, (a, f, bc), squares) in enumerate(rows):
            at = slice(index * count, (index + 1) * count)
            width = a.shape[1]
            for group, part in enumerate(done):
                hidden[at, group * width : (group + 1) * width] = part[...]
            hidden[at, ready * width :] = normed(a, f, bc, incoming, gain, squares, divisor)

    product = mm(hidden[...], w[...])
    send[...] = product[:count].astype(BF16)
    keep[...] = product[count:]


def product_kernel(meta, *refs):
    hiddens, (w, send, keep) = refs[:-3], refs[-3:]
    count = hiddens[0].shape[0] // 2
    for index, hidden in enumerate(hiddens):
        at = slice(index * count, (index + 1) * count)
        product = mm(hidden[...], w[...])
        send[at, :] = product[:count].astype(BF16)
        keep[at, :] = product[count:]


def local(
    x_input, gate_input, state_proj, mix_weight, mix_bias, state_weight, state_bias,
    step_raw, decay_log, skip_gain, norm_gain, out_weight, doc_lengths,
):
    half, channels = x_input.shape
    all_heads = step_raw.shape[1]
    groups, _, state_width = state_proj.shape[1:]
    taps = mix_weight.shape[0]
    features = out_weight.shape[1]
    head_width = channels // all_heads
    heads = all_heads // 2
    width = channels // 2
    count = 2 * half
    whole_groups = groups % 2 == 0
    parts = groups // 2 if whole_groups else groups
    part_heads = heads // parts
    part_width = part_heads * head_width
    block = 2 * state_width
    chunks = count // CHUNK
    splits = half // CHUNK
    sub = lax.axis_index("sub").astype(jnp.int32)
    ctx = lax.axis_index("ctx").astype(jnp.int32)
    tp = lax.axis_index("tp").astype(jnp.int32)
    tp_size = lax.axis_size("tp")
    ctx_size = lax.axis_size("ctx")
    docs = doc_lengths.astype(jnp.int32)
    meta = jnp.stack([sub, ctx * count, tp])
    params = pltpu.CompilerParams(vmem_limit_bytes=VMEM)
    fixed = lambda *shape: pl.BlockSpec(shape, lambda i, *m: (0,) * len(shape))
    shape_of = jax.ShapeDtypeStruct

    def call(body, name, grid, in_specs, out_specs, out_shape, scratch=(), flops=0, moved=0, prefetch=2):
        return pl.pallas_call(
            body,
            grid_spec=pltpu.PrefetchScalarGridSpec(
                num_scalar_prefetch=prefetch, grid=grid, in_specs=in_specs, out_specs=out_specs,
                scratch_shapes=list(scratch),
            ),
            out_shape=out_shape,
            compiler_params=params,
            cost_estimate=pl.CostEstimate(flops=flops, bytes_accessed=moved, transcendentals=0),
            name=name,
        )

    s_input = state_proj.reshape(half, groups * block)
    s_weight = state_weight.reshape(taps, groups * block)
    s_bias = state_bias.reshape(1, groups * block)
    bias = mix_bias.reshape(1, channels)
    rims = 16
    s_rim = state_proj[half - rims :].reshape(rims, groups * block)
    rim = shifted(jnp.concatenate([x_input[half - rims :], s_rim], axis=1), ("ctx", "sub"), 1)
    raw = step_raw.T
    got_raw = swapped(raw, "sub")
    mixed = (x_input, rim, mix_weight, bias, s_input, rim, s_weight, s_bias)

    def mix_specs(part, other):
        at = lambda m: (1 - m[0] if other else m[0]) * parts + part
        s_at = at if whole_groups else (lambda m: 0)
        rim_at = lambda m: channels // block + s_at(m)
        specs = []
        for size, places in ((part_width, (at, at, at, at)), (block, (s_at, rim_at, s_at, s_at))):
            for rows, place in zip((half, rims, taps, 1), places):
                specs.append(pl.BlockSpec((rows, size), lambda i, m, d, place=place: (0, place(m))))
        return specs

    got = []
    for part in range(parts):
        other = call(
            functools.partial(conv_kernel, taps=taps), "conv", (1,), mix_specs(part, True),
            fixed(half, part_width + block), shape_of((half, part_width + block), BF16),
            flops=2 * taps * half * half * part_width, moved=4 * half * part_width,
        )(meta, docs, *mixed)
        got.append(swapped(other, "sub"))

    cum, dlt, tail, kept = call(
        decay_kernel, "decay", (1,),
        [fixed(all_heads, half), fixed(all_heads, half), fixed(all_heads, 1)],
        [fixed(count, heads), fixed(heads, count), fixed(count, 2 * heads), fixed(8, 3 * heads)],
        [
            shape_of((count, heads), F32), shape_of((heads, count), F32),
            shape_of((count, 2 * heads), BF16), shape_of((8, 3 * heads), BF16),
        ],
        [pltpu.VMEM((heads, count), F32)], flops=2 * count * count * 128, moved=16 * count * heads,
    )(meta, docs, raw, got_raw, decay_log.reshape(all_heads, 1))

    def onward(shard):
        return lax.ppermute(shard, "ctx", [(i, (i + 1) % ctx_size) for i in range(ctx_size)])

    made = []
    for part in range(parts):
        x_cat, bc, state, decay = call(
            functools.partial(
                state_kernel, taps=taps, heads=heads, head_width=head_width, first_lane=part * part_width
            ),
            "state", (1,),
            mix_specs(part, False)
            + [fixed(half, part_width + block), fixed(count, 2 * heads), fixed(8, 3 * heads)],
            [
                fixed(count, part_width), fixed(count, block), fixed(state_width, part_width), fixed(8, part_width),
            ],
            [
                shape_of((count, part_width), BF16), shape_of((count, block), BF16),
                shape_of((state_width, part_width), BF16), shape_of((8, part_width), F32),
            ],
            flops=4 * half * count * part_width, moved=6 * count * part_width,
        )(meta, docs, *mixed, got[part], tail, kept)
        made.append((x_cat, bc, state, decay, onward(state)))

    got_gate = swapped(lax.dynamic_slice_in_dim(gate_input, (1 - sub) * width, width, 1), "sub")
    by_row = lambda n: pl.BlockSpec((CHUNK, n), lambda i, *m: (i, 0))
    skip = skip_gain.reshape(1, all_heads)
    ready = []
    for part in range(parts):
        x_cat, bc, state, decay, arriving = made[part]
        for _ in range(ctx_size // 2 - 1):
            arriving = onward((state.astype(F32) + decay[:1] * arriving.astype(F32)).astype(BF16))
        gate_at = lambda i, m, d, part=part: (lax.rem(i, splits), m[0] * parts + part)
        got_at = lambda i, m, d, part=part: (lax.rem(i, splits), part)
        gated, carry_gate = call(
            functools.partial(
                intra_kernel, head_width=head_width, first_head=part * part_heads, group_heads=part_heads
            ),
            "intra", (chunks,),
            [
                by_row(part_width), by_row(block), by_row(heads),
                pl.BlockSpec((heads, CHUNK), lambda i, *m: (0, i)),
                pl.BlockSpec((CHUNK, part_width), gate_at), pl.BlockSpec((CHUNK, part_width), got_at),
                fixed(1, all_heads),
            ],
            [by_row(part_width), by_row(part_width)],
            [shape_of((count, part_width), F32), shape_of((count, part_width), F32)],
            [
                pltpu.VMEM((state_width, part_width), F32), pltpu.VMEM((8, heads), F32),
                pltpu.VMEM((3 * heads, part_width), BF16), pltpu.VMEM((8, part_width), F32),
                pltpu.VMEM((CHUNK, part_width), F32), pltpu.VMEM((CHUNK, part_width), F32),
                pltpu.VMEM((CHUNK, part_width), F32),
            ],
            flops=10 * count * part_width * CHUNK, moved=14 * count * part_width,
        )(meta, docs, x_cat, bc, cum, dlt, gate_input, got_gate, skip)
        ready.append((gated, carry_gate, bc, arriving))

    divisor = HEADS // GROUPS * head_width
    gain = norm_gain.reshape(1, channels)
    gain_at = lambda part: pl.BlockSpec((1, part_width), lambda i, m: (0, m[0] * parts + part))
    hiddens = []
    for part, (gated, carry_gate, bc, arriving) in enumerate(ready[:-1]):
        hiddens.append(
            call(
                functools.partial(norm_kernel, divisor=divisor), "norm", (chunks,),
                [by_row(part_width), by_row(part_width), by_row(block), fixed(state_width, part_width), gain_at(part)],
                by_row(part_width), shape_of((count, part_width), BF16),
                flops=2 * count * part_width * state_width, moved=10 * count * part_width, prefetch=1,
            )(meta, gated, carry_gate, bc, arriving, gain)
        )

    gated, carry_gate, bc, arriving = ready[-1]
    squares = []
    if not whole_groups:
        total = gated + jnp.dot(bc[:, state_width:], arriving, preferred_element_type=F32) * carry_gate
        mine = jnp.sum(total * total, axis=1, keepdims=True)
        squares = [mine + swapped(mine, "sub")]
    operands = [*hiddens, gated, carry_gate, bc, *squares]
    out_cols = features // tp_size
    mm_cols = min(512, out_cols)
    pair = tp_size == 2
    near_blocks = out_cols // mm_cols
    far_blocks = near_blocks if pair else features // mm_cols
    far_at = (lambda i, m: (1 - m[2]) * near_blocks + i) if pair else (lambda i, m: i)
    far_cols = far_blocks * mm_cols
    far, kept_rows = [], []
    for split in range(splits):
        there = lambda i, m, split=split: ((1 - m[0]) * splits + split, 0)
        here = lambda i, m, split=split: (m[0] * splits + split, 0)
        specs = [pl.BlockSpec((CHUNK, v.shape[1]), at) for at in (there, here) for v in operands]
        specs += [
            fixed(state_width, part_width), gain_at(parts - 1),
            pl.BlockSpec((width, mm_cols), lambda i, m: (0, far_at(i, m))),
        ]
        hidden, send, keep = call(
            functools.partial(project_kernel, ready=len(hiddens), squared=len(squares), divisor=divisor),
            "project", (far_blocks,), specs,
            [
                fixed(2 * CHUNK, width),
                pl.BlockSpec((CHUNK, mm_cols), lambda i, m: (0, i)),
                pl.BlockSpec((CHUNK, mm_cols), lambda i, m: (0, i)),
            ],
            [
                shape_of((2 * CHUNK, width), BF16), shape_of((CHUNK, far_cols), BF16),
                shape_of((CHUNK, far_cols), F32),
            ],
            flops=4 * CHUNK * width * far_cols, moved=2 * width * far_cols, prefetch=1,
        )(meta, *operands, *operands, arriving, gain, out_weight)
        summed = (keep + swapped(send, "sub").astype(F32)).astype(BF16)
        far.append(swapped(summed, "tp") if pair else summed)
        kept_rows.append(hidden)
    if not pair:
        return lax.psum_scatter(jnp.concatenate(far), "tp", scatter_dimension=1, tiled=True)
    send, keep = call(
        product_kernel, "product", (near_blocks,),
        [fixed(2 * CHUNK, width)] * splits
        + [pl.BlockSpec((width, mm_cols), lambda i, m: (0, m[2] * near_blocks + i))],
        [pl.BlockSpec((half, mm_cols), lambda i, m: (0, i)), pl.BlockSpec((half, mm_cols), lambda i, m: (0, i))],
        [shape_of((half, out_cols), BF16), shape_of((half, out_cols), F32)],
        flops=2 * count * width * out_cols, moved=2 * width * out_cols, prefetch=1,
    )(meta, *kept_rows, out_weight)
    near = keep + swapped(send, "sub").astype(F32)
    return (near + jnp.concatenate(far).astype(F32)).astype(BF16)


def solution(mesh):
    in_specs = (
        P(("groups", "ctx", "sub"), "tp"),
        P(("groups", "ctx", "sub"), "tp"),
        P(("groups", "ctx", "sub"), "tp", None, None),
        P(None, "tp"),
        P("tp"),
        P(None, "tp", None, None),
        P("tp", None, None),
        P(("groups", "ctx", "sub"), "tp"),
        P("tp"),
        P("tp"),
        P("tp"),
        P(("tp", "sub"), None),
        P("groups"),
    )
    out_specs = P(("groups", "ctx", "sub"), "tp")
    return jax.shard_map(local, mesh=mesh, in_specs=in_specs, out_specs=out_specs, check_vma=False)
```

```python
import functools

import jax
import jax.numpy as jnp
from jax import lax
from jax.experimental import pallas as pl
from jax.experimental.pallas import tpu as pltpu
from jax.sharding import PartitionSpec as P

HEADS = 128
GROUPS = 8
CHUNK = 128
EPSILON = 1e-05
LOG2E = 1.4426950408889634
CEILING = 126.0
VMEM = 60 << 20
F32 = jnp.float32
BF16 = jnp.bfloat16


def shifted(shard, axis, by):
    peers = lax.axis_size(axis)
    pairs = [(i, i + by) for i in range(peers) if 0 <= i + by < peers]
    return lax.ppermute(shard, axis, pairs)


def swapped(shard, axis):
    return lax.ppermute(shard, axis, [(i, i ^ 1) for i in range(lax.axis_size(axis))])


def after(*values):
    return lax.optimization_barrier(values)


def doc_start(positions, docs_ref):
    start = jnp.zeros_like(positions)
    total = jnp.int32(0)
    for doc in range(docs_ref.shape[0]):
        start = jnp.where(positions >= total, total, start)
        total = total + docs_ref[doc]
    return start


def rows_of(count, first):
    return first + lax.broadcasted_iota(jnp.int32, (count, 1), 0)


def split2(value):
    high = value.astype(BF16)
    return high, (value - high.astype(F32)).astype(BF16)


def split3(value):
    high = value.astype(BF16)
    rest = value - high.astype(F32)
    mid = rest.astype(BF16)
    return high, mid, (rest - mid.astype(F32)).astype(BF16)


def mm(a, b):
    return jnp.dot(a, b, preferred_element_type=F32)


def contract_lanes(a, b):
    return lax.dot_general(a, b, (((1,), (1,)), ((), ())), preferred_element_type=F32)


def silu(value):
    half = 0.5 * value
    return half + half * jnp.tanh(half)


def head_lanes(copies, heads, head_width, lanes, first_lane):
    shape = (copies * heads, lanes)
    head = lax.rem(lax.broadcasted_iota(jnp.int32, shape, 0), heads)
    lane = first_lane + lax.broadcasted_iota(jnp.int32, shape, 1)
    low = head * head_width
    return jnp.where((lane >= low) & (lane < low + head_width), 1.0, 0.0).astype(BF16)


def convolved(first, docs, pieces, store, taps):
    count = pieces[0][0].shape[0]
    rims = pieces[0][1].shape[0]
    start = doc_start(rows_of(count, first), docs) - first
    row = lax.broadcasted_iota(jnp.int32, (count, count), 0)
    col = lax.broadcasted_iota(jnp.int32, (count, count), 1)
    rim_row = lax.broadcasted_iota(jnp.int32, (rims, rims), 0)
    rim_col = lax.broadcasted_iota(jnp.int32, (rims, rims), 1) - rims
    shifts = []
    for back in range(1, taps):
        hit = (col == row - back) & (col >= start)
        rim_hit = (rim_col == rim_row - back) & (rim_col >= start[:rims])
        shifts.append((jnp.where(hit, 1.0, 0.0).astype(BF16), jnp.where(rim_hit, 1.0, 0.0).astype(BF16)))
    for index, (x, rim, w, bias) in enumerate(pieces):
        span = min(256, x.shape[1])
        for low in range(0, x.shape[1], span):
            at = slice(low, low + span)
            value = x[:, at]
            weight = w[:, at].astype(F32)
            summed = bias[:, at] + value.astype(F32) * weight[taps - 1 : taps]
            top = jnp.zeros((rims, span), F32)
            for back in range(1, taps):
                line = weight[taps - 1 - back : taps - back]
                shift, rim_shift = shifts[back - 1]
                summed = summed + mm(shift, value) * line
                top = top + mm(rim_shift, rim[:, at]) * line
            store(index, at, slice(0, rims), silu(summed[:rims] + top).astype(BF16))
            store(index, at, slice(rims, count), silu(summed[rims:]).astype(BF16))


def conv_kernel(meta, docs, x, x_rim, w, bias, s, s_rim, sw, sbias, out, *, taps):
    width = x.shape[1]

    def store(index, at, rows, value):
        out[rows, slice(at.start + index * width, at.stop + index * width)] = value

    first = meta[1] + meta[0] * x.shape[0]
    convolved(first, docs, [(x, x_rim, w, bias), (s, s_rim, sw, sbias)], store, taps)


def decay_kernel(
    meta, docs, own_raw, got_raw, rate, cum_out, dlt_out, tail_out, kept_out, raw,
):
    half = own_raw.shape[1]
    heads, count = raw.shape
    mine = meta[0] == 0
    first = meta[1]
    own_at = pl.ds(pl.multiple_of(meta[0] * half, half), half)
    got_at = pl.ds(pl.multiple_of((1 - meta[0]) * half, half), half)
    last_start = doc_start(first + count - 1, docs)
    raw[:, own_at] = jnp.where(mine, own_raw[:heads], own_raw[heads:])
    raw[:, got_at] = jnp.where(mine, got_raw[:heads], got_raw[heads:])
    value = raw[...]
    size = jnp.maximum(value, 0.0) + jnp.log(1.0 + jnp.exp(-jnp.abs(value)))
    decay = (-LOG2E * jnp.exp(jnp.where(mine, rate[:heads], rate[heads:]))) * size
    row = lax.broadcasted_iota(jnp.int32, (count, count), 0)
    col = lax.broadcasted_iota(jnp.int32, (count, count), 1)
    above = jnp.where(row <= col, 1.0, 0.0).astype(BF16)
    high, mid, low = split3(decay)
    cum = mm(high, above) + (mm(mid, above) + mm(low, above))
    dlt_out[...] = cum - jnp.log2(size)
    end = cum[:, count - 1 :]
    places = first + lax.broadcasted_iota(jnp.int32, (1, count), 1)
    tail = jnp.where(places >= last_start, size * jnp.exp2(end - cum), 0.0)
    high, low = split2(tail.T)
    tail_out[:, :heads] = high
    tail_out[:, heads:] = low
    cum = cum.T
    cum_out[...] = cum
    kept = jnp.exp2(jnp.broadcast_to(cum[count - 1 :], (8, heads)))
    high, mid, low = split3(jnp.where(last_start < first, kept, 0.0))
    kept_out[:, :heads] = high
    kept_out[:, heads : 2 * heads] = mid
    kept_out[:, 2 * heads :] = low


def state_kernel(
    meta, docs, x, x_rim, w, bias, s, s_rim, sw, sbias, got, tail, kept,
    x_out, bc_out, s_out, d_out, *, taps, heads, head_width, first_lane,
):
    half, width = x.shape
    state_width = bc_out.shape[1] // 2
    own_row = pl.multiple_of(meta[0] * half, half)
    got_at = pl.ds(pl.multiple_of((1 - meta[0]) * half, half), half)

    def store(index, at, rows, value):
        place = pl.ds(pl.multiple_of(own_row + rows.start, 16), rows.stop - rows.start)
        if index:
            bc_out[place, at] = value
        else:
            x_out[place, at] = value

    convolved(meta[1] + meta[0] * half, docs, [(x, x_rim, w, bias), (s, s_rim, sw, sbias)], store, taps)
    x_out[got_at, :] = got[:, :width]
    bc_out[got_at, :] = got[:, width:]
    b = bc_out[:, :state_width].T
    span = min(256, width)
    for low in range(0, width, span):
        at = slice(low, low + span)
        tails = mm(tail[...], head_lanes(2, heads, head_width, span, first_lane + low))
        weighted = (x_out[:, at].astype(F32) * tails).astype(BF16)
        s_out[:, at] = mm(b, weighted).astype(BF16)
        d_out[:, at] = mm(kept[...], head_lanes(3, heads, head_width, span, first_lane + low))


def intra_kernel(
    meta, docs, x, bc, cum, dlt, gate_own, gate_got, gain,
    a_out, f_out, state, base, spread, skip, reach, into, tail,
    *, head_width, first_head, group_heads,
):
    step = pl.program_id(0)
    count, width = x.shape
    heads = cum.shape[1]
    state_width = bc.shape[1] // 2
    first = meta[1] + step * count

    @pl.when(step == 0)
    def _():
        state[...] = jnp.zeros_like(state)
        base[...] = jnp.zeros_like(base)
        spread[...] = head_lanes(3, heads, head_width, width, first_head * head_width)
        mine = jnp.where(meta[0] == 0, gain[:, :heads], gain[:, heads:])
        skip[...] = mm(jnp.concatenate(split3(jnp.broadcast_to(mine, (8, heads))), axis=1), spread[...])

    starts = doc_start(rows_of(count, first), docs)
    last_start = doc_start(first + count - 1, docs)
    here = cum[...]
    before = base[:1, :]
    end = here[count - 1 :]

    def spread_over(value):
        return mm(jnp.concatenate(split2(value), axis=1), spread[: 2 * heads])

    reach[...] = spread_over(jnp.where(starts < first, jnp.exp2(here - before), 0.0))
    into[...] = spread_over(jnp.where(starts < meta[1], jnp.exp2(here), 0.0))
    to_end = jnp.exp2(end - dlt[...].T)
    tail[...] = spread_over(jnp.where(rows_of(count, first) >= last_start, to_end, 0.0))
    kept = jnp.broadcast_to(jnp.where(last_start < first, jnp.exp2(end - before), 0.0), (8, heads))
    kept = mm(jnp.concatenate(split3(kept), axis=1), spread[...])[:1]
    row = lax.broadcasted_iota(jnp.int32, (count, count), 0)
    col = lax.broadcasted_iota(jnp.int32, (count, count), 1)
    is_own = (step * count) // (count * (pl.num_programs(0) // 2)) == meta[0]
    low_lanes = lax.broadcasted_iota(jnp.int32, (count, 2 * head_width), 1) < head_width
    zero = jnp.zeros((count, 2 * head_width), BF16)
    b = bc[:, :state_width]
    c = bc[:, state_width:]
    b_turned = b.T
    scores = jnp.where((col <= row) & (col >= starts - first), contract_lanes(c, b), 0.0)
    for head in range(0, group_heads, 2):
        at = slice(head * head_width, (head + 2) * head_width)
        pair = []
        for k in (first_head + head, first_head + head + 1):
            exponent = jnp.minimum(here[:, k : k + 1] - dlt[k : k + 1, :], CEILING)
            pair.append((jnp.exp2(exponent) * scores).astype(BF16))
        value = x[:, at]
        stacked = jnp.concatenate([jnp.where(low_lanes, value, zero), jnp.where(low_lanes, zero, value)], axis=0)
        within = mm(jnp.concatenate(pair, axis=1), stacked)
        old = state[:, at]
        carried = mm(c, old.astype(BF16)) * reach[:, at]
        x_part = value.astype(F32)
        y = within + carried + x_part * skip[:1, at]
        gate = silu(jnp.where(is_own, gate_own[:, at], gate_got[:, at]).astype(F32))
        a_out[:, at] = y * gate
        f_out[:, at] = gate * into[:, at]
        fresh = mm(b_turned, (x_part * tail[:, at]).astype(BF16))
        state[:, at] = old * kept[:, at] + fresh
    base[...] = jnp.broadcast_to(end, base.shape)


def normed(a, f, bc, incoming, gain, squares, divisor):
    state_width = bc.shape[1] // 2
    gated = a[...] + mm(bc[:, state_width:], incoming[...]) * f[...]
    total = jnp.sum(gated * gated, axis=1, keepdims=True) if squares is None else squares[...]
    return (gated * lax.rsqrt(total / divisor + EPSILON) * gain[...]).astype(BF16)


def norm_kernel(meta, a, f, bc, incoming, gain, hidden, *, divisor):
    hidden[...] = normed(a, f, bc, incoming, gain, None, divisor)


def project_kernel(meta, *refs, ready, squared, divisor):
    a, f, bc, incoming, gain = refs[ready : ready + 5]
    w, hidden, send, keep = refs[-4:]
    width = a.shape[1]

    @pl.when(pl.program_id(0) == 0)
    def _():
        for group, part in enumerate(refs[:ready]):
            hidden[:, group * width : (group + 1) * width] = part[...]
        squares = refs[ready + 5] if squared else None
        hidden[:, ready * width :] = normed(a, f, bc, incoming, gain, squares, divisor)

    multiply(meta, hidden, w, send, keep)


def multiply(meta, hidden, w, send, keep):
    half = send.shape[0]
    there = pl.ds(pl.multiple_of((1 - meta[0]) * half, half), half)
    here = pl.ds(pl.multiple_of(meta[0] * half, half), half)
    send[...] = mm(hidden[there, :], w[...]).astype(BF16)
    keep[...] = mm(hidden[here, :], w[...])


def add_kernel(a, b, out):
    out[...] = a[...] + b[...].astype(F32)


def local(
    x_input, gate_input, state_proj, mix_weight, mix_bias, state_weight, state_bias,
    step_raw, decay_log, skip_gain, norm_gain, out_weight, doc_lengths,
):
    half, channels = x_input.shape
    all_heads = step_raw.shape[1]
    groups, _, state_width = state_proj.shape[1:]
    taps = mix_weight.shape[0]
    features = out_weight.shape[1]
    head_width = channels // all_heads
    heads = all_heads // 2
    width = channels // 2
    count = 2 * half
    whole_groups = groups % 2 == 0
    parts = groups // 2 if whole_groups else groups
    part_heads = heads // parts
    part_width = part_heads * head_width
    block = 2 * state_width
    chunks = count // CHUNK
    splits = half // CHUNK
    sub = lax.axis_index("sub").astype(jnp.int32)
    ctx = lax.axis_index("ctx").astype(jnp.int32)
    tp = lax.axis_index("tp").astype(jnp.int32)
    tp_size = lax.axis_size("tp")
    ctx_size = lax.axis_size("ctx")
    docs = doc_lengths.astype(jnp.int32)
    meta = jnp.stack([sub, ctx * count, tp])
    params = pltpu.CompilerParams(vmem_limit_bytes=VMEM)
    fixed = lambda *shape: pl.BlockSpec(shape, lambda i, *m: (0,) * len(shape))
    shape_of = jax.ShapeDtypeStruct

    def call(body, name, grid, in_specs, out_specs, out_shape, scratch=(), flops=0, moved=0, prefetch=2):
        return pl.pallas_call(
            body,
            grid_spec=pltpu.PrefetchScalarGridSpec(
                num_scalar_prefetch=prefetch, grid=grid, in_specs=in_specs, out_specs=out_specs,
                scratch_shapes=list(scratch),
            ),
            out_shape=out_shape,
            compiler_params=params,
            cost_estimate=pl.CostEstimate(flops=flops, bytes_accessed=moved, transcendentals=0),
            name=name,
        )

    s_input = state_proj.reshape(half, groups * block)
    s_weight = state_weight.reshape(taps, groups * block)
    s_bias = state_bias.reshape(1, groups * block)
    bias = mix_bias.reshape(1, channels)
    rims = 16
    s_rim = state_proj[half - rims :].reshape(rims, groups * block)
    rim = shifted(jnp.concatenate([x_input[half - rims :], s_rim], axis=1), ("ctx", "sub"), 1)
    raw = step_raw.T
    got_raw = swapped(raw, "sub")
    rim, got_raw = after(rim, got_raw)
    mixed = (x_input, rim, mix_weight, bias, s_input, rim, s_weight, s_bias)

    def mix_specs(part, other):
        at = lambda m: (1 - m[0] if other else m[0]) * parts + part
        s_at = at if whole_groups else (lambda m: 0)
        rim_at = lambda m: channels // block + s_at(m)
        specs = []
        for size, places in ((part_width, (at, at, at, at)), (block, (s_at, rim_at, s_at, s_at))):
            for rows, place in zip((half, rims, taps, 1), places):
                specs.append(pl.BlockSpec((rows, size), lambda i, m, d, place=place: (0, place(m))))
        return specs

    got = []
    for part in range(parts):
        other = call(
            functools.partial(conv_kernel, taps=taps), "conv", (1,), mix_specs(part, True),
            fixed(half, part_width + block), shape_of((half, part_width + block), BF16),
            flops=2 * taps * half * half * part_width, moved=4 * half * part_width,
        )(meta, docs, *mixed)
        got.append(swapped(other, "sub"))

    cum, dlt, tail, kept = call(
        decay_kernel, "decay", (1,),
        [fixed(all_heads, half), fixed(all_heads, half), fixed(all_heads, 1)],
        [fixed(count, heads), fixed(heads, count), fixed(count, 2 * heads), fixed(8, 3 * heads)],
        [
            shape_of((count, heads), F32), shape_of((heads, count), F32),
            shape_of((count, 2 * heads), BF16), shape_of((8, 3 * heads), BF16),
        ],
        [pltpu.VMEM((heads, count), F32)], flops=2 * count * count * 128, moved=16 * count * heads,
    )(meta, docs, raw, got_raw, decay_log.reshape(all_heads, 1))

    def onward(shard):
        return lax.ppermute(shard, "ctx", [(i, (i + 1) % ctx_size) for i in range(ctx_size)])

    made = []
    for part in range(parts):
        x_cat, bc, state, decay = call(
            functools.partial(
                state_kernel, taps=taps, heads=heads, head_width=head_width, first_lane=part * part_width
            ),
            "state", (1,),
            mix_specs(part, False)
            + [fixed(half, part_width + block), fixed(count, 2 * heads), fixed(8, 3 * heads)],
            [
                fixed(count, part_width), fixed(count, block), fixed(state_width, part_width), fixed(8, part_width),
            ],
            [
                shape_of((count, part_width), BF16), shape_of((count, block), BF16),
                shape_of((state_width, part_width), BF16), shape_of((8, part_width), F32),
            ],
            flops=4 * half * count * part_width, moved=6 * count * part_width,
        )(meta, docs, *mixed, got[part], tail, kept)
        made.append((x_cat, bc, state, decay, onward(state)))

    got_gate = swapped(lax.dynamic_slice_in_dim(gate_input, (1 - sub) * width, width, 1), "sub")
    by_row = lambda n: pl.BlockSpec((CHUNK, n), lambda i, *m: (i, 0))
    skip = skip_gain.reshape(1, all_heads)
    ready = []
    for part in range(parts):
        x_cat, bc, state, decay, arriving = made[part]
        if ready:
            arriving, gate = after(arriving, ready[-1][0])
            ready[-1] = (gate, *ready[-1][1:])
        for _ in range(ctx_size // 2 - 1):
            leaving = (state.astype(F32) + decay[:1] * arriving.astype(F32)).astype(BF16)
            leaving, x_cat = after(leaving, x_cat)
            arriving = onward(leaving)
        gate_at = lambda i, m, d, part=part: (lax.rem(i, splits), m[0] * parts + part)
        got_at = lambda i, m, d, part=part: (lax.rem(i, splits), part)
        gated, carry_gate = call(
            functools.partial(
                intra_kernel, head_width=head_width, first_head=part * part_heads, group_heads=part_heads
            ),
            "intra", (chunks,),
            [
                by_row(part_width), by_row(block), by_row(heads),
                pl.BlockSpec((heads, CHUNK), lambda i, *m: (0, i)),
                pl.BlockSpec((CHUNK, part_width), gate_at), pl.BlockSpec((CHUNK, part_width), got_at),
                fixed(1, all_heads),
            ],
            [by_row(part_width), by_row(part_width)],
            [shape_of((count, part_width), F32), shape_of((count, part_width), F32)],
            [
                pltpu.VMEM((state_width, part_width), F32), pltpu.VMEM((8, heads), F32),
                pltpu.VMEM((3 * heads, part_width), BF16), pltpu.VMEM((8, part_width), F32),
                pltpu.VMEM((CHUNK, part_width), F32), pltpu.VMEM((CHUNK, part_width), F32),
                pltpu.VMEM((CHUNK, part_width), F32),
            ],
            flops=10 * count * part_width * CHUNK, moved=14 * count * part_width,
        )(meta, docs, x_cat, bc, cum, dlt, gate_input, got_gate, skip)
        ready.append((gated, carry_gate, bc, arriving))

    divisor = HEADS // GROUPS * head_width
    gain = norm_gain.reshape(1, channels)
    gain_at = lambda part: pl.BlockSpec((1, part_width), lambda i, m: (0, m[0] * parts + part))
    hiddens = []
    for part, (gated, carry_gate, bc, arriving) in enumerate(ready[:-1]):
        hiddens.append(
            call(
                functools.partial(norm_kernel, divisor=divisor), "norm", (chunks,),
                [by_row(part_width), by_row(part_width), by_row(block), fixed(state_width, part_width), gain_at(part)],
                by_row(part_width), shape_of((count, part_width), BF16),
                flops=2 * count * part_width * state_width, moved=10 * count * part_width, prefetch=1,
            )(meta, gated, carry_gate, bc, arriving, gain)
        )

    gated, carry_gate, bc, arriving = ready[-1]
    if hiddens:
        arriving, hiddens[-1] = after(arriving, hiddens[-1])
    squares = []
    if not whole_groups:
        total = gated + jnp.dot(bc[:, state_width:], arriving, preferred_element_type=F32) * carry_gate
        mine = jnp.sum(total * total, axis=1, keepdims=True)
        squares = [mine + swapped(mine, "sub")]
    out_cols = features // tp_size
    mm_cols = min(512, out_cols)
    pair = tp_size == 2
    near_blocks = out_cols // mm_cols
    row_specs = [pl.BlockSpec((half, mm_cols), lambda i, m: (0, i))] * 2

    def product(first, blocks, body, name, operands, specs, outs, out_shapes):
        cols = blocks * mm_cols
        return call(
            body, name, (blocks,),
            specs + [pl.BlockSpec((width, mm_cols), lambda i, m: (0, first(m) + i))],
            outs + row_specs,
            out_shapes + [shape_of((half, cols), BF16), shape_of((half, cols), F32)],
            flops=2 * count * width * cols, moved=2 * width * cols, prefetch=1,
        )(meta, *operands, out_weight)

    far_first = (lambda m: (1 - m[2]) * near_blocks) if pair else (lambda m: 0)
    far_blocks = near_blocks if pair else features // mm_cols
    lead = max(far_blocks // 2, 1)
    operands = [*hiddens, gated, carry_gate, bc, arriving, gain, *squares]
    specs = [fixed(*v.shape) for v in operands]
    specs[len(hiddens) + 4] = gain_at(parts - 1)
    hidden, send, keep = product(
        far_first, lead, functools.partial(project_kernel, ready=len(hiddens), squared=len(squares), divisor=divisor),
        "project", operands, specs, [fixed(count, width)], [shape_of((count, width), BF16)],
    )
    far = []
    rest = [(lambda m: far_first(m) + lead, far_blocks - lead)] if far_blocks > lead else []
    if pair:
        rest.append((lambda m: m[2] * near_blocks, near_blocks))
    for first, blocks in rest:
        summed = (keep + swapped(send, "sub").astype(F32)).astype(BF16)
        hidden, summed = after(hidden, summed)
        far.append(swapped(summed, "tp") if pair else summed)
        send, keep = product(first, blocks, multiply, "product", [hidden], [fixed(count, width)], [], [])
    if not pair:
        far.append((keep + swapped(send, "sub").astype(F32)).astype(BF16))
        return lax.psum_scatter(jnp.concatenate(far, axis=1), "tp", scatter_dimension=1, tiled=True)
    lead_cols = far[0].shape[1]
    early = call(
        add_kernel, "add", (1,), [fixed(half, lead_cols)] * 2, fixed(half, lead_cols),
        shape_of((half, lead_cols), F32), flops=1 << 38, moved=10 * half * lead_cols, prefetch=0,
    )(keep, far[0])
    late = [keep[:, lead_cols:] + v.astype(F32) for v in far[1:]]
    return (jnp.concatenate([early, *late], axis=1) + swapped(send, "sub").astype(F32)).astype(BF16)


def solution(mesh):
    in_specs = (
        P(("groups", "ctx", "sub"), "tp"),
        P(("groups", "ctx", "sub"), "tp"),
        P(("groups", "ctx", "sub"), "tp", None, None),
        P(None, "tp"),
        P("tp"),
        P(None, "tp", None, None),
        P("tp", None, None),
        P(("groups", "ctx", "sub"), "tp"),
        P("tp"),
        P("tp"),
        P("tp"),
        P(("tp", "sub"), None),
        P("groups"),
    )
    out_specs = P(("groups", "ctx", "sub"), "tp")
    return jax.shard_map(local, mesh=mesh, in_specs=in_specs, out_specs=out_specs, check_vma=False)
```

```python
import functools

import jax
import jax.numpy as jnp
from jax import lax
from jax.experimental import pallas as pl
from jax.experimental.pallas import tpu as pltpu
from jax.sharding import PartitionSpec as P

HEADS = 128
GROUPS = 8
CHUNK = 128
EPSILON = 1e-05
LOG2E = 1.4426950408889634
CEILING = 126.0
VMEM = 32 << 20
F32 = jnp.float32
BF16 = jnp.bfloat16


def shifted(shard, axis, by):
    peers = lax.axis_size(axis)
    pairs = [(i, i + by) for i in range(peers) if 0 <= i + by < peers]
    return lax.ppermute(shard, axis, pairs)


def swapped(shard, axis):
    return lax.ppermute(shard, axis, [(i, i ^ 1) for i in range(lax.axis_size(axis))])


def after(*values):
    return lax.optimization_barrier(values)


def doc_start(positions, docs_ref):
    start = jnp.zeros_like(positions)
    total = jnp.int32(0)
    for doc in range(docs_ref.shape[0]):
        start = jnp.where(positions >= total, total, start)
        total = total + docs_ref[doc]
    return start


def rows_of(count, first):
    return first + lax.broadcasted_iota(jnp.int32, (count, 1), 0)


def split2(value):
    high = value.astype(BF16)
    return high, (value - high.astype(F32)).astype(BF16)


def split3(value):
    high = value.astype(BF16)
    rest = value - high.astype(F32)
    mid = rest.astype(BF16)
    return high, mid, (rest - mid.astype(F32)).astype(BF16)


def mm(a, b):
    return jnp.dot(a, b, preferred_element_type=F32)


def contract_lanes(a, b):
    return lax.dot_general(a, b, (((1,), (1,)), ((), ())), preferred_element_type=F32)


def silu(value):
    half = 0.5 * value
    return half + half * jnp.tanh(half)


def head_lanes(copies, heads, head_width, lanes, first_lane):
    shape = (copies * heads, lanes)
    head = lax.rem(lax.broadcasted_iota(jnp.int32, shape, 0), heads)
    lane = first_lane + lax.broadcasted_iota(jnp.int32, shape, 1)
    low = head * head_width
    return jnp.where((lane >= low) & (lane < low + head_width), 1.0, 0.0).astype(BF16)


def convolved(first, docs, pieces, store, taps):
    count = pieces[0][0].shape[0]
    rims = pieces[0][1].shape[0]
    start = doc_start(rows_of(count, first), docs) - first
    row = lax.broadcasted_iota(jnp.int32, (count, count), 0)
    col = lax.broadcasted_iota(jnp.int32, (count, count), 1)
    rim_row = lax.broadcasted_iota(jnp.int32, (rims, rims), 0)
    rim_col = lax.broadcasted_iota(jnp.int32, (rims, rims), 1) - rims
    shifts = []
    for back in range(1, taps):
        hit = (col == row - back) & (col >= start)
        rim_hit = (rim_col == rim_row - back) & (rim_col >= start[:rims])
        shifts.append((jnp.where(hit, 1.0, 0.0).astype(BF16), jnp.where(rim_hit, 1.0, 0.0).astype(BF16)))
    for index, (x, rim, w, bias) in enumerate(pieces):
        weights = w[...].astype(F32)
        if index:
            weights = jnp.concatenate([weights[:, 0, 0, :], weights[:, 0, 1, :]], axis=1)
        span = min(256, x.shape[1])
        for low in range(0, x.shape[1], span):
            at = slice(low, low + span)
            value = x[:, at]
            weight = weights[:, at]
            summed = bias[:, at] + value.astype(F32) * weight[taps - 1 : taps]
            top = jnp.zeros((rims, span), F32)
            for back in range(1, taps):
                line = weight[taps - 1 - back : taps - back]
                shift, rim_shift = shifts[back - 1]
                summed = summed + mm(shift, value) * line
                top = top + mm(rim_shift, rim[:, at]) * line
            store(index, at, slice(0, rims), silu(summed[:rims] + top).astype(BF16))
            store(index, at, slice(rims, count), silu(summed[rims:]).astype(BF16))


def conv_kernel(meta, docs, x, x_rim, w, bias, s, s_rim, sw, sbias, out, *, taps):
    width = x.shape[1]

    def store(index, at, rows, value):
        out[rows, slice(at.start + index * width, at.stop + index * width)] = value

    first = meta[1] + meta[0] * x.shape[0]
    convolved(first, docs, [(x, x_rim, w, bias), (s, s_rim, sw, sbias)], store, taps)


def decay_kernel(
    meta, docs, own_raw, got_raw, rate, cum_out, dlt_out, tail_out, kept_out, raw,
):
    half = own_raw.shape[1]
    heads, count = raw.shape
    mine = meta[0] == 0
    first = meta[1]
    own_at = pl.ds(pl.multiple_of(meta[0] * half, half), half)
    got_at = pl.ds(pl.multiple_of((1 - meta[0]) * half, half), half)
    last_start = doc_start(first + count - 1, docs)
    raw[:, own_at] = jnp.where(mine, own_raw[:heads], own_raw[heads:])
    raw[:, got_at] = jnp.where(mine, got_raw[:heads], got_raw[heads:])
    value = raw[...]
    size = jnp.maximum(value, 0.0) + jnp.log(1.0 + jnp.exp(-jnp.abs(value)))
    wide = (heads, 2 * heads)
    own_head = lax.broadcasted_iota(jnp.int32, wide, 0) + meta[0] * heads
    chosen = own_head == lax.broadcasted_iota(jnp.int32, wide, 1)
    rates = jnp.sum(jnp.where(chosen, rate[...], 0.0), axis=1, keepdims=True)
    decay = (-LOG2E * jnp.exp(rates)) * size
    row = lax.broadcasted_iota(jnp.int32, (count, count), 0)
    col = lax.broadcasted_iota(jnp.int32, (count, count), 1)
    above = jnp.where(row <= col, 1.0, 0.0).astype(BF16)
    high, mid, low = split3(decay)
    cum = mm(high, above) + (mm(mid, above) + mm(low, above))
    dlt_out[...] = cum - jnp.log2(size)
    end = cum[:, count - 1 :]
    places = first + lax.broadcasted_iota(jnp.int32, (1, count), 1)
    tail = jnp.where(places >= last_start, size * jnp.exp2(end - cum), 0.0)
    high, low = split2(tail.T)
    tail_out[:, :heads] = high
    tail_out[:, heads:] = low
    cum = cum.T
    cum_out[...] = cum
    kept = jnp.exp2(jnp.broadcast_to(cum[count - 1 :], (8, heads)))
    high, mid, low = split3(jnp.where(last_start < first, kept, 0.0))
    kept_out[:, :heads] = high
    kept_out[:, heads : 2 * heads] = mid
    kept_out[:, 2 * heads :] = low


def state_kernel(
    meta, docs, x, x_rim, w, bias, s, s_rim, sw, sbias, got, tail, kept,
    x_out, bc_out, s_out, d_out, *, taps, heads, head_width, first_lane,
):
    half, width = x.shape
    state_width = bc_out.shape[1] // 2
    own_row = pl.multiple_of(meta[0] * half, half)
    got_at = pl.ds(pl.multiple_of((1 - meta[0]) * half, half), half)

    def store(index, at, rows, value):
        place = pl.ds(pl.multiple_of(own_row + rows.start, 16), rows.stop - rows.start)
        if index:
            bc_out[place, at] = value
        else:
            x_out[place, at] = value

    convolved(meta[1] + meta[0] * half, docs, [(x, x_rim, w, bias), (s, s_rim, sw, sbias)], store, taps)
    x_out[got_at, :] = got[:, :width]
    bc_out[got_at, :] = got[:, width:]
    b = bc_out[:, :state_width].T
    span = min(256, width)
    for low in range(0, width, span):
        at = slice(low, low + span)
        tails = mm(tail[...], head_lanes(2, heads, head_width, span, first_lane + low))
        weighted = (x_out[:, at].astype(F32) * tails).astype(BF16)
        s_out[:, at] = mm(b, weighted).astype(BF16)
        d_out[:, at] = mm(kept[...], head_lanes(3, heads, head_width, span, first_lane + low))[:1]


def intra_kernel(
    meta, docs, x, bc, cum, dlt, gate_own, gate_got, gain,
    a_out, f_out, state, base, spread, skip, reach, into, tail,
    *, head_width, first_head, group_heads,
):
    step = pl.program_id(0)
    count, width = x.shape
    heads = cum.shape[1]
    state_width = bc.shape[1] // 2
    first = meta[1] + step * count

    @pl.when(step == 0)
    def _():
        state[...] = jnp.zeros_like(state)
        base[...] = jnp.zeros_like(base)
        spread[...] = head_lanes(3, heads, head_width, width, first_head * head_width)
        mine = jnp.where(meta[0] == 0, gain[:, :heads], gain[:, heads:])
        skip[...] = mm(jnp.concatenate(split3(jnp.broadcast_to(mine, (8, heads))), axis=1), spread[...])

    starts = doc_start(rows_of(count, first), docs)
    last_start = doc_start(first + count - 1, docs)
    here = cum[...]
    before = base[:1, :]
    end = here[count - 1 :]

    def spread_over(value):
        return mm(jnp.concatenate(split2(value), axis=1), spread[: 2 * heads])

    reach[...] = spread_over(jnp.where(starts < first, jnp.exp2(here - before), 0.0))
    into[...] = spread_over(jnp.where(starts < meta[1], jnp.exp2(here), 0.0))
    to_end = jnp.exp2(end - dlt[...].T)
    tail[...] = spread_over(jnp.where(rows_of(count, first) >= last_start, to_end, 0.0))
    kept = jnp.broadcast_to(jnp.where(last_start < first, jnp.exp2(end - before), 0.0), (8, heads))
    kept = mm(jnp.concatenate(split3(kept), axis=1), spread[...])[:1]
    row = lax.broadcasted_iota(jnp.int32, (count, count), 0)
    col = lax.broadcasted_iota(jnp.int32, (count, count), 1)
    is_own = (step * count) // (count * (pl.num_programs(0) // 2)) == meta[0]
    low_lanes = lax.broadcasted_iota(jnp.int32, (count, 2 * head_width), 1) < head_width
    zero = jnp.zeros((count, 2 * head_width), BF16)
    b = bc[:, :state_width]
    c = bc[:, state_width:]
    b_turned = b.T
    scores = jnp.where((col <= row) & (col >= starts - first), contract_lanes(c, b), 0.0)
    for head in range(0, group_heads, 2):
        at = slice(head * head_width, (head + 2) * head_width)
        pair = []
        for k in (first_head + head, first_head + head + 1):
            exponent = jnp.minimum(here[:, k : k + 1] - dlt[k : k + 1, :], CEILING)
            pair.append((jnp.exp2(exponent) * scores).astype(BF16))
        value = x[:, at]
        stacked = jnp.concatenate([jnp.where(low_lanes, value, zero), jnp.where(low_lanes, zero, value)], axis=0)
        within = mm(jnp.concatenate(pair, axis=1), stacked)
        old = state[:, at]
        carried = mm(c, old.astype(BF16)) * reach[:, at]
        x_part = value.astype(F32)
        y = within + carried + x_part * skip[:1, at]
        gate = silu(jnp.where(is_own, gate_own[:, at], gate_got[:, at]).astype(F32))
        a_out[:, at] = y * gate
        f_out[:, at] = gate * into[:, at]
        fresh = mm(b_turned, (x_part * tail[:, at]).astype(BF16))
        state[:, at] = old * kept[:, at] + fresh
    base[...] = jnp.broadcast_to(end, base.shape)


def normed(a, f, bc, incoming, gain, squares, divisor):
    state_width = bc.shape[1] // 2
    gated = a[...] + mm(bc[:, state_width:], incoming[...]) * f[...]
    total = jnp.sum(gated * gated, axis=1, keepdims=True) if squares is None else squares[...]
    return (gated * lax.rsqrt(total / divisor + EPSILON) * gain[...]).astype(BF16)


def norm_kernel(meta, a, f, bc, incoming, gain, hidden, *, divisor):
    hidden[...] = normed(a, f, bc, incoming, gain, None, divisor)


def project_kernel(meta, *refs, ready, squared, divisor):
    a, f, bc, incoming, gain = refs[ready : ready + 5]
    w, hidden, send, keep = refs[-4:]
    width = a.shape[1]

    @pl.when(pl.program_id(0) == 0)
    def _():
        for group, part in enumerate(refs[:ready]):
            hidden[:, group * width : (group + 1) * width] = part[...]
        squares = refs[ready + 5] if squared else None
        hidden[:, ready * width :] = normed(a, f, bc, incoming, gain, squares, divisor)

    multiply(meta, hidden, w, send, keep)


def multiply(meta, hidden, w, send, keep):
    half = send.shape[0]
    there = pl.ds(pl.multiple_of((1 - meta[0]) * half, half), half)
    here = pl.ds(pl.multiple_of(meta[0] * half, half), half)
    send[...] = mm(hidden[there, :], w[...]).astype(BF16)
    keep[...] = mm(hidden[here, :], w[...])


def add_kernel(a, b, out):
    out[...] = a[...] + b[...].astype(F32)


def local(
    x_input, gate_input, state_proj, mix_weight, mix_bias, state_weight, state_bias,
    step_raw, decay_log, skip_gain, norm_gain, out_weight, doc_lengths,
):
    half, channels = x_input.shape
    all_heads = step_raw.shape[1]
    groups, _, state_width = state_proj.shape[1:]
    taps = mix_weight.shape[0]
    features = out_weight.shape[1]
    head_width = channels // all_heads
    heads = all_heads // 2
    width = channels // 2
    count = 2 * half
    whole_groups = groups % 2 == 0
    parts = groups // 2 if whole_groups else groups
    part_heads = heads // parts
    part_width = part_heads * head_width
    block = 2 * state_width
    chunks = count // CHUNK
    splits = half // CHUNK
    sub = lax.axis_index("sub").astype(jnp.int32)
    ctx = lax.axis_index("ctx").astype(jnp.int32)
    tp = lax.axis_index("tp").astype(jnp.int32)
    tp_size = lax.axis_size("tp")
    ctx_size = lax.axis_size("ctx")
    docs = doc_lengths.astype(jnp.int32)
    meta = jnp.stack([sub, ctx * count, tp])
    params = pltpu.CompilerParams(vmem_limit_bytes=VMEM)
    fixed = lambda *shape: pl.BlockSpec(shape, lambda i, *m: (0,) * len(shape))
    shape_of = jax.ShapeDtypeStruct

    def call(body, name, grid, in_specs, out_specs, out_shape, scratch=(), flops=0, moved=0, prefetch=2):
        kernel = pl.pallas_call(
            body,
            grid_spec=pltpu.PrefetchScalarGridSpec(
                num_scalar_prefetch=prefetch, grid=grid, in_specs=in_specs, out_specs=out_specs,
                scratch_shapes=list(scratch),
            ),
            out_shape=out_shape,
            compiler_params=params,
            cost_estimate=pl.CostEstimate(flops=flops, bytes_accessed=moved, transcendentals=0),
            name=name,
        )
        return lambda *operands: kernel(
            *(pltpu.with_memory_space_constraint(v, pltpu.HBM) if any(v is p for p in pinned) else v for v in operands)
        )

    s_input = state_proj.reshape(half, groups * block)
    s_bias = state_bias.reshape(1, groups * block)
    bias = mix_bias.reshape(1, channels)
    skip = skip_gain.reshape(1, all_heads)
    gain = norm_gain.reshape(1, channels)
    rate = decay_log.reshape(1, all_heads)
    pinned = [
        meta, docs, x_input, gate_input, mix_weight, bias, state_weight, s_bias, skip, gain, rate, out_weight
    ]
    rims = 16
    s_rim = state_proj[half - rims :].reshape(rims, groups * block)
    rim = shifted(jnp.concatenate([x_input[half - rims :], s_rim], axis=1), ("ctx", "sub"), 1)
    raw = step_raw.T
    got_raw = swapped(raw, "sub")
    rim, got_raw = after(rim, got_raw)
    mixed = (x_input, rim, mix_weight, bias, s_input, rim, state_weight, s_bias)

    def mix_specs(part, other):
        at = lambda m: (1 - m[0] if other else m[0]) * parts + part
        s_at = at if whole_groups else (lambda m: 0)
        rim_at = lambda m: channels // block + s_at(m)
        specs = []
        for size, places in ((part_width, (at, at, at, at)), (block, (s_at, rim_at, s_at, s_at))):
            for rows, place in zip((half, rims, taps, 1), places):
                specs.append(pl.BlockSpec((rows, size), lambda i, m, d, place=place: (0, place(m))))
        specs[6] = pl.BlockSpec((taps, 1, 2, state_width), lambda i, m, d: (0, s_at(m), 0, 0))
        return specs

    got = []
    for part in range(parts):
        other = call(
            functools.partial(conv_kernel, taps=taps), "conv", (1,), mix_specs(part, True),
            fixed(half, part_width + block), shape_of((half, part_width + block), BF16),
            flops=2 * taps * half * half * part_width, moved=4 * half * part_width,
        )(meta, docs, *mixed)
        got.append(swapped(other, "sub"))

    cum, dlt, tail, kept = call(
        decay_kernel, "decay", (1,),
        [fixed(all_heads, half), fixed(all_heads, half), fixed(1, all_heads)],
        [fixed(count, heads), fixed(heads, count), fixed(count, 2 * heads), fixed(8, 3 * heads)],
        [
            shape_of((count, heads), F32), shape_of((heads, count), F32),
            shape_of((count, 2 * heads), BF16), shape_of((8, 3 * heads), BF16),
        ],
        [pltpu.VMEM((heads, count), F32)], flops=2 * count * count * 128, moved=16 * count * heads,
    )(meta, docs, raw, got_raw, rate)

    def onward(shard):
        return lax.ppermute(shard, "ctx", [(i, (i + 1) % ctx_size) for i in range(ctx_size)])

    made = []
    for part in range(parts):
        x_cat, bc, state, decay = call(
            functools.partial(
                state_kernel, taps=taps, heads=heads, head_width=head_width, first_lane=part * part_width
            ),
            "state", (1,),
            mix_specs(part, False)
            + [fixed(half, part_width + block), fixed(count, 2 * heads), fixed(8, 3 * heads)],
            [
                fixed(count, part_width), fixed(count, block), fixed(state_width, part_width), fixed(1, part_width),
            ],
            [
                shape_of((count, part_width), BF16), shape_of((count, block), BF16),
                shape_of((state_width, part_width), BF16), shape_of((1, part_width), F32),
            ],
            flops=4 * half * count * part_width, moved=6 * count * part_width,
        )(meta, docs, *mixed, got[part], tail, kept)
        made.append((x_cat, bc, state, decay, onward(state)))

    got_gate = swapped(lax.dynamic_slice_in_dim(gate_input, (1 - sub) * width, width, 1), "sub")
    by_row = lambda n: pl.BlockSpec((CHUNK, n), lambda i, *m: (i, 0))
    ready = []
    for part in range(parts):
        x_cat, bc, state, decay, arriving = made[part]
        if ready:
            arriving, gate = after(arriving, ready[-1][0])
            ready[-1] = (gate, *ready[-1][1:])
        for _ in range(ctx_size // 2 - 1):
            leaving = (state.astype(F32) + decay * arriving.astype(F32)).astype(BF16)
            leaving, x_cat = after(leaving, x_cat)
            arriving = onward(leaving)
        gate_at = lambda i, m, d, part=part: (lax.rem(i, splits), m[0] * parts + part)
        got_at = lambda i, m, d, part=part: (lax.rem(i, splits), part)
        gated, carry_gate = call(
            functools.partial(
                intra_kernel, head_width=head_width, first_head=part * part_heads, group_heads=part_heads
            ),
            "intra", (chunks,),
            [
                by_row(part_width), by_row(block), by_row(heads),
                pl.BlockSpec((heads, CHUNK), lambda i, *m: (0, i)),
                pl.BlockSpec((CHUNK, part_width), gate_at), pl.BlockSpec((CHUNK, part_width), got_at),
                fixed(1, all_heads),
            ],
            [by_row(part_width), by_row(part_width)],
            [shape_of((count, part_width), F32), shape_of((count, part_width), F32)],
            [
                pltpu.VMEM((state_width, part_width), F32), pltpu.VMEM((8, heads), F32),
                pltpu.VMEM((3 * heads, part_width), BF16), pltpu.VMEM((8, part_width), F32),
                pltpu.VMEM((CHUNK, part_width), F32), pltpu.VMEM((CHUNK, part_width), F32),
                pltpu.VMEM((CHUNK, part_width), F32),
            ],
            flops=10 * count * part_width * CHUNK, moved=14 * count * part_width,
        )(meta, docs, x_cat, bc, cum, dlt, gate_input, got_gate, skip)
        ready.append((gated, carry_gate, bc, arriving))

    divisor = HEADS // GROUPS * head_width
    gain_at = lambda part: pl.BlockSpec((1, part_width), lambda i, m: (0, m[0] * parts + part))
    hiddens = []
    for part, (gated, carry_gate, bc, arriving) in enumerate(ready[:-1]):
        hiddens.append(
            call(
                functools.partial(norm_kernel, divisor=divisor), "norm", (chunks,),
                [by_row(part_width), by_row(part_width), by_row(block), fixed(state_width, part_width), gain_at(part)],
                by_row(part_width), shape_of((count, part_width), BF16),
                flops=2 * count * part_width * state_width, moved=10 * count * part_width, prefetch=1,
            )(meta, gated, carry_gate, bc, arriving, gain)
        )

    gated, carry_gate, bc, arriving = ready[-1]
    if hiddens:
        arriving, hiddens[-1] = after(arriving, hiddens[-1])
    squares = []
    if not whole_groups:
        total = gated + jnp.dot(bc[:, state_width:], arriving, preferred_element_type=F32) * carry_gate
        mine = jnp.sum(total * total, axis=1, keepdims=True)
        squares = [mine + swapped(mine, "sub")]
    out_cols = features // tp_size
    mm_cols = min(512, out_cols)
    pair = tp_size == 2
    near_blocks = out_cols // mm_cols
    row_specs = [pl.BlockSpec((half, mm_cols), lambda i, m: (0, i))] * 2

    def product(first, blocks, body, name, operands, specs, outs, out_shapes):
        cols = blocks * mm_cols
        return call(
            body, name, (blocks,),
            specs + [pl.BlockSpec((width, mm_cols), lambda i, m: (0, first(m) + i))],
            outs + row_specs,
            out_shapes + [shape_of((half, cols), BF16), shape_of((half, cols), F32)],
            flops=2 * count * width * cols, moved=2 * width * cols, prefetch=1,
        )(meta, *operands, out_weight)

    far_first = (lambda m: (1 - m[2]) * near_blocks) if pair else (lambda m: 0)
    far_blocks = near_blocks if pair else features // mm_cols
    lead = max(far_blocks // 2, 1)
    operands = [*hiddens, gated, carry_gate, bc, arriving, gain, *squares]
    specs = [fixed(*v.shape) for v in operands]
    specs[len(hiddens) + 4] = gain_at(parts - 1)
    hidden, send, keep = product(
        far_first, lead, functools.partial(project_kernel, ready=len(hiddens), squared=len(squares), divisor=divisor),
        "project", operands, specs, [fixed(count, width)], [shape_of((count, width), BF16)],
    )
    far = []
    rest = [(lambda m: far_first(m) + lead, far_blocks - lead)] if far_blocks > lead else []
    if pair:
        rest.append((lambda m: m[2] * near_blocks, near_blocks))
    for first, blocks in rest:
        summed = (keep + swapped(send, "sub").astype(F32)).astype(BF16)
        hidden, summed = after(hidden, summed)
        far.append(swapped(summed, "tp") if pair else summed)
        send, keep = product(first, blocks, multiply, "product", [hidden], [fixed(count, width)], [], [])
    if not pair:
        far.append((keep + swapped(send, "sub").astype(F32)).astype(BF16))
        return lax.psum_scatter(jnp.concatenate(far, axis=1), "tp", scatter_dimension=1, tiled=True)
    lead_cols = far[0].shape[1]
    early = call(
        add_kernel, "add", (1,), [fixed(half, lead_cols)] * 2, fixed(half, lead_cols),
        shape_of((half, lead_cols), F32), flops=1 << 38, moved=10 * half * lead_cols, prefetch=0,
    )(keep, far[0])
    late = [keep[:, lead_cols:] + v.astype(F32) for v in far[1:]]
    return (jnp.concatenate([early, *late], axis=1) + swapped(send, "sub").astype(F32)).astype(BF16)


def solution(mesh):
    in_specs = (
        P(("groups", "ctx", "sub"), "tp"),
        P(("groups", "ctx", "sub"), "tp"),
        P(("groups", "ctx", "sub"), "tp", None, None),
        P(None, "tp"),
        P("tp"),
        P(None, "tp", None, None),
        P("tp", None, None),
        P(("groups", "ctx", "sub"), "tp"),
        P("tp"),
        P("tp"),
        P("tp"),
        P(("tp", "sub"), None),
        P("groups"),
    )
    out_specs = P(("groups", "ctx", "sub"), "tp")
    return jax.shard_map(local, mesh=mesh, in_specs=in_specs, out_specs=out_specs, check_vma=False)
```

```python
import functools

import jax
import jax.numpy as jnp
from jax import lax
from jax.experimental import pallas as pl
from jax.experimental.pallas import tpu as pltpu
from jax.sharding import PartitionSpec as P

HEADS = 128
GROUPS = 8
CHUNK = 128
EPSILON = 1e-05
LOG2E = 1.4426950408889634
CEILING = 126.0
VMEM = 20 << 20
F32 = jnp.float32
BF16 = jnp.bfloat16


def shifted(shard, axis, by):
    peers = lax.axis_size(axis)
    pairs = [(i, i + by) for i in range(peers) if 0 <= i + by < peers]
    return lax.ppermute(shard, axis, pairs)


def swapped(shard, axis):
    return lax.ppermute(shard, axis, [(i, i ^ 1) for i in range(lax.axis_size(axis))])


def after(*values):
    return lax.optimization_barrier(values)


def doc_start(positions, docs_ref):
    start = jnp.zeros_like(positions)
    total = jnp.int32(0)
    for doc in range(docs_ref.shape[0]):
        start = jnp.where(positions >= total, total, start)
        total = total + docs_ref[doc]
    return start


def rows_of(count, first):
    return first + lax.broadcasted_iota(jnp.int32, (count, 1), 0)


def split2(value):
    high = value.astype(BF16)
    return high, (value - high.astype(F32)).astype(BF16)


def split3(value):
    high = value.astype(BF16)
    rest = value - high.astype(F32)
    mid = rest.astype(BF16)
    return high, mid, (rest - mid.astype(F32)).astype(BF16)


def mm(a, b):
    return jnp.dot(a, b, preferred_element_type=F32)


def contract_lanes(a, b):
    return lax.dot_general(a, b, (((1,), (1,)), ((), ())), preferred_element_type=F32)


def silu(value):
    half = 0.5 * value
    return half + half * jnp.tanh(half)


def head_lanes(copies, heads, head_width, lanes, first_lane):
    shape = (copies * heads, lanes)
    head = lax.rem(lax.broadcasted_iota(jnp.int32, shape, 0), heads)
    lane = first_lane + lax.broadcasted_iota(jnp.int32, shape, 1)
    low = head * head_width
    return jnp.where((lane >= low) & (lane < low + head_width), 1.0, 0.0).astype(BF16)


def convolved(first, docs, pieces, store, taps):
    count = pieces[0][0].shape[0]
    rims = pieces[0][1].shape[0]
    start = doc_start(rows_of(count, first), docs) - first
    row = lax.broadcasted_iota(jnp.int32, (count, count), 0)
    col = lax.broadcasted_iota(jnp.int32, (count, count), 1)
    rim_row = lax.broadcasted_iota(jnp.int32, (rims, rims), 0)
    rim_col = lax.broadcasted_iota(jnp.int32, (rims, rims), 1) - rims
    shifts = []
    for back in range(1, taps):
        hit = (col == row - back) & (col >= start)
        rim_hit = (rim_col == rim_row - back) & (rim_col >= start[:rims])
        shifts.append((jnp.where(hit, 1.0, 0.0).astype(BF16), jnp.where(rim_hit, 1.0, 0.0).astype(BF16)))
    for index, (x, rim, w, bias) in enumerate(pieces):
        weights = w[...].astype(F32)
        if index:
            weights = jnp.concatenate([weights[:, 0, 0, :], weights[:, 0, 1, :]], axis=1)
        span = min(256, x.shape[1])
        for low in range(0, x.shape[1], span):
            at = slice(low, low + span)
            value = x[:, at]
            weight = weights[:, at]
            summed = bias[:, at] + value.astype(F32) * weight[taps - 1 : taps]
            top = jnp.zeros((rims, span), F32)
            for back in range(1, taps):
                line = weight[taps - 1 - back : taps - back]
                shift, rim_shift = shifts[back - 1]
                summed = summed + mm(shift, value) * line
                top = top + mm(rim_shift, rim[:, at]) * line
            store(index, at, slice(0, rims), silu(summed[:rims] + top).astype(BF16))
            store(index, at, slice(rims, count), silu(summed[rims:]).astype(BF16))


def decay_kernel(
    meta, docs, own_raw, got_raw, rate, cum_out, dlt_out, tail_out, kept_out, raw,
):
    half = own_raw.shape[1]
    heads, count = raw.shape
    mine = meta[0] == 0
    first = meta[1]
    own_at = pl.ds(pl.multiple_of(meta[0] * half, half), half)
    got_at = pl.ds(pl.multiple_of((1 - meta[0]) * half, half), half)
    last_start = doc_start(first + count - 1, docs)
    raw[:, own_at] = jnp.where(mine, own_raw[:heads], own_raw[heads:])
    raw[:, got_at] = jnp.where(mine, got_raw[:heads], got_raw[heads:])
    value = raw[...]
    size = jnp.maximum(value, 0.0) + jnp.log(1.0 + jnp.exp(-jnp.abs(value)))
    wide = (heads, 2 * heads)
    own_head = lax.broadcasted_iota(jnp.int32, wide, 0) + meta[0] * heads
    chosen = own_head == lax.broadcasted_iota(jnp.int32, wide, 1)
    rates = jnp.sum(jnp.where(chosen, rate[...], 0.0), axis=1, keepdims=True)
    decay = (-LOG2E * jnp.exp(rates)) * size
    row = lax.broadcasted_iota(jnp.int32, (count, count), 0)
    col = lax.broadcasted_iota(jnp.int32, (count, count), 1)
    above = jnp.where(row <= col, 1.0, 0.0).astype(BF16)
    high, mid, low = split3(decay)
    cum = mm(high, above) + (mm(mid, above) + mm(low, above))
    dlt_out[...] = cum - jnp.log2(size)
    end = cum[:, count - 1 :]
    places = first + lax.broadcasted_iota(jnp.int32, (1, count), 1)
    tail = jnp.where(places >= last_start, size * jnp.exp2(end - cum), 0.0)
    high, low = split2(tail.T)
    tail_out[:, :heads] = high
    tail_out[:, heads:] = low
    cum = cum.T
    cum_out[...] = cum
    kept = jnp.exp2(jnp.broadcast_to(cum[count - 1 :], (8, heads)))
    high, mid, low = split3(jnp.where(last_start < first, kept, 0.0))
    kept_out[:, :heads] = high
    kept_out[:, heads : 2 * heads] = mid
    kept_out[:, 2 * heads :] = low


def state_kernel(
    meta, docs, x, got_x, rim_x, late_rim_x, w, bias, s, got_s, rim_s, late_rim_s, sw, sbias, tail, kept,
    x_out, bc_out, s_out, d_out, raw_x, raw_s, *, taps, heads, head_width, first_lane,
):
    half, width = x.shape
    rims = rim_x.shape[0]
    state_width = bc_out.shape[1] // 2
    own_at = pl.ds(pl.multiple_of(rims + meta[0] * half, 16), half)
    got_at = pl.ds(pl.multiple_of(rims + (1 - meta[0]) * half, 16), half)
    for raw, own, got, rim, late in ((raw_x, x, got_x, rim_x, late_rim_x), (raw_s, s, got_s, rim_s, late_rim_s)):
        raw[:rims, :] = rim[...] + late[...]
        raw[own_at, :] = own[...]
        raw[got_at, :] = got[...]
    for index in range(2):
        low = index * half

        def store(piece, at, rows, value, low=low):
            out = bc_out if piece else x_out
            out[low + rows.start : low + rows.stop, at] = value

        pieces = []
        for raw, weight, offset in ((raw_x, w, bias), (raw_s, sw, sbias)):
            pieces.append((raw.at[low + rims : low + rims + half], raw.at[low : low + rims], weight, offset))
        convolved(meta[1] + low, docs, pieces, store, taps)
    b = bc_out[:, :state_width].T
    span = min(256, width)
    for low in range(0, width, span):
        at = slice(low, low + span)
        tails = mm(tail[...], head_lanes(2, heads, head_width, span, first_lane + low))
        weighted = (x_out[:, at].astype(F32) * tails).astype(BF16)
        s_out[:, at] = mm(b, weighted).astype(BF16)
        d_out[:, at] = mm(kept[...], head_lanes(3, heads, head_width, span, first_lane + low))[:1]


def intra_kernel(
    meta, docs, x_all, bc_all, cum_all, dlt_all, gate_own, gate_got, gain,
    a_out, f_out, state, spread, gates, kept_part,
    *, head_width, first_head, group_heads,
):
    total, width = x_all.shape
    heads = cum_all.shape[1]
    count = CHUNK
    splits = total // 2 // count
    state_width = bc_all.shape[1] // 2
    state[...] = jnp.zeros_like(state)
    spread[...] = head_lanes(3, heads, head_width, width, first_head * head_width)
    mine = jnp.where(meta[0] == 0, gain[:, :heads], gain[:, heads:])
    skip = mm(jnp.concatenate(split3(jnp.broadcast_to(mine, (8, heads))), axis=1), spread[...])[:1]
    row = lax.broadcasted_iota(jnp.int32, (count, count), 0)
    col = lax.broadcasted_iota(jnp.int32, (count, count), 1)
    low_lanes = lax.broadcasted_iota(jnp.int32, (count, 2 * head_width), 1) < head_width
    zero = jnp.zeros((count, 2 * head_width), BF16)

    def spread_over(value):
        return mm(jnp.concatenate(split2(value), axis=1), spread[: 2 * heads])

    def chunk(step, before):
        first = meta[1] + step * count
        rows = pl.ds(pl.multiple_of(step * count, count), count)
        half_rows = pl.ds(pl.multiple_of(lax.rem(step, splits) * count, count), count)
        starts = doc_start(rows_of(count, first), docs)
        last_start = doc_start(first + count - 1, docs)
        here = cum_all[rows, :]
        dlt = dlt_all[:, rows]
        x = x_all[rows, :]
        end = here[count - 1 :]
        b = bc_all[rows, :state_width]
        c = bc_all[rows, state_width:]
        scores = jnp.where((col <= row) & (col >= starts - first), contract_lanes(c, b), 0.0)
        reach = spread_over(jnp.where(starts < first, jnp.exp2(here - before), 0.0))
        into = spread_over(jnp.where(starts < meta[1], jnp.exp2(here), 0.0))
        to_end = jnp.exp2(end - dlt.T)
        tail = spread_over(jnp.where(rows_of(count, first) >= last_start, to_end, 0.0))
        kept = jnp.broadcast_to(jnp.where(last_start < first, jnp.exp2(end - before), 0.0), (8, heads))
        kept = mm(jnp.concatenate(split3(kept), axis=1), spread[...])[:1]
        is_own = step // splits == meta[0]
        gate = silu(jnp.where(is_own, gate_own[half_rows, :], gate_got[half_rows, :]).astype(F32))
        gates[...] = gate
        f_out[rows, :] = gate * into
        x_part = x.astype(F32)
        old = state[...]
        kept_part[...] = mm(c, old.astype(BF16)) * reach + x_part * skip
        state[...] = old * kept + mm(b.T, (x_part * tail).astype(BF16))
        for head in range(0, group_heads, 2):
            at = slice(head * head_width, (head + 2) * head_width)
            pair = []
            for k in (first_head + head, first_head + head + 1):
                exponent = jnp.minimum(here[:, k : k + 1] - dlt[k : k + 1, :], CEILING)
                pair.append((jnp.exp2(exponent) * scores).astype(BF16))
            value = x[:, at]
            stacked = jnp.concatenate(
                [jnp.where(low_lanes, value, zero), jnp.where(low_lanes, zero, value)], axis=0
            )
            within = mm(jnp.concatenate(pair, axis=1), stacked)
            a_out[rows, at] = (within + kept_part[:, at]) * gates[:, at]
        return end

    lax.fori_loop(0, total // count, chunk, jnp.zeros((1, heads), F32))


def normed(a, f, bc, incoming, gain, squares, divisor):
    state_width = bc.shape[1] // 2
    gated = a[...] + mm(bc[:, state_width:], incoming[...]) * f[...]
    total = jnp.sum(gated * gated, axis=1, keepdims=True) if squares is None else squares[...]
    return (gated * lax.rsqrt(total / divisor + EPSILON) * gain[...]).astype(BF16)


def norm_kernel(meta, a, f, bc, incoming, gain, hidden, *, divisor):
    hidden[...] = normed(a, f, bc, incoming, gain, None, divisor)


def project_kernel(meta, *refs, ready, squared, divisor):
    a, f, bc, incoming, gain = refs[ready : ready + 5]
    w, hidden, send, keep = refs[-4:]
    width = a.shape[1]

    @pl.when(pl.program_id(0) == 0)
    def _():
        for group, part in enumerate(refs[:ready]):
            hidden[:, group * width : (group + 1) * width] = part[...]
        squares = refs[ready + 5] if squared else None
        hidden[:, ready * width :] = normed(a, f, bc, incoming, gain, squares, divisor)

    multiply(meta, hidden, w, send, keep)


def multiply(meta, hidden, w, send, keep):
    half = send.shape[0]
    product = mm(hidden[...], w[...])
    mine = meta[0] == 0
    send[...] = jnp.where(mine, product[half:], product[:half]).astype(BF16)
    keep[...] = jnp.where(mine, product[:half], product[half:])


def sum_kernel(*refs):
    out = refs[-1]
    total = refs[0][...]
    for ref in refs[1:-1]:
        if ref.shape == out.shape:
            total = total + ref[...].astype(F32)
    out[...] = total.astype(out.dtype)


def local(
    x_input, gate_input, state_proj, mix_weight, mix_bias, state_weight, state_bias,
    step_raw, decay_log, skip_gain, norm_gain, out_weight, doc_lengths,
):
    half, channels = x_input.shape
    all_heads = step_raw.shape[1]
    groups, _, state_width = state_proj.shape[1:]
    taps = mix_weight.shape[0]
    features = out_weight.shape[1]
    head_width = channels // all_heads
    heads = all_heads // 2
    width = channels // 2
    count = 2 * half
    whole_groups = groups % 2 == 0
    parts = groups // 2 if whole_groups else groups
    part_heads = heads // parts
    part_width = part_heads * head_width
    block = 2 * state_width
    sub = lax.axis_index("sub").astype(jnp.int32)
    ctx = lax.axis_index("ctx").astype(jnp.int32)
    tp = lax.axis_index("tp").astype(jnp.int32)
    tp_size = lax.axis_size("tp")
    ctx_size = lax.axis_size("ctx")
    docs = doc_lengths.astype(jnp.int32)
    meta = jnp.stack([sub, ctx * count, tp])
    params = pltpu.CompilerParams(vmem_limit_bytes=VMEM)
    fixed = lambda *shape: pl.BlockSpec(shape, lambda i, *m: (0,) * len(shape))
    shape_of = jax.ShapeDtypeStruct

    def call(body, name, grid, in_specs, out_specs, out_shape, scratch=(), flops=0, moved=0, prefetch=2):
        kernel = pl.pallas_call(
            body,
            grid_spec=pltpu.PrefetchScalarGridSpec(
                num_scalar_prefetch=prefetch, grid=grid, in_specs=in_specs, out_specs=out_specs,
                scratch_shapes=list(scratch),
            ),
            out_shape=out_shape,
            compiler_params=params,
            cost_estimate=pl.CostEstimate(flops=0 * flops, bytes_accessed=0 * moved, transcendentals=0),
            name=name,
        )
        return lambda *operands: kernel(
            *(pltpu.with_memory_space_constraint(v, pltpu.HBM) if any(v is p for p in pinned) else v for v in operands)
        )

    s_input = state_proj.reshape(half, groups * block)
    s_bias = state_bias.reshape(1, groups * block)
    bias = mix_bias.reshape(1, channels)
    skip = skip_gain.reshape(1, all_heads)
    gain = norm_gain.reshape(1, channels)
    rate = decay_log.reshape(1, all_heads)
    pinned = [
        meta, docs, x_input, gate_input, mix_weight, bias, state_weight, s_bias, skip, gain, rate, out_weight
    ]
    rims = 16
    s_width = parts * block
    s_half = (lambda v, core: lax.dynamic_slice_in_dim(v, core * s_width, s_width, 1)) if whole_groups else (
        lambda v, core: v
    )
    last_x, last_s = x_input[half - rims :], s_input[half - rims :]
    flat = 2 * ctx_size

    def rim_for(core):
        shard = jnp.concatenate([last_x[:, core * width : (core + 1) * width], s_half(last_s, core)], axis=1)
        return lax.ppermute(shard, ("ctx", "sub"), [(i, i + 1 + core) for i in range(1, flat - 2, 2)])

    rim, late_rim = rim_for(0), rim_for(1)
    raw = step_raw.T
    got_raw = swapped(raw, "sub")
    got_x = swapped(lax.dynamic_slice_in_dim(x_input, (1 - sub) * width, width, 1), "sub")
    got_s = swapped(s_half(s_input, 1 - sub), "sub")
    got_gate = swapped(lax.dynamic_slice_in_dim(gate_input, (1 - sub) * width, width, 1), "sub")
    got_gate, got_raw = after(got_gate, got_raw)
    mixed = (x_input, got_x, rim, late_rim, mix_weight, bias, s_input, got_s, rim, late_rim, state_weight, s_bias)

    def mix_specs(part):
        at = lambda m: m[0] * parts + part
        s_at = at if whole_groups else (lambda m: 0)
        here = lambda m: part
        rim_at = lambda m: width // block + part
        specs = []
        for size, places in ((part_width, (at, here, here, here, at, at)), (block, (s_at, here, rim_at, rim_at, s_at, s_at))):
            for rows, place in zip((half, half, rims, rims, taps, 1), places):
                specs.append(pl.BlockSpec((rows, size), lambda i, m, d, place=place: (0, place(m))))
        specs[10] = pl.BlockSpec((taps, 1, 2, state_width), lambda i, m, d: (0, s_at(m), 0, 0))
        return specs

    cum, dlt, tail, kept = call(
        decay_kernel, "decay", (1,),
        [fixed(all_heads, half), fixed(all_heads, half), fixed(1, all_heads)],
        [fixed(count, heads), fixed(heads, count), fixed(count, 2 * heads), fixed(8, 3 * heads)],
        [
            shape_of((count, heads), F32), shape_of((heads, count), F32),
            shape_of((count, 2 * heads), BF16), shape_of((8, 3 * heads), BF16),
        ],
        [pltpu.VMEM((heads, count), F32)], flops=2 * count * count * 128, moved=16 * count * heads,
    )(meta, docs, raw, got_raw, rate)

    def onward(shard):
        return lax.ppermute(shard, "ctx", [(i, (i + 1) % ctx_size) for i in range(ctx_size)])

    made = []
    next_meta = meta
    for part in range(parts):
        x_cat, bc, state, decay = call(
            functools.partial(
                state_kernel, taps=taps, heads=heads, head_width=head_width, first_lane=part * part_width
            ),
            "state", (1,),
            mix_specs(part) + [fixed(count, 2 * heads), fixed(8, 3 * heads)],
            [
                fixed(count, part_width), fixed(count, block), fixed(state_width, part_width), fixed(1, part_width),
            ],
            [
                shape_of((count, part_width), BF16), shape_of((count, block), BF16),
                shape_of((state_width, part_width), BF16), shape_of((1, part_width), F32),
            ],
            [pltpu.VMEM((rims + count, part_width), BF16), pltpu.VMEM((rims + count, block), BF16)],
            flops=4 * half * count * part_width, moved=6 * count * part_width,
        )(next_meta, docs, *mixed, tail, kept)
        state, next_meta = after(state, next_meta)
        pinned.append(next_meta)
        made.append([x_cat, bc, state, decay, onward(state)])
        if part:
            made[part - 1][4], made[part][0] = after(made[part - 1][4], x_cat)
    ready = []
    for part in range(parts):
        x_cat, bc, state, decay, arriving = made[part]
        if ready:
            arriving, gate = after(arriving, ready[-1][0])
            ready[-1] = (gate, *ready[-1][1:])
        for _ in range(ctx_size // 2 - 1):
            leaving = (state.astype(F32) + decay * arriving.astype(F32)).astype(BF16)
            leaving, x_cat = after(leaving, x_cat)
            arriving = onward(leaving)
        gated, carry_gate = call(
            functools.partial(
                intra_kernel, head_width=head_width, first_head=part * part_heads, group_heads=part_heads
            ),
            "intra", (1,),
            [
                fixed(count, part_width), fixed(count, block), fixed(count, heads), fixed(heads, count),
                pl.BlockSpec((half, part_width), lambda i, m, d, part=part: (0, m[0] * parts + part)),
                pl.BlockSpec((half, part_width), lambda i, m, d, part=part: (0, part)),
                fixed(1, all_heads),
            ],
            [fixed(count, part_width), fixed(count, part_width)],
            [shape_of((count, part_width), F32), shape_of((count, part_width), F32)],
            [
                pltpu.VMEM((state_width, part_width), F32), pltpu.VMEM((3 * heads, part_width), BF16),
                pltpu.VMEM((CHUNK, part_width), F32), pltpu.VMEM((CHUNK, part_width), F32),
            ],
            flops=10 * count * part_width * CHUNK, moved=14 * count * part_width,
        )(meta, docs, x_cat, bc, cum, dlt, gate_input, got_gate, skip)
        ready.append((gated, carry_gate, bc, arriving))

    divisor = HEADS // GROUPS * head_width
    gain_at = lambda part: pl.BlockSpec((1, part_width), lambda i, m: (0, m[0] * parts + part))
    hiddens = []
    for part, (gated, carry_gate, bc, arriving) in enumerate(ready[:-1]):
        hiddens.append(
            call(
                functools.partial(norm_kernel, divisor=divisor), "norm", (1,),
                [
                    fixed(count, part_width), fixed(count, part_width), fixed(count, block),
                    fixed(state_width, part_width), gain_at(part),
                ],
                fixed(count, part_width), shape_of((count, part_width), BF16),
                flops=2 * count * part_width * state_width, moved=10 * count * part_width, prefetch=1,
            )(meta, gated, carry_gate, bc, arriving, gain)
        )

    gated, carry_gate, bc, arriving = ready[-1]
    if hiddens:
        arriving, hiddens[-1] = after(arriving, hiddens[-1])
    squares = []
    if not whole_groups:
        total = gated + jnp.dot(bc[:, state_width:], arriving, preferred_element_type=F32) * carry_gate
        mine = jnp.sum(total * total, axis=1, keepdims=True)
        squares = [mine + swapped(mine, "sub")]
    out_cols = features // tp_size
    mm_cols = min(512, out_cols)
    pair = tp_size == 2
    near_blocks = out_cols // mm_cols
    row_specs = [pl.BlockSpec((half, mm_cols), lambda i, m: (0, i))] * 2

    def product(first, blocks, body, name, operands, specs, outs, out_shapes, declared=1):
        cols = blocks * mm_cols
        return call(
            body, name, (blocks,),
            specs + [pl.BlockSpec((width, mm_cols), lambda i, m: (0, first(m, i)))],
            outs + row_specs,
            out_shapes + [shape_of((half, cols), BF16), shape_of((half, cols), F32)],
            flops=declared * 2 * count * width * cols, moved=declared * 2 * width * cols, prefetch=1,
        )(meta, *operands, out_weight)

    operands = [*hiddens, gated, carry_gate, bc, arriving, gain, *squares]
    specs = [fixed(*v.shape) for v in operands]
    specs[len(hiddens) + 4] = gain_at(parts - 1)
    project = functools.partial(project_kernel, ready=len(hiddens), squared=len(squares), divisor=divisor)
    hidden_spec, hidden_shape = fixed(count, width), shape_of((count, width), BF16)
    if not pair:
        every = features // mm_cols
        _, send, keep = product(lambda m, i: i, every, project, "project", operands, specs, [hidden_spec], [hidden_shape])
        summed = (keep + swapped(send, "sub").astype(F32)).astype(BF16)
        return lax.psum_scatter(summed, "tp", scatter_dimension=1, tiled=True)
    lead = max(3 * near_blocks // 4, 1)
    far_first = lambda m: (1 - m[2]) * near_blocks
    hidden, send, keep = product(
        lambda m, i: far_first(m) + i, lead, project, "project", operands, specs, [hidden_spec], [hidden_shape]
    )
    summed = (keep + swapped(send, "sub").astype(F32)).astype(BF16)
    hidden, summed = after(hidden, summed)
    far_lead = swapped(summed, "tp")
    rest = near_blocks - lead
    send, keep = product(
        lambda m, i: far_first(m) + lead + i, rest, multiply, "product", [hidden], [hidden_spec], [], []
    )
    summed = (keep + swapped(send, "sub").astype(F32)).astype(BF16)
    hidden, summed = after(hidden, summed)
    far_rest = swapped(summed, "tp")
    send, keep = product(
        lambda m, i: m[2] * near_blocks + i, near_blocks, multiply, "product", [hidden], [hidden_spec], [], [],
        declared=0,
    )
    got = swapped(send, "sub")

    def finish(first, terms, name, dtype, old=(), weight=0):
        blocks = min(v.shape[1] for v in terms) // mm_cols
        at = lambda v: (lambda i: (0, i + (first if v.shape[1] == out_cols else 0)))
        cols = out_cols if dtype == BF16 else blocks * mm_cols
        return pl.pallas_call(
            sum_kernel, grid=(blocks,),
            in_specs=[pl.BlockSpec((half, mm_cols), at(v)) for v in terms]
            + [pl.BlockSpec(memory_space=pl.ANY)] * len(old),
            out_specs=pl.BlockSpec((half, mm_cols), lambda i: (0, i + (first if dtype == BF16 else 0))),
            out_shape=shape_of((half, cols), dtype),
            input_output_aliases={len(terms): 0} if old else {},
            compiler_params=params,
            cost_estimate=pl.CostEstimate(flops=weight, bytes_accessed=0, transcendentals=0),
            name=name,
        )(*terms, *old)

    early = finish(0, [keep, far_lead], "early", F32, weight=1 << 38)
    output = finish(0, [early, got], "lead", BF16)
    return finish(lead, [keep, got, far_rest], "rest", BF16, old=(output,))


def solution(mesh):
    in_specs = (
        P(("groups", "ctx", "sub"), "tp"),
        P(("groups", "ctx", "sub"), "tp"),
        P(("groups", "ctx", "sub"), "tp", None, None),
        P(None, "tp"),
        P("tp"),
        P(None, "tp", None, None),
        P("tp", None, None),
        P(("groups", "ctx", "sub"), "tp"),
        P("tp"),
        P("tp"),
        P("tp"),
        P(("tp", "sub"), None),
        P("groups"),
    )
    out_specs = P(("groups", "ctx", "sub"), "tp")
    return jax.shard_map(local, mesh=mesh, in_specs=in_specs, out_specs=out_specs, check_vma=False)
```

```python
import functools

import jax
import jax.numpy as jnp
from jax import lax
from jax.experimental import pallas as pl
from jax.experimental.pallas import tpu as pltpu
from jax.sharding import PartitionSpec as P

HEADS = 128
GROUPS = 8
CHUNK = 128
EPSILON = 1e-05
LOG2E = 1.4426950408889634
CEILING = 126.0
VMEM = 20 << 20
F32 = jnp.float32
BF16 = jnp.bfloat16


def shifted_ring(shard, axis):
    peers = lax.axis_size(axis)
    return lax.ppermute(shard, axis, [(i, (i + 1) % peers) for i in range(peers)])


def swapped(shard, axis):
    return lax.ppermute(shard, axis, [(i, i ^ 1) for i in range(lax.axis_size(axis))])


def after(*values):
    return lax.optimization_barrier(values)


def doc_start(positions, docs_ref):
    start = jnp.zeros_like(positions)
    total = jnp.int32(0)
    for doc in range(docs_ref.shape[0]):
        start = jnp.where(positions >= total, total, start)
        total = total + docs_ref[doc]
    return start


def rows_of(count, first):
    return first + lax.broadcasted_iota(jnp.int32, (count, 1), 0)


def split2(value):
    high = value.astype(BF16)
    return high, (value - high.astype(F32)).astype(BF16)


def split3(value):
    high = value.astype(BF16)
    rest = value - high.astype(F32)
    mid = rest.astype(BF16)
    return high, mid, (rest - mid.astype(F32)).astype(BF16)


def mm(a, b):
    return jnp.dot(a, b, preferred_element_type=F32)


def contract_lanes(a, b):
    return lax.dot_general(a, b, (((1,), (1,)), ((), ())), preferred_element_type=F32)


def silu(value):
    half = 0.5 * value
    return half + half * jnp.tanh(half)


def head_lanes(copies, heads, head_width, lanes, first_lane):
    shape = (copies * heads, lanes)
    head = lax.rem(lax.broadcasted_iota(jnp.int32, shape, 0), heads)
    lane = first_lane + lax.broadcasted_iota(jnp.int32, shape, 1)
    low = head * head_width
    return jnp.where((lane >= low) & (lane < low + head_width), 1.0, 0.0).astype(BF16)


def convolved(shifts, x, rim, w, bias, store, taps):
    count = x.shape[0]
    rims = rim.shape[0]
    weights = w[...].astype(F32)
    if len(weights.shape) == 4:
        weights = jnp.concatenate([weights[:, 0, 0, :], weights[:, 0, 1, :]], axis=1)
    span = min(256, x.shape[1])
    for low in range(0, x.shape[1], span):
        at = slice(low, low + span)
        value = x[:, at]
        weight = weights[:, at]
        summed = bias[:, at] + value.astype(F32) * weight[taps - 1 : taps]
        top = jnp.zeros((rims, span), F32)
        for back in range(1, taps):
            line = weight[taps - 1 - back : taps - back]
            shift, rim_shift = shifts[back - 1]
            summed = summed + mm(shift[...], value) * line
            top = top + mm(rim_shift[...], rim[:, at]) * line
        store(at, slice(0, rims), silu(summed[:rims] + top).astype(BF16))
        store(at, slice(rims, count), silu(summed[rims:]).astype(BF16))


def decay_kernel(
    meta, docs, own_raw, got_raw, rate, cum_out, dlt_out, tail_out, kept_out, raw,
):
    half = own_raw.shape[1]
    heads, count = raw.shape
    mine = meta[0] == 0
    first = meta[1]
    own_at = pl.ds(pl.multiple_of(meta[0] * half, half), half)
    got_at = pl.ds(pl.multiple_of((1 - meta[0]) * half, half), half)
    last_start = doc_start(first + count - 1, docs)
    raw[:, own_at] = jnp.where(mine, own_raw[:heads], own_raw[heads:])
    raw[:, got_at] = jnp.where(mine, got_raw[:heads], got_raw[heads:])
    value = raw[...]
    size = jnp.maximum(value, 0.0) + jnp.log(1.0 + jnp.exp(-jnp.abs(value)))
    wide = (heads, 2 * heads)
    own_head = lax.broadcasted_iota(jnp.int32, wide, 0) + meta[0] * heads
    chosen = own_head == lax.broadcasted_iota(jnp.int32, wide, 1)
    rates = jnp.sum(jnp.where(chosen, rate[...], 0.0), axis=1, keepdims=True)
    decay = (-LOG2E * jnp.exp(rates)) * size
    row = lax.broadcasted_iota(jnp.int32, (count, count), 0)
    col = lax.broadcasted_iota(jnp.int32, (count, count), 1)
    above = jnp.where(row <= col, 1.0, 0.0).astype(BF16)
    high, mid, low = split3(decay)
    cum = mm(high, above) + (mm(mid, above) + mm(low, above))
    dlt_out[...] = cum - jnp.log2(size)
    end = cum[:, count - 1 :]
    places = first + lax.broadcasted_iota(jnp.int32, (1, count), 1)
    tail = jnp.where(places >= last_start, size * jnp.exp2(end - cum), 0.0)
    high, low = split2(tail.T)
    tail_out[:, :heads] = high
    tail_out[:, heads:] = low
    cum = cum.T
    cum_out[...] = cum
    kept = jnp.exp2(jnp.broadcast_to(cum[count - 1 :], (8, heads)))
    high, mid, low = split3(jnp.where(last_start < first, kept, 0.0))
    kept_out[:, :heads] = high
    kept_out[:, heads : 2 * heads] = mid
    kept_out[:, 2 * heads :] = low


def state_kernel(
    meta, docs, x, got_x, rim_x, late_rim_x, w, bias, s, got_s, rim_s, late_rim_s, sw, sbias, tail, kept,
    x_out, bc_out, s_out, d_out, raw_x, raw_s, shift, rim_shift, b_turned,
    *, taps, heads, head_width, first_lane,
):
    step = pl.program_id(0)
    half, width = x.shape
    rims = rim_x.shape[0]
    state_width = bc_out.shape[1] // 2

    def mixed(raw, own, got, rim, late, weight, offset, out):
        raw[:rims, :] = jnp.where(meta[0] == 0, rim[...], late[...])
        raw[pl.ds(pl.multiple_of(rims + meta[0] * half, 16), half), :] = own[...]
        raw[pl.ds(pl.multiple_of(rims + (1 - meta[0]) * half, 16), half), :] = got[...]
        for index in range(2):
            low = index * half

            def store(at, rows, value, low=low):
                out[low + rows.start : low + rows.stop, at] = value

            shifts = [(shift.at[index, back], rim_shift.at[index, back]) for back in range(taps - 1)]
            convolved(
                shifts, raw.at[low + rims : low + rims + half], raw.at[low : low + rims], weight, offset, store, taps
            )

    @pl.when(step == 0)
    def _():
        row = lax.broadcasted_iota(jnp.int32, (half, half), 0)
        col = lax.broadcasted_iota(jnp.int32, (half, half), 1)
        rim_row = lax.broadcasted_iota(jnp.int32, (rims, rims), 0)
        rim_col = lax.broadcasted_iota(jnp.int32, (rims, rims), 1) - rims
        for index in range(2):
            first = meta[1] + index * half
            start = doc_start(rows_of(half, first), docs) - first
            for back in range(1, taps):
                hit = (col == row - back) & (col >= start)
                rim_hit = (rim_col == rim_row - back) & (rim_col >= start[:rims])
                shift[index, back - 1] = jnp.where(hit, 1.0, 0.0).astype(BF16)
                rim_shift[index, back - 1] = jnp.where(rim_hit, 1.0, 0.0).astype(BF16)
        mixed(raw_s, s, got_s, rim_s, late_rim_s, sw, sbias, bc_out)
        b_turned[...] = bc_out[:, :state_width].T

    mixed(raw_x, x, got_x, rim_x, late_rim_x, w, bias, x_out)
    lanes = first_lane + step * width
    tails = mm(tail[...], head_lanes(2, heads, head_width, width, lanes))
    weighted = (x_out[...].astype(F32) * tails).astype(BF16)
    s_out[...] = mm(b_turned[...], weighted).astype(BF16)
    d_out[...] = mm(kept[...], head_lanes(3, heads, head_width, width, lanes))[:1]


def intra_kernel(
    meta, docs, x_all, bc_all, cum_all, dlt_all, gate_own, gate_got, gain,
    a_out, f_out, state, spread, gates, kept_part,
    *, head_width, first_head, group_heads,
):
    total, width = x_all.shape
    heads = cum_all.shape[1]
    count = CHUNK
    splits = total // 2 // count
    state_width = bc_all.shape[1] // 2
    state[...] = jnp.zeros_like(state)
    spread[...] = head_lanes(3, heads, head_width, width, first_head * head_width)
    mine = jnp.where(meta[0] == 0, gain[:, :heads], gain[:, heads:])
    skip = mm(jnp.concatenate(split3(jnp.broadcast_to(mine, (8, heads))), axis=1), spread[...])[:1]
    row = lax.broadcasted_iota(jnp.int32, (count, count), 0)
    col = lax.broadcasted_iota(jnp.int32, (count, count), 1)
    low_lanes = lax.broadcasted_iota(jnp.int32, (count, 2 * head_width), 1) < head_width
    zero = jnp.zeros((count, 2 * head_width), BF16)

    def spread_over(value):
        return mm(jnp.concatenate(split2(value), axis=1), spread[: 2 * heads])

    def chunk(step, before):
        first = meta[1] + step * count
        rows = pl.ds(pl.multiple_of(step * count, count), count)
        half_rows = pl.ds(pl.multiple_of(lax.rem(step, splits) * count, count), count)
        starts = doc_start(rows_of(count, first), docs)
        last_start = doc_start(first + count - 1, docs)
        here = cum_all[rows, :]
        dlt = dlt_all[:, rows]
        x = x_all[rows, :]
        end = here[count - 1 :]
        b = bc_all[rows, :state_width]
        c = bc_all[rows, state_width:]
        scores = jnp.where((col <= row) & (col >= starts - first), contract_lanes(c, b), 0.0)
        reach = spread_over(jnp.where(starts < first, jnp.exp2(here - before), 0.0))
        into = spread_over(jnp.where(starts < meta[1], jnp.exp2(here), 0.0))
        to_end = jnp.exp2(end - dlt.T)
        tail = spread_over(jnp.where(rows_of(count, first) >= last_start, to_end, 0.0))
        kept = jnp.broadcast_to(jnp.where(last_start < first, jnp.exp2(end - before), 0.0), (8, heads))
        kept = mm(jnp.concatenate(split3(kept), axis=1), spread[...])[:1]
        is_own = step // splits == meta[0]
        gate = silu(jnp.where(is_own, gate_own[half_rows, :], gate_got[half_rows, :]).astype(F32))
        gates[...] = gate
        f_out[rows, :] = gate * into
        x_part = x.astype(F32)
        old = state[...]
        kept_part[...] = mm(c, old.astype(BF16)) * reach + x_part * skip
        state[...] = old * kept + mm(b.T, (x_part * tail).astype(BF16))
        for head in range(0, group_heads, 2):
            at = slice(head * head_width, (head + 2) * head_width)
            pair = []
            for k in (first_head + head, first_head + head + 1):
                exponent = jnp.minimum(here[:, k : k + 1] - dlt[k : k + 1, :], CEILING)
                pair.append((jnp.exp2(exponent) * scores).astype(BF16))
            value = x[:, at]
            stacked = jnp.concatenate(
                [jnp.where(low_lanes, value, zero), jnp.where(low_lanes, zero, value)], axis=0
            )
            within = mm(jnp.concatenate(pair, axis=1), stacked)
            a_out[rows, at] = (within + kept_part[:, at]) * gates[:, at]
        return end

    lax.fori_loop(0, total // count, chunk, jnp.zeros((1, heads), F32))


def normed(a, f, bc, incoming, gain, squares, divisor):
    state_width = bc.shape[1] // 2
    gated = a[...] + mm(bc[:, state_width:], incoming[...]) * f[...]
    total = jnp.sum(gated * gated, axis=1, keepdims=True) if squares is None else squares[...]
    return (gated * lax.rsqrt(total / divisor + EPSILON) * gain[...]).astype(BF16)


def norm_kernel(meta, a, f, bc, incoming, gain, hidden, *, divisor):
    hidden[...] = normed(a, f, bc, incoming, gain, None, divisor)


def project_kernel(meta, *refs, ready, squared, divisor):
    a, f, bc, incoming, gain = refs[ready : ready + 5]
    w, hidden, send, keep = refs[-4:]
    width = a.shape[1]

    @pl.when(pl.program_id(0) == 0)
    def _():
        for group, part in enumerate(refs[:ready]):
            hidden[:, group * width : (group + 1) * width] = part[...]
        squares = refs[ready + 5] if squared else None
        hidden[:, ready * width :] = normed(a, f, bc, incoming, gain, squares, divisor)

    multiply(meta, hidden, w, send, keep)


def multiply(meta, hidden, w, send, keep):
    half = send.shape[0]
    product = mm(hidden[...], w[...])
    mine = meta[0] == 0
    send[...] = jnp.where(mine, product[half:], product[:half]).astype(BF16)
    keep[...] = jnp.where(mine, product[:half], product[half:])


def sum_kernel(*refs):
    out = refs[-1]
    total = refs[0][...]
    for ref in refs[1:-1]:
        if ref.shape == out.shape:
            total = total + ref[...].astype(F32)
    out[...] = total.astype(out.dtype)


def local(
    x_input, gate_input, state_proj, mix_weight, mix_bias, state_weight, state_bias,
    step_raw, decay_log, skip_gain, norm_gain, out_weight, doc_lengths,
):
    half, channels = x_input.shape
    all_heads = step_raw.shape[1]
    groups, _, state_width = state_proj.shape[1:]
    taps = mix_weight.shape[0]
    features = out_weight.shape[1]
    head_width = channels // all_heads
    heads = all_heads // 2
    width = channels // 2
    count = 2 * half
    whole_groups = groups % 2 == 0
    parts = groups // 2 if whole_groups else groups
    part_heads = heads // parts
    part_width = part_heads * head_width
    block = 2 * state_width
    sub = lax.axis_index("sub").astype(jnp.int32)
    ctx = lax.axis_index("ctx").astype(jnp.int32)
    tp = lax.axis_index("tp").astype(jnp.int32)
    tp_size = lax.axis_size("tp")
    ctx_size = lax.axis_size("ctx")
    docs = doc_lengths.astype(jnp.int32)
    meta = jnp.stack([sub, ctx * count, tp])
    params = pltpu.CompilerParams(vmem_limit_bytes=VMEM)
    fixed = lambda *shape: pl.BlockSpec(shape, lambda i, *m: (0,) * len(shape))
    shape_of = jax.ShapeDtypeStruct

    def call(body, name, grid, in_specs, out_specs, out_shape, scratch=(), prefetch=2):
        kernel = pl.pallas_call(
            body,
            grid_spec=pltpu.PrefetchScalarGridSpec(
                num_scalar_prefetch=prefetch, grid=grid, in_specs=in_specs, out_specs=out_specs,
                scratch_shapes=list(scratch),
            ),
            out_shape=out_shape,
            compiler_params=params,
            cost_estimate=pl.CostEstimate(flops=0, bytes_accessed=0, transcendentals=0),
            name=name,
        )
        return lambda *operands: kernel(
            *(pltpu.with_memory_space_constraint(v, pltpu.HBM) if any(v is p for p in pinned) else v for v in operands)
        )

    s_input = state_proj.reshape(half, groups * block)
    s_bias = state_bias.reshape(1, groups * block)
    bias = mix_bias.reshape(1, channels)
    skip = skip_gain.reshape(1, all_heads)
    gain = norm_gain.reshape(1, channels)
    rate = decay_log.reshape(1, all_heads)
    pinned = [
        meta, docs, x_input, gate_input, mix_weight, bias, state_weight, s_bias, skip, gain, rate, out_weight
    ]
    rims = 16
    cut_width = min(1024, part_width)
    cuts = part_width // cut_width
    s_width = parts * block if whole_groups else groups * block
    raw = step_raw.T
    got_raw, x_later, gate_later = after(swapped(raw, "sub"), x_input, gate_input)
    got_x = swapped(x_later, "sub")
    got_s = swapped(s_input, "sub")
    last_x, last_s = x_input[half - rims :], state_proj[half - rims :].reshape(rims, groups * block)
    rim = shifted_ring(jnp.concatenate([last_x[:, :width], last_s[:, :s_width]], axis=1), ("ctx", "sub"))
    late_rim = shifted_ring(jnp.concatenate([last_x[:, width:], last_s[:, -s_width:]], axis=1), "ctx")
    got_gate = swapped(gate_later, "sub")
    mixed = (x_input, got_x, rim, late_rim, mix_weight, bias, s_input, got_s, rim, late_rim, state_weight, s_bias)

    def mix_specs(part):
        at = lambda m: m[0] * parts + part
        s_at = at if whole_groups else (lambda m: 0)
        here = lambda m: part
        rim_at = lambda m: width // block + part
        specs = []
        x_at = lambda m, i: at(m) * cuts + i
        x_here = lambda m, i: here(m) * cuts + i
        specs = []
        for rows, place in zip((half, half, rims, rims, taps, 1), (x_at, x_at, x_here, x_here, x_at, x_at)):
            specs.append(pl.BlockSpec((rows, cut_width), lambda i, m, d, place=place: (0, place(m, i))))
        for rows, place in zip((half, half, rims, rims, taps, 1), (s_at, s_at, rim_at, rim_at, s_at, s_at)):
            specs.append(pl.BlockSpec((rows, block), lambda i, m, d, place=place: (0, place(m))))
        specs[10] = pl.BlockSpec((taps, 1, 2, state_width), lambda i, m, d: (0, s_at(m), 0, 0))
        return specs

    cum, dlt, tail, kept = call(
        decay_kernel, "decay", (1,),
        [fixed(all_heads, half), fixed(all_heads, half), fixed(1, all_heads)],
        [fixed(count, heads), fixed(heads, count), fixed(count, 2 * heads), fixed(8, 3 * heads)],
        [
            shape_of((count, heads), F32), shape_of((heads, count), F32),
            shape_of((count, 2 * heads), BF16), shape_of((8, 3 * heads), BF16),
        ],
        [pltpu.VMEM((heads, count), F32)],
    )(meta, docs, raw, got_raw, rate)

    made = []
    next_meta = meta
    for part in range(parts):
        x_cat, bc, state, decay = call(
            functools.partial(
                state_kernel, taps=taps, heads=heads, head_width=head_width, first_lane=part * part_width
            ),
            "state", (cuts,),
            mix_specs(part) + [fixed(count, 2 * heads), fixed(8, 3 * heads)],
            [
                pl.BlockSpec((count, cut_width), lambda i, m, d: (0, i)), fixed(count, block),
                pl.BlockSpec((state_width, cut_width), lambda i, m, d: (0, i)),
                pl.BlockSpec((1, cut_width), lambda i, m, d: (0, i)),
            ],
            [
                shape_of((count, part_width), BF16), shape_of((count, block), BF16),
                shape_of((state_width, part_width), BF16), shape_of((1, part_width), F32),
            ],
            [
                pltpu.VMEM((rims + count, cut_width), BF16), pltpu.VMEM((rims + count, block), BF16),
                pltpu.VMEM((2, taps - 1, half, half), BF16), pltpu.VMEM((2, taps - 1, rims, rims), BF16),
                pltpu.VMEM((state_width, count), BF16),
            ],
        )(next_meta, docs, *mixed, tail, kept)
        state, next_meta = after(state, next_meta)
        pinned.append(next_meta)
        made.append([x_cat, bc, state, decay, shifted_ring(state, "ctx")])
        if part:
            made[part - 1][4], made[part][0] = after(made[part - 1][4], x_cat)
    ready = []
    for part in range(parts):
        x_cat, bc, state, decay, arriving = made[part]
        if ready:
            arriving, gate = after(arriving, ready[-1][0])
            ready[-1] = (gate, *ready[-1][1:])
        for _ in range(ctx_size // 2 - 1):
            leaving = (state.astype(F32) + decay * arriving.astype(F32)).astype(BF16)
            leaving, x_cat = after(leaving, x_cat)
            arriving = shifted_ring(leaving, "ctx")
        gated, carry_gate = call(
            functools.partial(
                intra_kernel, head_width=head_width, first_head=part * part_heads, group_heads=part_heads
            ),
            "intra", (1,),
            [
                fixed(count, part_width), fixed(count, block), fixed(count, heads), fixed(heads, count),
                pl.BlockSpec((half, part_width), lambda i, m, d, part=part: (0, m[0] * parts + part)),
                pl.BlockSpec((half, part_width), lambda i, m, d, part=part: (0, m[0] * parts + part)),
                fixed(1, all_heads),
            ],
            [fixed(count, part_width), fixed(count, part_width)],
            [shape_of((count, part_width), F32)] * 2,
            [
                pltpu.VMEM((state_width, part_width), F32), pltpu.VMEM((3 * heads, part_width), BF16),
                pltpu.VMEM((CHUNK, part_width), F32), pltpu.VMEM((CHUNK, part_width), F32),
            ],
        )(meta, docs, x_cat, bc, cum, dlt, gate_input, got_gate, skip)
        ready.append((gated, carry_gate, bc, arriving))

    divisor = HEADS // GROUPS * head_width
    gain_at = lambda part: pl.BlockSpec((1, part_width), lambda i, m: (0, m[0] * parts + part))
    hiddens = []
    for part, (gated, carry_gate, bc, arriving) in enumerate(ready[:-1]):
        hiddens.append(
            call(
                functools.partial(norm_kernel, divisor=divisor), "norm", (1,),
                [
                    fixed(count, part_width), fixed(count, part_width), fixed(count, block),
                    fixed(state_width, part_width), gain_at(part),
                ],
                fixed(count, part_width), shape_of((count, part_width), BF16),
                prefetch=1,
            )(meta, gated, carry_gate, bc, arriving, gain)
        )

    gated, carry_gate, bc, arriving = ready[-1]
    if hiddens:
        arriving, hiddens[-1] = after(arriving, hiddens[-1])
    squares = []
    if not whole_groups:
        total = gated + jnp.dot(bc[:, state_width:], arriving, preferred_element_type=F32) * carry_gate
        mine = jnp.sum(total * total, axis=1, keepdims=True)
        squares = [mine + swapped(mine, "sub")]
    out_cols = features // tp_size
    mm_cols = min(512, out_cols)
    pair = tp_size == 2
    near_blocks = out_cols // mm_cols
    row_specs = [pl.BlockSpec((half, mm_cols), lambda i, m: (0, i))] * 2

    def product(first, blocks, body, name, operands, specs, outs, out_shapes):
        cols = blocks * mm_cols
        return call(
            body, name, (blocks,),
            specs + [pl.BlockSpec((width, mm_cols), lambda i, m: (0, first(m, i)))],
            outs + row_specs,
            out_shapes + [shape_of((half, cols), BF16), shape_of((half, cols), F32)],
            prefetch=1,
        )(meta, *operands, out_weight)

    operands = [*hiddens, gated, carry_gate, bc, arriving, gain, *squares]
    specs = [fixed(*v.shape) for v in operands]
    specs[len(hiddens) + 4] = gain_at(parts - 1)
    project = functools.partial(project_kernel, ready=len(hiddens), squared=len(squares), divisor=divisor)
    hidden_spec, hidden_shape = fixed(count, width), shape_of((count, width), BF16)
    if not pair:
        every = features // mm_cols
        _, send, keep = product(lambda m, i: i, every, project, "project", operands, specs, [hidden_spec], [hidden_shape])
        summed = (keep + swapped(send, "sub").astype(F32)).astype(BF16)
        return lax.psum_scatter(summed, "tp", scatter_dimension=1, tiled=True)
    lead = max(3 * near_blocks // 4, 1)
    far_first = lambda m: (1 - m[2]) * near_blocks
    hidden, send, keep = product(
        lambda m, i: far_first(m) + i, lead, project, "project", operands, specs, [hidden_spec], [hidden_shape]
    )
    summed = (keep + swapped(send, "sub").astype(F32)).astype(BF16)
    hidden, summed = after(hidden, summed)
    far_lead = swapped(summed, "tp")
    rest = near_blocks - lead
    send, keep = product(
        lambda m, i: far_first(m) + lead + i, rest, multiply, "product", [hidden], [hidden_spec], [], []
    )
    summed = (keep + swapped(send, "sub").astype(F32)).astype(BF16)
    hidden, summed = after(hidden, summed)
    far_rest = swapped(summed, "tp")
    send, keep = product(
        lambda m, i: m[2] * near_blocks + i, near_blocks, multiply, "product", [hidden], [hidden_spec], [], [],
    )
    got = swapped(send, "sub")

    def finish(first, terms, name, dtype, old=(), weight=0):
        blocks = min(v.shape[1] for v in terms) // mm_cols
        at = lambda v: (lambda i: (0, i + (first if v.shape[1] == out_cols else 0)))
        cols = out_cols if dtype == BF16 else blocks * mm_cols
        return pl.pallas_call(
            sum_kernel, grid=(blocks,),
            in_specs=[pl.BlockSpec((half, mm_cols), at(v)) for v in terms]
            + [pl.BlockSpec(memory_space=pl.ANY)] * len(old),
            out_specs=pl.BlockSpec((half, mm_cols), lambda i: (0, i + (first if dtype == BF16 else 0))),
            out_shape=shape_of((half, cols), dtype),
            input_output_aliases={len(terms): 0} if old else {},
            compiler_params=params,
            cost_estimate=pl.CostEstimate(flops=weight, bytes_accessed=0, transcendentals=0),
            name=name,
        )(*terms, *old)

    early = finish(0, [keep, far_lead], "early", F32, weight=1 << 38)
    output = finish(0, [early, got], "lead", BF16)
    cut = lead * mm_cols
    last = (keep[:, cut:] + got[:, cut:].astype(F32) + far_rest.astype(F32)).astype(BF16)
    return lax.dynamic_update_slice(output, last, (0, cut))


def solution(mesh):
    in_specs = (
        P(("groups", "ctx", "sub"), "tp"),
        P(("groups", "ctx", "sub"), "tp"),
        P(("groups", "ctx", "sub"), "tp", None, None),
        P(None, "tp"),
        P("tp"),
        P(None, "tp", None, None),
        P("tp", None, None),
        P(("groups", "ctx", "sub"), "tp"),
        P("tp"),
        P("tp"),
        P("tp"),
        P(("tp", "sub"), None),
        P("groups"),
    )
    out_specs = P(("groups", "ctx", "sub"), "tp")
    return jax.shard_map(local, mesh=mesh, in_specs=in_specs, out_specs=out_specs, check_vma=False)
```

```python
import functools

import jax
import jax.numpy as jnp
from jax import lax
from jax.experimental import pallas as pl
from jax.experimental.pallas import tpu as pltpu
from jax.sharding import PartitionSpec as P

HEADS = 128
GROUPS = 8
CHUNK = 128
EPSILON = 1e-05
LOG2E = 1.4426950408889634
CEILING = 126.0
VMEM = 20 << 20
F32 = jnp.float32
BF16 = jnp.bfloat16


def shifted_ring(shard, axis):
    peers = lax.axis_size(axis)
    return lax.ppermute(shard, axis, [(i, (i + 1) % peers) for i in range(peers)])


def swapped(shard, axis):
    return lax.ppermute(shard, axis, [(i, i ^ 1) for i in range(lax.axis_size(axis))])


def after(*values):
    return lax.optimization_barrier(values)


def doc_start(positions, docs_ref):
    start = jnp.zeros_like(positions)
    total = jnp.int32(0)
    for doc in range(docs_ref.shape[0]):
        start = jnp.where(positions >= total, total, start)
        total = total + docs_ref[doc]
    return start


def rows_of(count, first):
    return first + lax.broadcasted_iota(jnp.int32, (count, 1), 0)


def split2(value):
    high = value.astype(BF16)
    return high, (value - high.astype(F32)).astype(BF16)


def split3(value):
    high = value.astype(BF16)
    rest = value - high.astype(F32)
    mid = rest.astype(BF16)
    return high, mid, (rest - mid.astype(F32)).astype(BF16)


def mm(a, b):
    return jnp.dot(a, b, preferred_element_type=F32)


def contract_lanes(a, b):
    return lax.dot_general(a, b, (((1,), (1,)), ((), ())), preferred_element_type=F32)


def silu(value):
    half = 0.5 * value
    return half + half * jnp.tanh(half)


def head_lanes(copies, heads, head_width, lanes, first_lane):
    shape = (copies * heads, lanes)
    head = lax.rem(lax.broadcasted_iota(jnp.int32, shape, 0), heads)
    lane = first_lane + lax.broadcasted_iota(jnp.int32, shape, 1)
    low = head * head_width
    return jnp.where((lane >= low) & (lane < low + head_width), 1.0, 0.0).astype(BF16)


def convolved(shifts, x, rim, w, bias, store, taps):
    count = x.shape[0]
    rims = rim.shape[0]
    weights = w[...].astype(F32)
    if len(weights.shape) == 4:
        weights = jnp.concatenate([weights[:, 0, 0, :], weights[:, 0, 1, :]], axis=1)
    span = min(256, x.shape[1])
    for low in range(0, x.shape[1], span):
        at = slice(low, low + span)
        value = x[:, at]
        weight = weights[:, at]
        summed = bias[:, at] + value.astype(F32) * weight[taps - 1 : taps]
        top = jnp.zeros((rims, span), F32)
        for back in range(1, taps):
            line = weight[taps - 1 - back : taps - back]
            shift, rim_shift = shifts[back - 1]
            summed = summed + mm(shift[...], value) * line
            top = top + mm(rim_shift[...], rim[:, at]) * line
        store(at, slice(0, rims), silu(summed[:rims] + top).astype(BF16))
        store(at, slice(rims, count), silu(summed[rims:]).astype(BF16))


def decay_kernel(
    meta, docs, own_raw, got_raw, rate, cum_out, dlt_out, tail_out, kept_out, raw,
):
    half = own_raw.shape[1]
    heads, count = raw.shape
    mine = meta[0] == 0
    first = meta[1]
    own_at = pl.ds(pl.multiple_of(meta[0] * half, half), half)
    got_at = pl.ds(pl.multiple_of((1 - meta[0]) * half, half), half)
    last_start = doc_start(first + count - 1, docs)
    raw[:, own_at] = jnp.where(mine, own_raw[:heads], own_raw[heads:])
    raw[:, got_at] = jnp.where(mine, got_raw[:heads], got_raw[heads:])
    value = raw[...]
    size = jnp.maximum(value, 0.0) + jnp.log(1.0 + jnp.exp(-jnp.abs(value)))
    wide = (heads, 2 * heads)
    own_head = lax.broadcasted_iota(jnp.int32, wide, 0) + meta[0] * heads
    chosen = own_head == lax.broadcasted_iota(jnp.int32, wide, 1)
    rates = jnp.sum(jnp.where(chosen, rate[...], 0.0), axis=1, keepdims=True)
    decay = (-LOG2E * jnp.exp(rates)) * size
    row = lax.broadcasted_iota(jnp.int32, (count, count), 0)
    col = lax.broadcasted_iota(jnp.int32, (count, count), 1)
    above = jnp.where(row <= col, 1.0, 0.0).astype(BF16)
    high, mid, low = split3(decay)
    cum = mm(high, above) + (mm(mid, above) + mm(low, above))
    dlt_out[...] = cum - jnp.log2(size)
    end = cum[:, count - 1 :]
    places = first + lax.broadcasted_iota(jnp.int32, (1, count), 1)
    tail = jnp.where(places >= last_start, size * jnp.exp2(end - cum), 0.0)
    high, low = split2(tail.T)
    tail_out[:, :heads] = high
    tail_out[:, heads:] = low
    cum = cum.T
    cum_out[...] = cum
    kept = jnp.exp2(jnp.broadcast_to(cum[count - 1 :], (8, heads)))
    high, mid, low = split3(jnp.where(last_start < first, kept, 0.0))
    kept_out[:, :heads] = high
    kept_out[:, heads : 2 * heads] = mid
    kept_out[:, 2 * heads :] = low


def state_kernel(
    meta, docs, x, got_x, rim_x, late_rim_x, w, bias, s, got_s, rim_s, late_rim_s, sw, sbias, tail, kept,
    x_out, bc_out, s_out, d_out, raw_x, raw_s, shift, rim_shift, b_turned,
    *, taps, heads, head_width, first_lane,
):
    step = pl.program_id(0)
    half, width = x.shape
    rims = rim_x.shape[0]
    state_width = bc_out.shape[1] // 2

    def mixed(raw, own, got, rim, late, weight, offset, out):
        raw[:rims, :] = jnp.where(meta[0] == 0, rim[...], late[...])
        raw[pl.ds(pl.multiple_of(rims + meta[0] * half, 16), half), :] = own[...]
        raw[pl.ds(pl.multiple_of(rims + (1 - meta[0]) * half, 16), half), :] = got[...]
        for index in range(2):
            low = index * half

            def store(at, rows, value, low=low):
                out[low + rows.start : low + rows.stop, at] = value

            shifts = [(shift.at[index, back], rim_shift.at[index, back]) for back in range(taps - 1)]
            convolved(
                shifts, raw.at[low + rims : low + rims + half], raw.at[low : low + rims], weight, offset, store, taps
            )

    @pl.when(step == 0)
    def _():
        row = lax.broadcasted_iota(jnp.int32, (half, half), 0)
        col = lax.broadcasted_iota(jnp.int32, (half, half), 1)
        rim_row = lax.broadcasted_iota(jnp.int32, (rims, rims), 0)
        rim_col = lax.broadcasted_iota(jnp.int32, (rims, rims), 1) - rims
        for index in range(2):
            first = meta[1] + index * half
            start = doc_start(rows_of(half, first), docs) - first
            for back in range(1, taps):
                hit = (col == row - back) & (col >= start)
                rim_hit = (rim_col == rim_row - back) & (rim_col >= start[:rims])
                shift[index, back - 1] = jnp.where(hit, 1.0, 0.0).astype(BF16)
                rim_shift[index, back - 1] = jnp.where(rim_hit, 1.0, 0.0).astype(BF16)
        mixed(raw_s, s, got_s, rim_s, late_rim_s, sw, sbias, bc_out)
        b_turned[...] = bc_out[:, :state_width].T

    mixed(raw_x, x, got_x, rim_x, late_rim_x, w, bias, x_out)
    lanes = first_lane + step * width
    tails = mm(tail[...], head_lanes(2, heads, head_width, width, lanes))
    weighted = (x_out[...].astype(F32) * tails).astype(BF16)
    s_out[...] = mm(b_turned[...], weighted).astype(BF16)
    d_out[...] = mm(kept[...], head_lanes(3, heads, head_width, width, lanes))[:1]


def intra_kernel(
    meta, docs, x_all, bc_all, cum_all, dlt_all, gate_own, gate_got, gain,
    a_out, f_out, state, spread, gates, kept_part,
    *, head_width, first_head, group_heads,
):
    total, width = x_all.shape
    heads = cum_all.shape[1]
    count = CHUNK
    splits = total // 2 // count
    state_width = bc_all.shape[1] // 2
    state[...] = jnp.zeros_like(state)
    spread[...] = head_lanes(3, heads, head_width, width, first_head * head_width)
    mine = jnp.where(meta[0] == 0, gain[:, :heads], gain[:, heads:])
    skip = mm(jnp.concatenate(split3(jnp.broadcast_to(mine, (8, heads))), axis=1), spread[...])[:1]
    row = lax.broadcasted_iota(jnp.int32, (count, count), 0)
    col = lax.broadcasted_iota(jnp.int32, (count, count), 1)
    low_lanes = lax.broadcasted_iota(jnp.int32, (count, 2 * head_width), 1) < head_width
    zero = jnp.zeros((count, 2 * head_width), BF16)

    def spread_over(value):
        return mm(jnp.concatenate(split2(value), axis=1), spread[: 2 * heads])

    def chunk(step, before):
        first = meta[1] + step * count
        rows = pl.ds(pl.multiple_of(step * count, count), count)
        half_rows = pl.ds(pl.multiple_of(lax.rem(step, splits) * count, count), count)
        starts = doc_start(rows_of(count, first), docs)
        last_start = doc_start(first + count - 1, docs)
        here = cum_all[rows, :]
        dlt = dlt_all[:, rows]
        x = x_all[rows, :]
        end = here[count - 1 :]
        b = bc_all[rows, :state_width]
        c = bc_all[rows, state_width:]
        scores = jnp.where((col <= row) & (col >= starts - first), contract_lanes(c, b), 0.0)
        reach = spread_over(jnp.where(starts < first, jnp.exp2(here - before), 0.0))
        into = spread_over(jnp.where(starts < meta[1], jnp.exp2(here), 0.0))
        to_end = jnp.exp2(end - dlt.T)
        tail = spread_over(jnp.where(rows_of(count, first) >= last_start, to_end, 0.0))
        kept = jnp.broadcast_to(jnp.where(last_start < first, jnp.exp2(end - before), 0.0), (8, heads))
        kept = mm(jnp.concatenate(split3(kept), axis=1), spread[...])[:1]
        is_own = step // splits == meta[0]
        gate = silu(jnp.where(is_own, gate_own[half_rows, :], gate_got[half_rows, :]).astype(F32))
        gates[...] = gate
        f_out[rows, :] = gate * into
        x_part = x.astype(F32)
        old = state[...]
        kept_part[...] = mm(c, old.astype(BF16)) * reach + x_part * skip
        state[...] = old * kept + mm(b.T, (x_part * tail).astype(BF16))
        for head in range(0, group_heads, 2):
            at = slice(head * head_width, (head + 2) * head_width)
            pair = []
            for k in (first_head + head, first_head + head + 1):
                exponent = jnp.minimum(here[:, k : k + 1] - dlt[k : k + 1, :], CEILING)
                pair.append((jnp.exp2(exponent) * scores).astype(BF16))
            value = x[:, at]
            stacked = jnp.concatenate(
                [jnp.where(low_lanes, value, zero), jnp.where(low_lanes, zero, value)], axis=0
            )
            within = mm(jnp.concatenate(pair, axis=1), stacked)
            a_out[rows, at] = (within + kept_part[:, at]) * gates[:, at]
        return end

    lax.fori_loop(0, total // count, chunk, jnp.zeros((1, heads), F32))


def normed(a, f, bc, incoming, gain, squares, divisor):
    state_width = bc.shape[1] // 2
    gated = a[...] + mm(bc[:, state_width:], incoming[...]) * f[...]
    total = jnp.sum(gated * gated, axis=1, keepdims=True) if squares is None else squares[...]
    return (gated * lax.rsqrt(total / divisor + EPSILON) * gain[...]).astype(BF16)


def norm_kernel(meta, a, f, bc, incoming, gain, hidden, *, divisor):
    hidden[...] = normed(a, f, bc, incoming, gain, None, divisor)


def project_kernel(meta, *refs, ready, squared, divisor):
    a, f, bc, incoming, gain = refs[ready : ready + 5]
    w, hidden, send, keep = refs[-4:]
    width = a.shape[1]

    @pl.when(pl.program_id(0) == 0)
    def _():
        for group, part in enumerate(refs[:ready]):
            hidden[:, group * width : (group + 1) * width] = part[...]
        squares = refs[ready + 5] if squared else None
        hidden[:, ready * width :] = normed(a, f, bc, incoming, gain, squares, divisor)

    multiply(meta, hidden, w, send, keep)


def multiply(meta, hidden, w, send, keep):
    half = send.shape[0]
    there = pl.ds(pl.multiple_of((1 - meta[0]) * half, half), half)
    here = pl.ds(pl.multiple_of(meta[0] * half, half), half)
    send[...] = mm(hidden[there, :], w[...]).astype(BF16)
    keep[...] = mm(hidden[here, :], w[...])


def sum_kernel(*refs):
    out = refs[-1]
    total = refs[0][...]
    for ref in refs[1:-1]:
        if ref.shape == out.shape:
            total = total + ref[...].astype(F32)
    out[...] = total.astype(out.dtype)


def local(
    x_input, gate_input, state_proj, mix_weight, mix_bias, state_weight, state_bias,
    step_raw, decay_log, skip_gain, norm_gain, out_weight, doc_lengths,
):
    half, channels = x_input.shape
    all_heads = step_raw.shape[1]
    groups, _, state_width = state_proj.shape[1:]
    taps = mix_weight.shape[0]
    features = out_weight.shape[1]
    head_width = channels // all_heads
    heads = all_heads // 2
    width = channels // 2
    count = 2 * half
    whole_groups = groups % 2 == 0
    parts = groups // 2 if whole_groups else groups
    part_heads = heads // parts
    part_width = part_heads * head_width
    block = 2 * state_width
    sub = lax.axis_index("sub").astype(jnp.int32)
    ctx = lax.axis_index("ctx").astype(jnp.int32)
    tp = lax.axis_index("tp").astype(jnp.int32)
    tp_size = lax.axis_size("tp")
    ctx_size = lax.axis_size("ctx")
    docs = doc_lengths.astype(jnp.int32)
    meta = jnp.stack([sub, ctx * count, tp])
    params = pltpu.CompilerParams(vmem_limit_bytes=VMEM)
    fixed = lambda *shape: pl.BlockSpec(shape, lambda i, *m: (0,) * len(shape))
    shape_of = jax.ShapeDtypeStruct

    def call(body, name, grid, in_specs, out_specs, out_shape, scratch=(), prefetch=2):
        kernel = pl.pallas_call(
            body,
            grid_spec=pltpu.PrefetchScalarGridSpec(
                num_scalar_prefetch=prefetch, grid=grid, in_specs=in_specs, out_specs=out_specs,
                scratch_shapes=list(scratch),
            ),
            out_shape=out_shape,
            compiler_params=params,
            cost_estimate=pl.CostEstimate(flops=0, bytes_accessed=0, transcendentals=0),
            name=name,
        )
        return lambda *operands: kernel(
            *(pltpu.with_memory_space_constraint(v, pltpu.HBM) if any(v is p for p in pinned) else v for v in operands)
        )

    s_input = state_proj.reshape(half, groups * block)
    s_bias = state_bias.reshape(1, groups * block)
    bias = mix_bias.reshape(1, channels)
    skip = skip_gain.reshape(1, all_heads)
    gain = norm_gain.reshape(1, channels)
    rate = decay_log.reshape(1, all_heads)
    pinned = [
        meta, docs, x_input, gate_input, mix_weight, bias, state_weight, s_bias, skip, gain, rate, out_weight
    ]
    rims = 16
    cut_width = min(1024, part_width)
    cuts = part_width // cut_width
    s_width = parts * block if whole_groups else groups * block
    raw = step_raw.T
    pinned.append(raw)
    last_x, last_s = x_input[half - rims :], state_proj[half - rims :].reshape(rims, groups * block)
    early_rows = jnp.concatenate([last_x[:, :width], last_s[:, :s_width]], axis=1)
    late_rows = jnp.concatenate([last_x[:, width:], last_s[:, -s_width:]], axis=1)
    got_raw, early_rows, late_rows, x_later, gate_later = after(
        swapped(raw, "sub"), early_rows, late_rows, x_input, gate_input
    )
    rim = shifted_ring(early_rows, ("ctx", "sub"))
    late_rim = shifted_ring(late_rows, "ctx")
    got_x = swapped(x_later, "sub")
    got_s = swapped(s_input, "sub")
    got_gate = swapped(gate_later, "sub")
    mixed = (x_input, got_x, rim, late_rim, mix_weight, bias, s_input, got_s, rim, late_rim, state_weight, s_bias)

    def mix_specs(part):
        at = lambda m: m[0] * parts + part
        s_at = at if whole_groups else (lambda m: 0)
        here = lambda m: part
        rim_at = lambda m: width // block + part
        specs = []
        x_at = lambda m, i: at(m) * cuts + i
        x_here = lambda m, i: here(m) * cuts + i
        specs = []
        for rows, place in zip((half, half, rims, rims, taps, 1), (x_at, x_at, x_here, x_here, x_at, x_at)):
            specs.append(pl.BlockSpec((rows, cut_width), lambda i, m, d, place=place: (0, place(m, i))))
        for rows, place in zip((half, half, rims, rims, taps, 1), (s_at, s_at, rim_at, rim_at, s_at, s_at)):
            specs.append(pl.BlockSpec((rows, block), lambda i, m, d, place=place: (0, place(m))))
        specs[10] = pl.BlockSpec((taps, 1, 2, state_width), lambda i, m, d: (0, s_at(m), 0, 0))
        return specs

    cum, dlt, tail, kept = call(
        decay_kernel, "decay", (1,),
        [fixed(all_heads, half), fixed(all_heads, half), fixed(1, all_heads)],
        [fixed(count, heads), fixed(heads, count), fixed(count, 2 * heads), fixed(8, 3 * heads)],
        [
            shape_of((count, heads), F32), shape_of((heads, count), F32),
            shape_of((count, 2 * heads), BF16), shape_of((8, 3 * heads), BF16),
        ],
        [pltpu.VMEM((heads, count), F32)],
    )(meta, docs, raw, got_raw, rate)

    made = []
    next_meta = meta
    for part in range(parts):
        x_cat, bc, state, decay = call(
            functools.partial(
                state_kernel, taps=taps, heads=heads, head_width=head_width, first_lane=part * part_width
            ),
            "state", (cuts,),
            mix_specs(part) + [fixed(count, 2 * heads), fixed(8, 3 * heads)],
            [
                pl.BlockSpec((count, cut_width), lambda i, m, d: (0, i)), fixed(count, block),
                pl.BlockSpec((state_width, cut_width), lambda i, m, d: (0, i)),
                pl.BlockSpec((1, cut_width), lambda i, m, d: (0, i)),
            ],
            [
                shape_of((count, part_width), BF16), shape_of((count, block), BF16),
                shape_of((state_width, part_width), BF16), shape_of((1, part_width), F32),
            ],
            [
                pltpu.VMEM((rims + count, cut_width), BF16), pltpu.VMEM((rims + count, block), BF16),
                pltpu.VMEM((2, taps - 1, half, half), BF16), pltpu.VMEM((2, taps - 1, rims, rims), BF16),
                pltpu.VMEM((state_width, count), BF16),
            ],
        )(next_meta, docs, *mixed, tail, kept)
        state, next_meta = after(state, next_meta)
        pinned.append(next_meta)
        made.append([x_cat, bc, state, decay, shifted_ring(state, "ctx")])
        if part:
            made[part - 1][4], made[part][0] = after(made[part - 1][4], x_cat)
    ready = []
    for part in range(parts):
        x_cat, bc, state, decay, arriving = made[part]
        if ready:
            arriving, gate = after(arriving, ready[-1][0])
            ready[-1] = (gate, *ready[-1][1:])
        for _ in range(ctx_size // 2 - 1):
            leaving = (state.astype(F32) + decay * arriving.astype(F32)).astype(BF16)
            leaving, x_cat = after(leaving, x_cat)
            arriving = shifted_ring(leaving, "ctx")
        gated, carry_gate = call(
            functools.partial(
                intra_kernel, head_width=head_width, first_head=part * part_heads, group_heads=part_heads
            ),
            "intra", (1,),
            [
                fixed(count, part_width), fixed(count, block), fixed(count, heads), fixed(heads, count),
                pl.BlockSpec((half, part_width), lambda i, m, d, part=part: (0, m[0] * parts + part)),
                pl.BlockSpec((half, part_width), lambda i, m, d, part=part: (0, m[0] * parts + part)),
                fixed(1, all_heads),
            ],
            [fixed(count, part_width), fixed(count, part_width)],
            [shape_of((count, part_width), F32)] * 2,
            [
                pltpu.VMEM((state_width, part_width), F32), pltpu.VMEM((3 * heads, part_width), BF16),
                pltpu.VMEM((CHUNK, part_width), F32), pltpu.VMEM((CHUNK, part_width), F32),
            ],
        )(meta, docs, x_cat, bc, cum, dlt, gate_input, got_gate, skip)
        ready.append((gated, carry_gate, bc, arriving))

    divisor = HEADS // GROUPS * head_width
    gain_at = lambda part: pl.BlockSpec((1, part_width), lambda i, m: (0, m[0] * parts + part))
    hiddens = []
    for part, (gated, carry_gate, bc, arriving) in enumerate(ready[:-1]):
        hiddens.append(
            call(
                functools.partial(norm_kernel, divisor=divisor), "norm", (1,),
                [
                    fixed(count, part_width), fixed(count, part_width), fixed(count, block),
                    fixed(state_width, part_width), gain_at(part),
                ],
                fixed(count, part_width), shape_of((count, part_width), BF16),
                prefetch=1,
            )(meta, gated, carry_gate, bc, arriving, gain)
        )

    gated, carry_gate, bc, arriving = ready[-1]
    if hiddens:
        arriving, hiddens[-1] = after(arriving, hiddens[-1])
    squares = []
    if not whole_groups:
        total = gated + jnp.dot(bc[:, state_width:], arriving, preferred_element_type=F32) * carry_gate
        mine = jnp.sum(total * total, axis=1, keepdims=True)
        squares = [mine + swapped(mine, "sub")]
    out_cols = features // tp_size
    mm_cols = min(512, out_cols)
    pair = tp_size == 2
    near_blocks = out_cols // mm_cols
    row_specs = [pl.BlockSpec((half, mm_cols), lambda i, m: (0, i))] * 2

    def product(first, blocks, body, name, operands, specs, outs, out_shapes):
        cols = blocks * mm_cols
        return call(
            body, name, (blocks,),
            specs + [pl.BlockSpec((width, mm_cols), lambda i, m: (0, first(m, i)))],
            outs + row_specs,
            out_shapes + [shape_of((half, cols), BF16), shape_of((half, cols), F32)],
            prefetch=1,
        )(meta, *operands, out_weight)

    operands = [*hiddens, gated, carry_gate, bc, arriving, gain, *squares]
    specs = [fixed(*v.shape) for v in operands]
    specs[len(hiddens) + 4] = gain_at(parts - 1)
    project = functools.partial(project_kernel, ready=len(hiddens), squared=len(squares), divisor=divisor)
    hidden_spec, hidden_shape = fixed(count, width), shape_of((count, width), BF16)
    if not pair:
        every = features // mm_cols
        _, send, keep = product(lambda m, i: i, every, project, "project", operands, specs, [hidden_spec], [hidden_shape])
        summed = (keep + swapped(send, "sub").astype(F32)).astype(BF16)
        return lax.psum_scatter(summed, "tp", scatter_dimension=1, tiled=True)
    lead = max(3 * near_blocks // 4, 1)
    far_first = lambda m: (1 - m[2]) * near_blocks
    hidden, send, keep = product(
        lambda m, i: far_first(m) + i, lead, project, "project", operands, specs, [hidden_spec], [hidden_shape]
    )
    summed = (keep + swapped(send, "sub").astype(F32)).astype(BF16)
    hidden, summed = after(hidden, summed)
    far_lead = swapped(summed, "tp")
    rest = near_blocks - lead
    send, keep = product(
        lambda m, i: far_first(m) + lead + i, rest, multiply, "product", [hidden], [hidden_spec], [], []
    )
    summed = (keep + swapped(send, "sub").astype(F32)).astype(BF16)
    hidden, summed = after(hidden, summed)
    far_rest = swapped(summed, "tp")
    send, keep = product(
        lambda m, i: m[2] * near_blocks + i, near_blocks, multiply, "product", [hidden], [hidden_spec], [], [],
    )
    got = swapped(send, "sub")

    def finish(first, terms, name, dtype, old=(), weight=0):
        blocks = min(v.shape[1] for v in terms) // mm_cols
        at = lambda v: (lambda i: (0, i + (first if v.shape[1] == out_cols else 0)))
        cols = out_cols if dtype == BF16 else blocks * mm_cols
        return pl.pallas_call(
            sum_kernel, grid=(blocks,),
            in_specs=[pl.BlockSpec((half, mm_cols), at(v)) for v in terms]
            + [pl.BlockSpec(memory_space=pl.ANY)] * len(old),
            out_specs=pl.BlockSpec((half, mm_cols), lambda i: (0, i + (first if dtype == BF16 else 0))),
            out_shape=shape_of((half, cols), dtype),
            input_output_aliases={len(terms): 0} if old else {},
            compiler_params=params,
            cost_estimate=pl.CostEstimate(flops=weight, bytes_accessed=0, transcendentals=0),
            name=name,
        )(*terms, *old)

    early = finish(0, [keep, far_lead], "early", F32, weight=1 << 38)
    output = finish(0, [early, got], "lead", BF16)
    cut = lead * mm_cols
    last = (keep[:, cut:] + got[:, cut:].astype(F32) + far_rest.astype(F32)).astype(BF16)
    return lax.dynamic_update_slice(output, last, (0, cut))


def solution(mesh):
    in_specs = (
        P(("groups", "ctx", "sub"), "tp"),
        P(("groups", "ctx", "sub"), "tp"),
        P(("groups", "ctx", "sub"), "tp", None, None),
        P(None, "tp"),
        P("tp"),
        P(None, "tp", None, None),
        P("tp", None, None),
        P(("groups", "ctx", "sub"), "tp"),
        P("tp"),
        P("tp"),
        P("tp"),
        P(("tp", "sub"), None),
        P("groups"),
    )
    out_specs = P(("groups", "ctx", "sub"), "tp")
    return jax.shard_map(local, mesh=mesh, in_specs=in_specs, out_specs=out_specs, check_vma=False)
```

```python
import functools

import jax
import jax.numpy as jnp
from jax import lax
from jax.experimental import pallas as pl
from jax.experimental.pallas import tpu as pltpu
from jax.sharding import PartitionSpec as P

HEADS = 128
GROUPS = 8
CHUNK = 128
EPSILON = 1e-05
LOG2E = 1.4426950408889634
CEILING = 126.0
VMEM = 28 << 20
F32 = jnp.float32
BF16 = jnp.bfloat16


def shifted_ring(shard, axis):
    peers = lax.axis_size(axis)
    return lax.ppermute(shard, axis, [(i, (i + 1) % peers) for i in range(peers)])


def swapped(shard, axis):
    return lax.ppermute(shard, axis, [(i, i ^ 1) for i in range(lax.axis_size(axis))])


def after(*values):
    return lax.optimization_barrier(values)


def doc_start(positions, docs_ref):
    start = jnp.zeros_like(positions)
    total = jnp.int32(0)
    for doc in range(docs_ref.shape[0]):
        start = jnp.where(positions >= total, total, start)
        total = total + docs_ref[doc]
    return start


def rows_of(count, first):
    return first + lax.broadcasted_iota(jnp.int32, (count, 1), 0)


def split2(value):
    high = value.astype(BF16)
    return high, (value - high.astype(F32)).astype(BF16)


def split3(value):
    high = value.astype(BF16)
    rest = value - high.astype(F32)
    mid = rest.astype(BF16)
    return high, mid, (rest - mid.astype(F32)).astype(BF16)


def mm(a, b):
    return jnp.dot(a, b, preferred_element_type=F32)


def contract_lanes(a, b):
    return lax.dot_general(a, b, (((1,), (1,)), ((), ())), preferred_element_type=F32)


def silu(value):
    half = 0.5 * value
    return half + half * jnp.tanh(half)


def head_lanes(copies, heads, head_width, lanes, first_lane):
    shape = (copies * heads, lanes)
    head = lax.rem(lax.broadcasted_iota(jnp.int32, shape, 0), heads)
    lane = first_lane + lax.broadcasted_iota(jnp.int32, shape, 1)
    low = head * head_width
    return jnp.where((lane >= low) & (lane < low + head_width), 1.0, 0.0).astype(BF16)


def convolved(shifts, x, rim, w, bias, store, taps):
    count = x.shape[0]
    rims = rim.shape[0]
    weights = w[...].astype(F32)
    if len(weights.shape) == 4:
        weights = jnp.concatenate([weights[:, 0, 0, :], weights[:, 0, 1, :]], axis=1)
    span = min(256, x.shape[1])
    for low in range(0, x.shape[1], span):
        at = slice(low, low + span)
        value = x[:, at]
        weight = weights[:, at]
        summed = bias[:, at] + value.astype(F32) * weight[taps - 1 : taps]
        top = jnp.zeros((rims, span), F32)
        for back in range(1, taps):
            line = weight[taps - 1 - back : taps - back]
            shift, rim_shift = shifts[back - 1]
            summed = summed + mm(shift[...], value) * line
            top = top + mm(rim_shift[...], rim[:, at]) * line
        store(at, slice(0, rims), silu(summed[:rims] + top).astype(BF16))
        store(at, slice(rims, count), silu(summed[rims:]).astype(BF16))


def decay_kernel(
    meta, docs, own_raw, got_raw, rate, cum_out, dlt_out, tail_out, kept_out, raw,
):
    half = own_raw.shape[1]
    heads, count = raw.shape
    mine = meta[0] == 0
    first = meta[1]
    own_at = pl.ds(pl.multiple_of(meta[0] * half, half), half)
    got_at = pl.ds(pl.multiple_of((1 - meta[0]) * half, half), half)
    last_start = doc_start(first + count - 1, docs)
    raw[:, own_at] = jnp.where(mine, own_raw[:heads], own_raw[heads:])
    raw[:, got_at] = jnp.where(mine, got_raw[:heads], got_raw[heads:])
    value = raw[...]
    size = jnp.maximum(value, 0.0) + jnp.log(1.0 + jnp.exp(-jnp.abs(value)))
    wide = (heads, 2 * heads)
    own_head = lax.broadcasted_iota(jnp.int32, wide, 0) + meta[0] * heads
    chosen = own_head == lax.broadcasted_iota(jnp.int32, wide, 1)
    rates = jnp.sum(jnp.where(chosen, rate[...], 0.0), axis=1, keepdims=True)
    decay = (-LOG2E * jnp.exp(rates)) * size
    row = lax.broadcasted_iota(jnp.int32, (count, count), 0)
    col = lax.broadcasted_iota(jnp.int32, (count, count), 1)
    above = jnp.where(row <= col, 1.0, 0.0).astype(BF16)
    high, mid, low = split3(decay)
    cum = mm(high, above) + (mm(mid, above) + mm(low, above))
    dlt_out[...] = cum - jnp.log2(size)
    end = cum[:, count - 1 :]
    places = first + lax.broadcasted_iota(jnp.int32, (1, count), 1)
    tail = jnp.where(places >= last_start, size * jnp.exp2(end - cum), 0.0)
    high, low = split2(tail.T)
    tail_out[:, :heads] = high
    tail_out[:, heads:] = low
    cum = cum.T
    cum_out[...] = cum
    kept = jnp.exp2(jnp.broadcast_to(cum[count - 1 :], (8, heads)))
    high, mid, low = split3(jnp.where(last_start < first, kept, 0.0))
    kept_out[:, :heads] = high
    kept_out[:, heads : 2 * heads] = mid
    kept_out[:, 2 * heads :] = low


def state_kernel(
    meta, docs, x, got_x, rim_x, late_rim_x, w, bias, s, got_s, rim_s, late_rim_s, sw, sbias, tail, kept,
    x_out, bc_out, s_out, d_out, raw_x, raw_s, shift, rim_shift, b_turned,
    *, taps, heads, head_width, first_lane,
):
    step = pl.program_id(0)
    half, width = x.shape
    rims = rim_x.shape[0]
    state_width = bc_out.shape[1] // 2

    def mixed(raw, own, got, rim, late, weight, offset, out):
        raw[:rims, :] = jnp.where(meta[0] == 0, rim[...], late[...])
        raw[pl.ds(pl.multiple_of(rims + meta[0] * half, 16), half), :] = own[...]
        raw[pl.ds(pl.multiple_of(rims + (1 - meta[0]) * half, 16), half), :] = got[...]
        for index in range(2):
            low = index * half

            def store(at, rows, value, low=low):
                out[low + rows.start : low + rows.stop, at] = value

            shifts = [(shift.at[index, back], rim_shift.at[index, back]) for back in range(taps - 1)]
            convolved(
                shifts, raw.at[low + rims : low + rims + half], raw.at[low : low + rims], weight, offset, store, taps
            )

    @pl.when(step == 0)
    def _():
        row = lax.broadcasted_iota(jnp.int32, (half, half), 0)
        col = lax.broadcasted_iota(jnp.int32, (half, half), 1)
        rim_row = lax.broadcasted_iota(jnp.int32, (rims, rims), 0)
        rim_col = lax.broadcasted_iota(jnp.int32, (rims, rims), 1) - rims
        for index in range(2):
            first = meta[1] + index * half
            start = doc_start(rows_of(half, first), docs) - first
            for back in range(1, taps):
                hit = (col == row - back) & (col >= start)
                rim_hit = (rim_col == rim_row - back) & (rim_col >= start[:rims])
                shift[index, back - 1] = jnp.where(hit, 1.0, 0.0).astype(BF16)
                rim_shift[index, back - 1] = jnp.where(rim_hit, 1.0, 0.0).astype(BF16)
        mixed(raw_s, s, got_s, rim_s, late_rim_s, sw, sbias, bc_out)
        b_turned[...] = bc_out[:, :state_width].T

    mixed(raw_x, x, got_x, rim_x, late_rim_x, w, bias, x_out)
    lanes = first_lane + step * width
    tails = mm(tail[...], head_lanes(2, heads, head_width, width, lanes))
    weighted = (x_out[...].astype(F32) * tails).astype(BF16)
    s_out[...] = mm(b_turned[...], weighted).astype(BF16)
    d_out[...] = mm(kept[...], head_lanes(3, heads, head_width, width, lanes))[:1]


def intra_kernel(
    meta, docs, x_all, bc_all, cum_all, dlt_all, gate_own, gate_got, gain,
    a_out, f_out, state, spread, gates, kept_part,
    *, head_width, first_head, group_heads,
):
    total, width = x_all.shape
    heads = cum_all.shape[1]
    count = CHUNK
    splits = total // 2 // count
    state_width = bc_all.shape[1] // 2
    state[...] = jnp.zeros_like(state)
    spread[...] = head_lanes(3, heads, head_width, width, first_head * head_width)
    mine = jnp.where(meta[0] == 0, gain[:, :heads], gain[:, heads:])
    skip = mm(jnp.concatenate(split3(jnp.broadcast_to(mine, (8, heads))), axis=1), spread[...])[:1]
    row = lax.broadcasted_iota(jnp.int32, (count, count), 0)
    col = lax.broadcasted_iota(jnp.int32, (count, count), 1)
    low_lanes = lax.broadcasted_iota(jnp.int32, (count, 2 * head_width), 1) < head_width
    zero = jnp.zeros((count, 2 * head_width), BF16)

    def spread_over(value):
        return mm(jnp.concatenate(split2(value), axis=1), spread[: 2 * heads])

    def chunk(step, before):
        first = meta[1] + step * count
        rows = pl.ds(pl.multiple_of(step * count, count), count)
        half_rows = pl.ds(pl.multiple_of(lax.rem(step, splits) * count, count), count)
        starts = doc_start(rows_of(count, first), docs)
        last_start = doc_start(first + count - 1, docs)
        here = cum_all[rows, :]
        dlt = dlt_all[:, rows]
        x = x_all[rows, :]
        end = here[count - 1 :]
        b = bc_all[rows, :state_width]
        c = bc_all[rows, state_width:]
        scores = jnp.where((col <= row) & (col >= starts - first), contract_lanes(c, b), 0.0)
        reach = spread_over(jnp.where(starts < first, jnp.exp2(here - before), 0.0))
        into = spread_over(jnp.where(starts < meta[1], jnp.exp2(here), 0.0))
        to_end = jnp.exp2(end - dlt.T)
        tail = spread_over(jnp.where(rows_of(count, first) >= last_start, to_end, 0.0))
        kept = jnp.broadcast_to(jnp.where(last_start < first, jnp.exp2(end - before), 0.0), (8, heads))
        kept = mm(jnp.concatenate(split3(kept), axis=1), spread[...])[:1]
        is_own = step // splits == meta[0]
        gate = silu(jnp.where(is_own, gate_own[half_rows, :], gate_got[half_rows, :]).astype(F32))
        gates[...] = gate
        f_out[rows, :] = gate * into
        x_part = x.astype(F32)
        old = state[...]
        kept_part[...] = mm(c, old.astype(BF16)) * reach + x_part * skip
        state[...] = old * kept + mm(b.T, (x_part * tail).astype(BF16))
        for head in range(0, group_heads, 2):
            at = slice(head * head_width, (head + 2) * head_width)
            pair = []
            for k in (first_head + head, first_head + head + 1):
                exponent = jnp.minimum(here[:, k : k + 1] - dlt[k : k + 1, :], CEILING)
                pair.append((jnp.exp2(exponent) * scores).astype(BF16))
            value = x[:, at]
            stacked = jnp.concatenate(
                [jnp.where(low_lanes, value, zero), jnp.where(low_lanes, zero, value)], axis=0
            )
            within = mm(jnp.concatenate(pair, axis=1), stacked)
            a_out[rows, at] = (within + kept_part[:, at]) * gates[:, at]
        return end

    lax.fori_loop(0, total // count, chunk, jnp.zeros((1, heads), F32))


def normed(a, f, bc, incoming, gain, squares, divisor):
    state_width = bc.shape[1] // 2
    gated = a[...] + mm(bc[:, state_width:], incoming[...]) * f[...]
    total = jnp.sum(gated * gated, axis=1, keepdims=True) if squares is None else squares[...]
    return (gated * lax.rsqrt(total / divisor + EPSILON) * gain[...]).astype(BF16)


def norm_kernel(meta, a, f, bc, incoming, gain, hidden, *, divisor):
    hidden[...] = normed(a, f, bc, incoming, gain, None, divisor)


def project_kernel(meta, *refs, ready, squared, divisor):
    a, f, bc, incoming, gain = refs[ready : ready + 5]
    w, hidden, send, keep = refs[-4:]
    width = a.shape[1]

    @pl.when(pl.program_id(0) == 0)
    def _():
        for group, part in enumerate(refs[:ready]):
            hidden[:, group * width : (group + 1) * width] = part[...]
        squares = refs[ready + 5] if squared else None
        hidden[:, ready * width :] = normed(a, f, bc, incoming, gain, squares, divisor)

    multiply(meta, hidden, w, send, keep)


def multiply(meta, hidden, w, send, keep):
    half = send.shape[0]
    there = pl.ds(pl.multiple_of((1 - meta[0]) * half, half), half)
    here = pl.ds(pl.multiple_of(meta[0] * half, half), half)
    send[...] = mm(hidden[there, :], w[...]).astype(BF16)
    keep[...] = mm(hidden[here, :], w[...])


def sum_kernel(*refs):
    out = refs[-1]
    total = refs[0][...]
    for ref in refs[1:-1]:
        if ref.shape == out.shape:
            total = total + ref[...].astype(F32)
    out[...] = total.astype(out.dtype)


def local(
    x_input, gate_input, state_proj, mix_weight, mix_bias, state_weight, state_bias,
    step_raw, decay_log, skip_gain, norm_gain, out_weight, doc_lengths,
):
    half, channels = x_input.shape
    all_heads = step_raw.shape[1]
    groups, _, state_width = state_proj.shape[1:]
    taps = mix_weight.shape[0]
    features = out_weight.shape[1]
    head_width = channels // all_heads
    heads = all_heads // 2
    width = channels // 2
    count = 2 * half
    whole_groups = groups % 2 == 0
    parts = groups // 2 if whole_groups else groups
    part_heads = heads // parts
    part_width = part_heads * head_width
    block = 2 * state_width
    sub = lax.axis_index("sub").astype(jnp.int32)
    ctx = lax.axis_index("ctx").astype(jnp.int32)
    tp = lax.axis_index("tp").astype(jnp.int32)
    tp_size = lax.axis_size("tp")
    ctx_size = lax.axis_size("ctx")
    docs = doc_lengths.astype(jnp.int32)
    meta = jnp.stack([sub, ctx * count, tp])
    params = pltpu.CompilerParams(vmem_limit_bytes=VMEM)
    fixed = lambda *shape: pl.BlockSpec(shape, lambda i, *m: (0,) * len(shape))
    shape_of = jax.ShapeDtypeStruct

    def call(body, name, grid, in_specs, out_specs, out_shape, scratch=(), prefetch=2):
        kernel = pl.pallas_call(
            body,
            grid_spec=pltpu.PrefetchScalarGridSpec(
                num_scalar_prefetch=prefetch, grid=grid, in_specs=in_specs, out_specs=out_specs,
                scratch_shapes=list(scratch),
            ),
            out_shape=out_shape,
            compiler_params=params,
            cost_estimate=pl.CostEstimate(flops=0, bytes_accessed=0, transcendentals=0),
            name=name,
        )
        return lambda *operands: kernel(
            *(pltpu.with_memory_space_constraint(v, pltpu.HBM) if any(v is p for p in pinned) else v for v in operands)
        )

    s_input = state_proj.reshape(half, groups * block)
    s_bias = state_bias.reshape(1, groups * block)
    bias = mix_bias.reshape(1, channels)
    skip = skip_gain.reshape(1, all_heads)
    gain = norm_gain.reshape(1, channels)
    rate = decay_log.reshape(1, all_heads)
    pinned = [
        meta, docs, x_input, gate_input, mix_weight, bias, state_weight, s_bias, skip, gain, rate, out_weight
    ]
    rims = 16
    cut_width = min(1024, part_width)
    cuts = part_width // cut_width
    s_width = parts * block if whole_groups else groups * block
    raw = step_raw.T
    pinned.append(raw)
    last_x, last_s = x_input[half - rims :], state_proj[half - rims :].reshape(rims, groups * block)
    early_rows = jnp.concatenate([last_x[:, :width], last_s[:, :s_width]], axis=1)
    late_rows = jnp.concatenate([last_x[:, width:], last_s[:, -s_width:]], axis=1)
    got_raw, early_rows, late_rows, x_later, gate_later = after(
        swapped(raw, "sub"), early_rows, late_rows, x_input, gate_input
    )
    rim = shifted_ring(early_rows, ("ctx", "sub"))
    late_rim = shifted_ring(late_rows, "ctx")
    got_x = swapped(x_later, "sub")
    got_s = swapped(s_input, "sub")
    got_gate = swapped(gate_later, "sub")
    mixed = (x_input, got_x, rim, late_rim, mix_weight, bias, s_input, got_s, rim, late_rim, state_weight, s_bias)

    def mix_specs(part):
        at = lambda m: m[0] * parts + part
        s_at = at if whole_groups else (lambda m: 0)
        here = lambda m: part
        rim_at = lambda m: width // block + part
        specs = []
        x_at = lambda m, i: at(m) * cuts + i
        x_here = lambda m, i: here(m) * cuts + i
        specs = []
        for rows, place in zip((half, half, rims, rims, taps, 1), (x_at, x_at, x_here, x_here, x_at, x_at)):
            specs.append(pl.BlockSpec((rows, cut_width), lambda i, m, d, place=place: (0, place(m, i))))
        for rows, place in zip((half, half, rims, rims, taps, 1), (s_at, s_at, rim_at, rim_at, s_at, s_at)):
            specs.append(pl.BlockSpec((rows, block), lambda i, m, d, place=place: (0, place(m))))
        specs[10] = pl.BlockSpec((taps, 1, 2, state_width), lambda i, m, d: (0, s_at(m), 0, 0))
        return specs

    cum, dlt, tail, kept = call(
        decay_kernel, "decay", (1,),
        [fixed(all_heads, half), fixed(all_heads, half), fixed(1, all_heads)],
        [fixed(count, heads), fixed(heads, count), fixed(count, 2 * heads), fixed(8, 3 * heads)],
        [
            shape_of((count, heads), F32), shape_of((heads, count), F32),
            shape_of((count, 2 * heads), BF16), shape_of((8, 3 * heads), BF16),
        ],
        [pltpu.VMEM((heads, count), F32)],
    )(meta, docs, raw, got_raw, rate)

    made = []
    next_meta = meta
    for part in range(parts):
        x_cat, bc, state, decay = call(
            functools.partial(
                state_kernel, taps=taps, heads=heads, head_width=head_width, first_lane=part * part_width
            ),
            "state", (cuts,),
            mix_specs(part) + [fixed(count, 2 * heads), fixed(8, 3 * heads)],
            [
                pl.BlockSpec((count, cut_width), lambda i, m, d: (0, i)), fixed(count, block),
                pl.BlockSpec((state_width, cut_width), lambda i, m, d: (0, i)),
                pl.BlockSpec((1, cut_width), lambda i, m, d: (0, i)),
            ],
            [
                shape_of((count, part_width), BF16), shape_of((count, block), BF16),
                shape_of((state_width, part_width), BF16), shape_of((1, part_width), F32),
            ],
            [
                pltpu.VMEM((rims + count, cut_width), BF16), pltpu.VMEM((rims + count, block), BF16),
                pltpu.VMEM((2, taps - 1, half, half), BF16), pltpu.VMEM((2, taps - 1, rims, rims), BF16),
                pltpu.VMEM((state_width, count), BF16),
            ],
        )(next_meta, docs, *mixed, tail, kept)
        state, next_meta = after(state, next_meta)
        pinned.append(next_meta)
        made.append([x_cat, bc, state, decay, shifted_ring(state, "ctx")])
        if part:
            made[part - 1][4], made[part][0] = after(made[part - 1][4], x_cat)
    ready = []
    for part in range(parts):
        x_cat, bc, state, decay, arriving = made[part]
        if ready:
            arriving, gate = after(arriving, ready[-1][0])
            ready[-1] = (gate, *ready[-1][1:])
        for _ in range(ctx_size // 2 - 1):
            leaving = (state.astype(F32) + decay * arriving.astype(F32)).astype(BF16)
            leaving, x_cat = after(leaving, x_cat)
            arriving = shifted_ring(leaving, "ctx")
        gated, carry_gate = call(
            functools.partial(
                intra_kernel, head_width=head_width, first_head=part * part_heads, group_heads=part_heads
            ),
            "intra", (1,),
            [
                fixed(count, part_width), fixed(count, block), fixed(count, heads), fixed(heads, count),
                pl.BlockSpec((half, part_width), lambda i, m, d, part=part: (0, m[0] * parts + part)),
                pl.BlockSpec((half, part_width), lambda i, m, d, part=part: (0, m[0] * parts + part)),
                fixed(1, all_heads),
            ],
            [fixed(count, part_width), fixed(count, part_width)],
            [shape_of((count, part_width), F32)] * 2,
            [
                pltpu.VMEM((state_width, part_width), F32), pltpu.VMEM((3 * heads, part_width), BF16),
                pltpu.VMEM((CHUNK, part_width), F32), pltpu.VMEM((CHUNK, part_width), F32),
            ],
        )(meta, docs, x_cat, bc, cum, dlt, gate_input, got_gate, skip)
        ready.append((gated, carry_gate, bc, arriving))

    divisor = HEADS // GROUPS * head_width
    gain_at = lambda part: pl.BlockSpec((1, part_width), lambda i, m: (0, m[0] * parts + part))
    hiddens = []
    for part, (gated, carry_gate, bc, arriving) in enumerate(ready[:-1]):
        hiddens.append(
            call(
                functools.partial(norm_kernel, divisor=divisor), "norm", (1,),
                [
                    fixed(count, part_width), fixed(count, part_width), fixed(count, block),
                    fixed(state_width, part_width), gain_at(part),
                ],
                fixed(count, part_width), shape_of((count, part_width), BF16),
                prefetch=1,
            )(meta, gated, carry_gate, bc, arriving, gain)
        )

    gated, carry_gate, bc, arriving = ready[-1]
    if hiddens:
        arriving, hiddens[-1] = after(arriving, hiddens[-1])
    squares = []
    if not whole_groups:
        total = gated + jnp.dot(bc[:, state_width:], arriving, preferred_element_type=F32) * carry_gate
        mine = jnp.sum(total * total, axis=1, keepdims=True)
        squares = [mine + swapped(mine, "sub")]
    out_cols = features // tp_size
    mm_cols = min(512, out_cols)
    pair = tp_size == 2
    near_blocks = out_cols // mm_cols
    row_specs = [pl.BlockSpec((half, mm_cols), lambda i, m: (0, i))] * 2

    def product(first, blocks, body, name, operands, specs, outs, out_shapes):
        cols = blocks * mm_cols
        return call(
            body, name, (blocks,),
            specs + [pl.BlockSpec((width, mm_cols), lambda i, m: (0, first(m, i)))],
            outs + row_specs,
            out_shapes + [shape_of((half, cols), BF16), shape_of((half, cols), F32)],
            prefetch=1,
        )(meta, *operands, out_weight)

    operands = [*hiddens, gated, carry_gate, bc, arriving, gain, *squares]
    specs = [fixed(*v.shape) for v in operands]
    specs[len(hiddens) + 4] = gain_at(parts - 1)
    project = functools.partial(project_kernel, ready=len(hiddens), squared=len(squares), divisor=divisor)
    hidden_spec, hidden_shape = fixed(count, width), shape_of((count, width), BF16)
    if not pair:
        every = features // mm_cols
        _, send, keep = product(lambda m, i: i, every, project, "project", operands, specs, [hidden_spec], [hidden_shape])
        summed = (keep + swapped(send, "sub").astype(F32)).astype(BF16)
        return lax.psum_scatter(summed, "tp", scatter_dimension=1, tiled=True)
    lead = max(3 * near_blocks // 4, 1)
    far_first = lambda m: (1 - m[2]) * near_blocks
    hidden, send, keep = product(
        lambda m, i: far_first(m) + i, lead, project, "project", operands, specs, [hidden_spec], [hidden_shape]
    )
    summed = (keep + swapped(send, "sub").astype(F32)).astype(BF16)
    hidden, summed = after(hidden, summed)
    far_lead = swapped(summed, "tp")
    rest = near_blocks - lead
    send, keep = product(
        lambda m, i: far_first(m) + lead + i, rest, multiply, "product", [hidden], [hidden_spec], [], []
    )
    summed = (keep + swapped(send, "sub").astype(F32)).astype(BF16)
    hidden, summed = after(hidden, summed)
    far_rest = swapped(summed, "tp")
    send, keep = product(
        lambda m, i: m[2] * near_blocks + i, near_blocks, multiply, "product", [hidden], [hidden_spec], [], [],
    )
    got = swapped(send, "sub")

    def finish(first, terms, name, dtype, old=(), weight=0):
        blocks = min(v.shape[1] for v in terms) // mm_cols
        at = lambda v: (lambda i: (0, i + (first if v.shape[1] == out_cols else 0)))
        cols = out_cols if dtype == BF16 else blocks * mm_cols
        return pl.pallas_call(
            sum_kernel, grid=(blocks,),
            in_specs=[pl.BlockSpec((half, mm_cols), at(v)) for v in terms]
            + [pl.BlockSpec(memory_space=pl.ANY)] * len(old),
            out_specs=pl.BlockSpec((half, mm_cols), lambda i: (0, i + (first if dtype == BF16 else 0))),
            out_shape=shape_of((half, cols), dtype),
            input_output_aliases={len(terms): 0} if old else {},
            compiler_params=params,
            cost_estimate=pl.CostEstimate(flops=weight, bytes_accessed=0, transcendentals=0),
            name=name,
        )(*terms, *old)

    early = finish(0, [keep, far_lead], "early", F32, weight=1 << 38)
    output = finish(0, [early, got], "lead", BF16)
    cut = lead * mm_cols
    (near,) = after(keep[:, cut:] + got[:, cut:].astype(F32))
    last = (near + far_rest.astype(F32)).astype(BF16)
    return lax.dynamic_update_slice(output, last, (0, cut))


def solution(mesh):
    in_specs = (
        P(("groups", "ctx", "sub"), "tp"),
        P(("groups", "ctx", "sub"), "tp"),
        P(("groups", "ctx", "sub"), "tp", None, None),
        P(None, "tp"),
        P("tp"),
        P(None, "tp", None, None),
        P("tp", None, None),
        P(("groups", "ctx", "sub"), "tp"),
        P("tp"),
        P("tp"),
        P("tp"),
        P(("tp", "sub"), None),
        P("groups"),
    )
    out_specs = P(("groups", "ctx", "sub"), "tp")
    return jax.shard_map(local, mesh=mesh, in_specs=in_specs, out_specs=out_specs, check_vma=False)
```

```python
import functools

import jax
import jax.numpy as jnp
from jax import lax
from jax.experimental import pallas as pl
from jax.experimental.pallas import tpu as pltpu
from jax.sharding import PartitionSpec as P

HEADS = 128
GROUPS = 8
CHUNK = 128
EPSILON = 1e-05
LOG2E = 1.4426950408889634
CEILING = 126.0
VMEM = 20 << 20
F32 = jnp.float32
BF16 = jnp.bfloat16


def shifted_ring(shard, axis):
    peers = lax.axis_size(axis)
    return lax.ppermute(shard, axis, [(i, (i + 1) % peers) for i in range(peers)])


def swapped(shard, axis):
    return lax.ppermute(shard, axis, [(i, i ^ 1) for i in range(lax.axis_size(axis))])


def after(*values):
    return lax.optimization_barrier(values)


def doc_start(positions, docs_ref):
    start = jnp.zeros_like(positions)
    total = jnp.int32(0)
    for doc in range(docs_ref.shape[0]):
        start = jnp.where(positions >= total, total, start)
        total = total + docs_ref[doc]
    return start


def rows_of(count, first):
    return first + lax.broadcasted_iota(jnp.int32, (count, 1), 0)


def split2(value):
    high = value.astype(BF16)
    return high, (value - high.astype(F32)).astype(BF16)


def split3(value):
    high = value.astype(BF16)
    rest = value - high.astype(F32)
    mid = rest.astype(BF16)
    return high, mid, (rest - mid.astype(F32)).astype(BF16)


def mm(a, b):
    return jnp.dot(a, b, preferred_element_type=F32)


def contract_lanes(a, b):
    return lax.dot_general(a, b, (((1,), (1,)), ((), ())), preferred_element_type=F32)


def silu(value):
    half = 0.5 * value
    return half + half * jnp.tanh(half)


def head_lanes(copies, heads, head_width, lanes, first_lane):
    shape = (copies * heads, lanes)
    head = lax.rem(lax.broadcasted_iota(jnp.int32, shape, 0), heads)
    lane = first_lane + lax.broadcasted_iota(jnp.int32, shape, 1)
    low = head * head_width
    return jnp.where((lane >= low) & (lane < low + head_width), 1.0, 0.0).astype(BF16)


def convolved(shifts, x, rim, w, bias, store, taps):
    count = x.shape[0]
    rims = rim.shape[0]
    weights = w[...].astype(F32)
    if len(weights.shape) == 4:
        weights = jnp.concatenate([weights[:, 0, 0, :], weights[:, 0, 1, :]], axis=1)
    span = min(256, x.shape[1])
    for low in range(0, x.shape[1], span):
        at = slice(low, low + span)
        value = x[:, at]
        weight = weights[:, at]
        summed = bias[:, at] + value.astype(F32) * weight[taps - 1 : taps]
        top = jnp.zeros((rims, span), F32)
        for back in range(1, taps):
            line = weight[taps - 1 - back : taps - back]
            shift, rim_shift = shifts[back - 1]
            summed = summed + mm(shift[...], value) * line
            top = top + mm(rim_shift[...], rim[:, at]) * line
        store(at, slice(0, rims), silu(summed[:rims] + top).astype(BF16))
        store(at, slice(rims, count), silu(summed[rims:]).astype(BF16))


def decay_kernel(
    meta, docs, own_raw, got_raw, rate, cum_out, dlt_out, tail_out, kept_out, raw,
):
    half = own_raw.shape[1]
    heads, count = raw.shape
    mine = meta[0] == 0
    first = meta[1]
    own_at = pl.ds(pl.multiple_of(meta[0] * half, half), half)
    got_at = pl.ds(pl.multiple_of((1 - meta[0]) * half, half), half)
    last_start = doc_start(first + count - 1, docs)
    raw[:, own_at] = jnp.where(mine, own_raw[:heads], own_raw[heads:])
    raw[:, got_at] = jnp.where(mine, got_raw[:heads], got_raw[heads:])
    value = raw[...]
    size = jnp.maximum(value, 0.0) + jnp.log(1.0 + jnp.exp(-jnp.abs(value)))
    wide = (heads, 2 * heads)
    own_head = lax.broadcasted_iota(jnp.int32, wide, 0) + meta[0] * heads
    chosen = own_head == lax.broadcasted_iota(jnp.int32, wide, 1)
    rates = jnp.sum(jnp.where(chosen, rate[...], 0.0), axis=1, keepdims=True)
    decay = (-LOG2E * jnp.exp(rates)) * size
    row = lax.broadcasted_iota(jnp.int32, (count, count), 0)
    col = lax.broadcasted_iota(jnp.int32, (count, count), 1)
    above = jnp.where(row <= col, 1.0, 0.0).astype(BF16)
    sums = mm(jnp.concatenate(split3(decay), axis=0), above)
    cum = sums[:heads] + (sums[heads : 2 * heads] + sums[2 * heads :])
    dlt_out[...] = cum - jnp.log2(size)
    end = cum[:, count - 1 :]
    places = first + lax.broadcasted_iota(jnp.int32, (1, count), 1)
    tail = jnp.where(places >= last_start, size * jnp.exp2(end - cum), 0.0)
    high, low = split2(tail.T)
    tail_out[:, :heads] = high
    tail_out[:, heads:] = low
    cum = cum.T
    cum_out[...] = cum
    kept = jnp.exp2(jnp.broadcast_to(cum[count - 1 :], (8, heads)))
    high, mid, low = split3(jnp.where(last_start < first, kept, 0.0))
    kept_out[:, :heads] = high
    kept_out[:, heads : 2 * heads] = mid
    kept_out[:, 2 * heads :] = low


def state_kernel(
    meta, docs, x, got_x, rim_x, late_rim_x, w, bias, s, got_s, rim_s, late_rim_s, sw, sbias, tail, kept,
    x_out, bc_out, s_out, d_out, raw_x, raw_s, shift, rim_shift, b_turned,
    *, taps, heads, head_width, first_lane,
):
    step = pl.program_id(0)
    half, width = x.shape
    rims = rim_x.shape[0]
    state_width = bc_out.shape[1] // 2

    def mixed(raw, own, got, rim, late, weight, offset, out):
        raw[:rims, :] = jnp.where(meta[0] == 0, rim[...], late[...])
        raw[pl.ds(pl.multiple_of(rims + meta[0] * half, 16), half), :] = own[...]
        raw[pl.ds(pl.multiple_of(rims + (1 - meta[0]) * half, 16), half), :] = got[...]
        for index in range(2):
            low = index * half

            def store(at, rows, value, low=low):
                out[low + rows.start : low + rows.stop, at] = value

            shifts = [(shift.at[index, back], rim_shift.at[index, back]) for back in range(taps - 1)]
            convolved(
                shifts, raw.at[low + rims : low + rims + half], raw.at[low : low + rims], weight, offset, store, taps
            )

    @pl.when(step == 0)
    def _():
        row = lax.broadcasted_iota(jnp.int32, (half, half), 0)
        col = lax.broadcasted_iota(jnp.int32, (half, half), 1)
        rim_row = lax.broadcasted_iota(jnp.int32, (rims, rims), 0)
        rim_col = lax.broadcasted_iota(jnp.int32, (rims, rims), 1) - rims
        for index in range(2):
            first = meta[1] + index * half
            start = doc_start(rows_of(half, first), docs) - first
            for back in range(1, taps):
                hit = (col == row - back) & (col >= start)
                rim_hit = (rim_col == rim_row - back) & (rim_col >= start[:rims])
                shift[index, back - 1] = jnp.where(hit, 1.0, 0.0).astype(BF16)
                rim_shift[index, back - 1] = jnp.where(rim_hit, 1.0, 0.0).astype(BF16)
        mixed(raw_s, s, got_s, rim_s, late_rim_s, sw, sbias, bc_out)
        b_turned[...] = bc_out[:, :state_width].T

    mixed(raw_x, x, got_x, rim_x, late_rim_x, w, bias, x_out)
    lanes = first_lane + step * width
    tails = mm(tail[...], head_lanes(2, heads, head_width, width, lanes))
    weighted = (x_out[...].astype(F32) * tails).astype(BF16)
    s_out[...] = mm(b_turned[...], weighted).astype(BF16)
    d_out[...] = mm(kept[...], head_lanes(3, heads, head_width, width, lanes))[:1]


def intra_kernel(
    meta, docs, x_all, bc_all, cum_all, dlt_all, gate_own, gate_got, gain,
    a_out, f_out, state, spread, gates, kept_part,
    *, head_width, first_head, group_heads,
):
    total, width = x_all.shape
    heads = cum_all.shape[1]
    count = CHUNK
    splits = total // 2 // count
    state_width = bc_all.shape[1] // 2
    state[...] = jnp.zeros_like(state)
    spread[...] = head_lanes(3, heads, head_width, width, first_head * head_width)
    mine = jnp.where(meta[0] == 0, gain[:, :heads], gain[:, heads:])
    skip = mm(jnp.concatenate(split3(jnp.broadcast_to(mine, (8, heads))), axis=1), spread[...])[:1]
    row = lax.broadcasted_iota(jnp.int32, (count, count), 0)
    col = lax.broadcasted_iota(jnp.int32, (count, count), 1)
    low_lanes = lax.broadcasted_iota(jnp.int32, (count, 2 * head_width), 1) < head_width
    zero = jnp.zeros((count, 2 * head_width), BF16)

    def spread_over(value):
        return mm(jnp.concatenate(split2(value), axis=1), spread[: 2 * heads])

    def chunk(step, before):
        first = meta[1] + step * count
        rows = pl.ds(pl.multiple_of(step * count, count), count)
        half_rows = pl.ds(pl.multiple_of(lax.rem(step, splits) * count, count), count)
        starts = doc_start(rows_of(count, first), docs)
        last_start = doc_start(first + count - 1, docs)
        here = cum_all[rows, :]
        dlt = dlt_all[:, rows]
        x = x_all[rows, :]
        end = here[count - 1 :]
        b = bc_all[rows, :state_width]
        c = bc_all[rows, state_width:]
        scores = jnp.where((col <= row) & (col >= starts - first), contract_lanes(c, b), 0.0)
        reach = spread_over(jnp.where(starts < first, jnp.exp2(here - before), 0.0))
        into = spread_over(jnp.where(starts < meta[1], jnp.exp2(here), 0.0))
        to_end = jnp.exp2(end - dlt.T)
        tail = spread_over(jnp.where(rows_of(count, first) >= last_start, to_end, 0.0))
        kept = jnp.broadcast_to(jnp.where(last_start < first, jnp.exp2(end - before), 0.0), (8, heads))
        kept = mm(jnp.concatenate(split3(kept), axis=1), spread[...])[:1]
        is_own = step // splits == meta[0]
        gate = silu(jnp.where(is_own, gate_own[half_rows, :], gate_got[half_rows, :]).astype(F32))
        gates[...] = gate
        f_out[rows, :] = gate * into
        x_part = x.astype(F32)
        old = state[...]
        kept_part[...] = mm(c, old.astype(BF16)) * reach + x_part * skip
        state[...] = old * kept + mm(b.T, (x_part * tail).astype(BF16))
        for head in range(0, group_heads, 2):
            at = slice(head * head_width, (head + 2) * head_width)
            pair = []
            for k in (first_head + head, first_head + head + 1):
                exponent = jnp.minimum(here[:, k : k + 1] - dlt[k : k + 1, :], CEILING)
                pair.append((jnp.exp2(exponent) * scores).astype(BF16))
            value = x[:, at]
            stacked = jnp.concatenate(
                [jnp.where(low_lanes, value, zero), jnp.where(low_lanes, zero, value)], axis=0
            )
            within = mm(jnp.concatenate(pair, axis=1), stacked)
            a_out[rows, at] = (within + kept_part[:, at]) * gates[:, at]
        return end

    lax.fori_loop(0, total // count, chunk, jnp.zeros((1, heads), F32))


def normed(a, f, bc, incoming, gain, squares, divisor):
    state_width = bc.shape[1] // 2
    gated = a[...] + mm(bc[:, state_width:], incoming[...]) * f[...]
    total = jnp.sum(gated * gated, axis=1, keepdims=True) if squares is None else squares[...]
    return (gated * lax.rsqrt(total / divisor + EPSILON) * gain[...]).astype(BF16)


def norm_kernel(meta, a, f, bc, incoming, gain, hidden, *, divisor):
    hidden[...] = normed(a, f, bc, incoming, gain, None, divisor)


def project_kernel(meta, *refs, ready, squared, divisor):
    a, f, bc, incoming, gain = refs[ready : ready + 5]
    w, hidden, send, keep = refs[-4:]
    width = a.shape[1]

    @pl.when(pl.program_id(0) == 0)
    def _():
        for group, part in enumerate(refs[:ready]):
            hidden[:, group * width : (group + 1) * width] = part[...]
        squares = refs[ready + 5] if squared else None
        hidden[:, ready * width :] = normed(a, f, bc, incoming, gain, squares, divisor)

    multiply(meta, hidden, w, send, keep)


def multiply(meta, hidden, w, send, keep):
    half = send.shape[0]
    there = pl.ds(pl.multiple_of((1 - meta[0]) * half, half), half)
    here = pl.ds(pl.multiple_of(meta[0] * half, half), half)
    send[...] = mm(hidden[there, :], w[...]).astype(BF16)
    keep[...] = mm(hidden[here, :], w[...])


def sum_kernel(*refs):
    out = refs[-1]
    total = refs[0][...]
    for ref in refs[1:-1]:
        if ref.shape == out.shape:
            total = total + ref[...].astype(F32)
    out[...] = total.astype(out.dtype)


def local(
    x_input, gate_input, state_proj, mix_weight, mix_bias, state_weight, state_bias,
    step_raw, decay_log, skip_gain, norm_gain, out_weight, doc_lengths,
):
    half, channels = x_input.shape
    all_heads = step_raw.shape[1]
    groups, _, state_width = state_proj.shape[1:]
    taps = mix_weight.shape[0]
    features = out_weight.shape[1]
    head_width = channels // all_heads
    heads = all_heads // 2
    width = channels // 2
    count = 2 * half
    whole_groups = groups % 2 == 0
    parts = groups // 2 if whole_groups else groups
    part_heads = heads // parts
    part_width = part_heads * head_width
    block = 2 * state_width
    sub = lax.axis_index("sub").astype(jnp.int32)
    ctx = lax.axis_index("ctx").astype(jnp.int32)
    tp = lax.axis_index("tp").astype(jnp.int32)
    tp_size = lax.axis_size("tp")
    ctx_size = lax.axis_size("ctx")
    docs = doc_lengths.astype(jnp.int32)
    meta = jnp.stack([sub, ctx * count, tp])
    params = pltpu.CompilerParams(vmem_limit_bytes=VMEM)
    fixed = lambda *shape: pl.BlockSpec(shape, lambda i, *m: (0,) * len(shape))
    shape_of = jax.ShapeDtypeStruct

    def call(body, name, grid, in_specs, out_specs, out_shape, scratch=(), prefetch=2):
        kernel = pl.pallas_call(
            body,
            grid_spec=pltpu.PrefetchScalarGridSpec(
                num_scalar_prefetch=prefetch, grid=grid, in_specs=in_specs, out_specs=out_specs,
                scratch_shapes=list(scratch),
            ),
            out_shape=out_shape,
            compiler_params=params,
            cost_estimate=pl.CostEstimate(flops=0, bytes_accessed=0, transcendentals=0),
            name=name,
        )
        return lambda *operands: kernel(
            *(pltpu.with_memory_space_constraint(v, pltpu.HBM) if any(v is p for p in pinned) else v for v in operands)
        )

    s_input = state_proj.reshape(half, groups * block)
    s_bias = state_bias.reshape(1, groups * block)
    bias = mix_bias.reshape(1, channels)
    skip = skip_gain.reshape(1, all_heads)
    gain = norm_gain.reshape(1, channels)
    rate = decay_log.reshape(1, all_heads)
    pinned = [
        meta, docs, x_input, gate_input, mix_weight, bias, state_weight, s_bias, skip, gain, rate, out_weight
    ]
    rims = 16
    cut_width = min(1024, part_width)
    cuts = part_width // cut_width
    s_width = parts * block if whole_groups else groups * block
    raw = step_raw.T
    pinned.append(raw)
    last_x, last_s = x_input[half - rims :], state_proj[half - rims :].reshape(rims, groups * block)
    early_rows = jnp.concatenate([last_x[:, :width], last_s[:, :s_width]], axis=1)
    late_rows = jnp.concatenate([last_x[:, width:], last_s[:, -s_width:]], axis=1)
    got_raw, early_rows, late_rows, x_later, gate_later = after(
        swapped(raw, "sub"), early_rows, late_rows, x_input, gate_input
    )
    rim = shifted_ring(early_rows, ("ctx", "sub"))
    late_rim = shifted_ring(late_rows, "ctx")
    got_x = swapped(x_later, "sub")
    got_s = swapped(s_input, "sub")
    got_gate = swapped(gate_later, "sub")
    mixed = (x_input, got_x, rim, late_rim, mix_weight, bias, s_input, got_s, rim, late_rim, state_weight, s_bias)

    def mix_specs(part):
        at = lambda m: m[0] * parts + part
        s_at = at if whole_groups else (lambda m: 0)
        here = lambda m: part
        rim_at = lambda m: width // block + part
        specs = []
        x_at = lambda m, i: at(m) * cuts + i
        x_here = lambda m, i: here(m) * cuts + i
        specs = []
        for rows, place in zip((half, half, rims, rims, taps, 1), (x_at, x_at, x_here, x_here, x_at, x_at)):
            specs.append(pl.BlockSpec((rows, cut_width), lambda i, m, d, place=place: (0, place(m, i))))
        for rows, place in zip((half, half, rims, rims, taps, 1), (s_at, s_at, rim_at, rim_at, s_at, s_at)):
            specs.append(pl.BlockSpec((rows, block), lambda i, m, d, place=place: (0, place(m))))
        specs[10] = pl.BlockSpec((taps, 1, 2, state_width), lambda i, m, d: (0, s_at(m), 0, 0))
        return specs

    cum, dlt, tail, kept = call(
        decay_kernel, "decay", (1,),
        [fixed(all_heads, half), fixed(all_heads, half), fixed(1, all_heads)],
        [fixed(count, heads), fixed(heads, count), fixed(count, 2 * heads), fixed(8, 3 * heads)],
        [
            shape_of((count, heads), F32), shape_of((heads, count), F32),
            shape_of((count, 2 * heads), BF16), shape_of((8, 3 * heads), BF16),
        ],
        [pltpu.VMEM((heads, count), F32)],
    )(meta, docs, raw, got_raw, rate)

    made = []
    next_meta = meta
    for part in range(parts):
        x_cat, bc, state, decay = call(
            functools.partial(
                state_kernel, taps=taps, heads=heads, head_width=head_width, first_lane=part * part_width
            ),
            "state", (cuts,),
            mix_specs(part) + [fixed(count, 2 * heads), fixed(8, 3 * heads)],
            [
                pl.BlockSpec((count, cut_width), lambda i, m, d: (0, i)), fixed(count, block),
                pl.BlockSpec((state_width, cut_width), lambda i, m, d: (0, i)),
                pl.BlockSpec((1, cut_width), lambda i, m, d: (0, i)),
            ],
            [
                shape_of((count, part_width), BF16), shape_of((count, block), BF16),
                shape_of((state_width, part_width), BF16), shape_of((1, part_width), F32),
            ],
            [
                pltpu.VMEM((rims + count, cut_width), BF16), pltpu.VMEM((rims + count, block), BF16),
                pltpu.VMEM((2, taps - 1, half, half), BF16), pltpu.VMEM((2, taps - 1, rims, rims), BF16),
                pltpu.VMEM((state_width, count), BF16),
            ],
        )(next_meta, docs, *mixed, tail, kept)
        state, next_meta = after(state, next_meta)
        pinned.append(next_meta)
        made.append([x_cat, bc, state, decay, shifted_ring(state, "ctx")])
        if part:
            made[part - 1][4], made[part][0] = after(made[part - 1][4], x_cat)
    ready = []
    for part in range(parts):
        x_cat, bc, state, decay, arriving = made[part]
        if ready:
            arriving, gate = after(arriving, ready[-1][0])
            ready[-1] = (gate, *ready[-1][1:])
        for _ in range(ctx_size // 2 - 1):
            leaving = (state.astype(F32) + decay * arriving.astype(F32)).astype(BF16)
            leaving, x_cat = after(leaving, x_cat)
            arriving = shifted_ring(leaving, "ctx")
        gated, carry_gate = call(
            functools.partial(
                intra_kernel, head_width=head_width, first_head=part * part_heads, group_heads=part_heads
            ),
            "intra", (1,),
            [
                fixed(count, part_width), fixed(count, block), fixed(count, heads), fixed(heads, count),
                pl.BlockSpec((half, part_width), lambda i, m, d, part=part: (0, m[0] * parts + part)),
                pl.BlockSpec((half, part_width), lambda i, m, d, part=part: (0, m[0] * parts + part)),
                fixed(1, all_heads),
            ],
            [fixed(count, part_width), fixed(count, part_width)],
            [shape_of((count, part_width), F32)] * 2,
            [
                pltpu.VMEM((state_width, part_width), F32), pltpu.VMEM((3 * heads, part_width), BF16),
                pltpu.VMEM((CHUNK, part_width), F32), pltpu.VMEM((CHUNK, part_width), F32),
            ],
        )(meta, docs, x_cat, bc, cum, dlt, gate_input, got_gate, skip)
        ready.append((gated, carry_gate, bc, arriving))

    divisor = HEADS // GROUPS * head_width
    gain_at = lambda part: pl.BlockSpec((1, part_width), lambda i, m: (0, m[0] * parts + part))
    hiddens = []
    for part, (gated, carry_gate, bc, arriving) in enumerate(ready[:-1]):
        hiddens.append(
            call(
                functools.partial(norm_kernel, divisor=divisor), "norm", (1,),
                [
                    fixed(count, part_width), fixed(count, part_width), fixed(count, block),
                    fixed(state_width, part_width), gain_at(part),
                ],
                fixed(count, part_width), shape_of((count, part_width), BF16),
                prefetch=1,
            )(meta, gated, carry_gate, bc, arriving, gain)
        )

    gated, carry_gate, bc, arriving = ready[-1]
    if hiddens:
        arriving, hiddens[-1] = after(arriving, hiddens[-1])
    squares = []
    if not whole_groups:
        total = gated + jnp.dot(bc[:, state_width:], arriving, preferred_element_type=F32) * carry_gate
        mine = jnp.sum(total * total, axis=1, keepdims=True)
        squares = [mine + swapped(mine, "sub")]
    out_cols = features // tp_size
    mm_cols = min(512, out_cols)
    pair = tp_size == 2
    near_blocks = out_cols // mm_cols
    row_specs = [pl.BlockSpec((half, mm_cols), lambda i, m: (0, i))] * 2

    def product(first, blocks, body, name, operands, specs, outs, out_shapes):
        cols = blocks * mm_cols
        return call(
            body, name, (blocks,),
            specs + [pl.BlockSpec((width, mm_cols), lambda i, m: (0, first(m, i)))],
            outs + row_specs,
            out_shapes + [shape_of((half, cols), BF16), shape_of((half, cols), F32)],
            prefetch=1,
        )(meta, *operands, out_weight)

    operands = [*hiddens, gated, carry_gate, bc, arriving, gain, *squares]
    specs = [fixed(*v.shape) for v in operands]
    specs[len(hiddens) + 4] = gain_at(parts - 1)
    project = functools.partial(project_kernel, ready=len(hiddens), squared=len(squares), divisor=divisor)
    hidden_spec, hidden_shape = fixed(count, width), shape_of((count, width), BF16)
    if not pair:
        every = features // mm_cols
        _, send, keep = product(lambda m, i: i, every, project, "project", operands, specs, [hidden_spec], [hidden_shape])
        summed = (keep + swapped(send, "sub").astype(F32)).astype(BF16)
        return lax.psum_scatter(summed, "tp", scatter_dimension=1, tiled=True)
    lead = max(3 * near_blocks // 4, 1)
    far_first = lambda m: (1 - m[2]) * near_blocks
    hidden, send, keep = product(
        lambda m, i: far_first(m) + i, lead, project, "project", operands, specs, [hidden_spec], [hidden_shape]
    )
    summed = (keep + swapped(send, "sub").astype(F32)).astype(BF16)
    hidden, summed = after(hidden, summed)
    far_lead = swapped(summed, "tp")
    rest = near_blocks - lead
    send, keep = product(
        lambda m, i: far_first(m) + lead + i, rest, multiply, "product", [hidden], [hidden_spec], [], []
    )
    summed = (keep + swapped(send, "sub").astype(F32)).astype(BF16)
    hidden, summed = after(hidden, summed)
    far_rest = swapped(summed, "tp")
    send, keep = product(
        lambda m, i: m[2] * near_blocks + i, near_blocks, multiply, "product", [hidden], [hidden_spec], [], [],
    )
    got = swapped(send, "sub")

    def finish(first, terms, name, dtype, old=(), weight=0):
        blocks = min(v.shape[1] for v in terms) // mm_cols
        at = lambda v: (lambda i: (0, i + (first if v.shape[1] == out_cols else 0)))
        cols = out_cols if dtype == BF16 else blocks * mm_cols
        return pl.pallas_call(
            sum_kernel, grid=(blocks,),
            in_specs=[pl.BlockSpec((half, mm_cols), at(v)) for v in terms]
            + [pl.BlockSpec(memory_space=pl.ANY)] * len(old),
            out_specs=pl.BlockSpec((half, mm_cols), lambda i: (0, i + (first if dtype == BF16 else 0))),
            out_shape=shape_of((half, cols), dtype),
            input_output_aliases={len(terms): 0} if old else {},
            compiler_params=params,
            cost_estimate=pl.CostEstimate(flops=weight, bytes_accessed=0, transcendentals=0),
            name=name,
        )(*terms, *old)

    early = finish(0, [keep, far_lead], "early", F32, weight=1 << 38)
    output = finish(0, [early, got], "lead", BF16)
    cut = lead * mm_cols
    last = (keep[:, cut:] + got[:, cut:].astype(F32) + far_rest.astype(F32)).astype(BF16)
    return lax.dynamic_update_slice(output, last, (0, cut))


def solution(mesh):
    in_specs = (
        P(("groups", "ctx", "sub"), "tp"),
        P(("groups", "ctx", "sub"), "tp"),
        P(("groups", "ctx", "sub"), "tp", None, None),
        P(None, "tp"),
        P("tp"),
        P(None, "tp", None, None),
        P("tp", None, None),
        P(("groups", "ctx", "sub"), "tp"),
        P("tp"),
        P("tp"),
        P("tp"),
        P(("tp", "sub"), None),
        P("groups"),
    )
    out_specs = P(("groups", "ctx", "sub"), "tp")
    return jax.shard_map(local, mesh=mesh, in_specs=in_specs, out_specs=out_specs, check_vma=False)
```

```python
import functools

import jax
import jax.numpy as jnp
from jax import lax
from jax.experimental import pallas as pl
from jax.experimental.pallas import tpu as pltpu
from jax.sharding import PartitionSpec as P

HEADS = 128
GROUPS = 8
CHUNK = 128
EPSILON = 1e-05
LOG2E = 1.4426950408889634
CEILING = 126.0
VMEM = 20 << 20
F32 = jnp.float32
BF16 = jnp.bfloat16


def shifted_ring(shard, axis):
    peers = lax.axis_size(axis)
    return lax.ppermute(shard, axis, [(i, (i + 1) % peers) for i in range(peers)])


def swapped(shard, axis):
    return lax.ppermute(shard, axis, [(i, i ^ 1) for i in range(lax.axis_size(axis))])


def after(*values):
    return lax.optimization_barrier(values)


def doc_start(positions, docs_ref):
    start = jnp.zeros_like(positions)
    total = jnp.int32(0)
    for doc in range(docs_ref.shape[0]):
        start = jnp.where(positions >= total, total, start)
        total = total + docs_ref[doc]
    return start


def rows_of(count, first):
    return first + lax.broadcasted_iota(jnp.int32, (count, 1), 0)


def split2(value):
    high = value.astype(BF16)
    return high, (value - high.astype(F32)).astype(BF16)


def split3(value):
    high = value.astype(BF16)
    rest = value - high.astype(F32)
    mid = rest.astype(BF16)
    return high, mid, (rest - mid.astype(F32)).astype(BF16)


def mm(a, b):
    return jnp.dot(a, b, preferred_element_type=F32)


def contract_lanes(a, b):
    return lax.dot_general(a, b, (((1,), (1,)), ((), ())), preferred_element_type=F32)


def silu(value):
    half = 0.5 * value
    return half + half * jnp.tanh(half)


def head_lanes(copies, heads, head_width, lanes, first_lane):
    shape = (copies * heads, lanes)
    head = lax.broadcasted_iota(jnp.int32, shape, 0)
    for copy in range(1, copies):
        head = jnp.where(head >= heads, head - heads, head)
    lane = first_lane + lax.broadcasted_iota(jnp.int32, shape, 1)
    low = head * head_width
    return jnp.where((lane >= low) & (lane < low + head_width), 1.0, 0.0).astype(BF16)


def convolved(shifts, x, rim, w, bias, store, taps):
    count = x.shape[0]
    rims = rim.shape[0]
    weights = w[...].astype(F32)
    if len(weights.shape) == 4:
        weights = jnp.concatenate([weights[:, 0, 0, :], weights[:, 0, 1, :]], axis=1)
    span = min(256, x.shape[1])
    for low in range(0, x.shape[1], span):
        at = slice(low, low + span)
        value = x[:, at]
        weight = weights[:, at]
        summed = bias[:, at] + value.astype(F32) * weight[taps - 1 : taps]
        top = jnp.zeros((rims, span), F32)
        for back in range(1, taps):
            line = weight[taps - 1 - back : taps - back]
            shift, rim_shift = shifts[back - 1]
            summed = summed + mm(shift[...], value) * line
            top = top + mm(rim_shift[...], rim[:, at]) * line
        store(at, slice(0, rims), silu(summed[:rims] + top).astype(BF16))
        store(at, slice(rims, count), silu(summed[rims:]).astype(BF16))


def decay_kernel(
    meta, docs, own_raw, got_raw, rate, cum_out, dlt_out, tail_out, kept_out, raw,
):
    half = own_raw.shape[1]
    heads, count = raw.shape
    mine = meta[0] == 0
    first = meta[1]
    own_at = pl.ds(pl.multiple_of(meta[0] * half, half), half)
    got_at = pl.ds(pl.multiple_of((1 - meta[0]) * half, half), half)
    last_start = doc_start(first + count - 1, docs)
    raw[:, own_at] = jnp.where(mine, own_raw[:heads], own_raw[heads:])
    raw[:, got_at] = jnp.where(mine, got_raw[:heads], got_raw[heads:])
    value = raw[...]
    size = jnp.maximum(value, 0.0) + jnp.log(1.0 + jnp.exp(-jnp.abs(value)))
    wide = (heads, 2 * heads)
    own_head = lax.broadcasted_iota(jnp.int32, wide, 0) + meta[0] * heads
    chosen = own_head == lax.broadcasted_iota(jnp.int32, wide, 1)
    rates = jnp.sum(jnp.where(chosen, rate[...], 0.0), axis=1, keepdims=True)
    decay = (-LOG2E * jnp.exp(rates)) * size
    row = lax.broadcasted_iota(jnp.int32, (count, count), 0)
    col = lax.broadcasted_iota(jnp.int32, (count, count), 1)
    above = jnp.where(row <= col, 1.0, 0.0).astype(BF16)
    high, mid, low = split3(decay)
    cum = mm(high, above) + (mm(mid, above) + mm(low, above))
    dlt_out[...] = cum - jnp.log2(size)
    end = cum[:, count - 1 :]
    places = first + lax.broadcasted_iota(jnp.int32, (1, count), 1)
    tail = jnp.where(places >= last_start, size * jnp.exp2(end - cum), 0.0)
    high, low = split2(tail.T)
    tail_out[:, :heads] = high
    tail_out[:, heads:] = low
    cum = cum.T
    cum_out[...] = cum
    kept = jnp.exp2(jnp.broadcast_to(cum[count - 1 :], (8, heads)))
    high, mid, low = split3(jnp.where(last_start < first, kept, 0.0))
    kept_out[:, :heads] = high
    kept_out[:, heads : 2 * heads] = mid
    kept_out[:, 2 * heads :] = low


def state_kernel(
    meta, docs, x, got_x, rim_x, late_rim_x, w, bias, s, got_s, rim_s, late_rim_s, sw, sbias, tail, kept,
    x_out, bc_out, s_out, d_out, raw_x, raw_s, shift, rim_shift, b_turned,
    *, taps, heads, head_width, first_lane,
):
    step = pl.program_id(0)
    half, width = x.shape
    rims = rim_x.shape[0]
    state_width = bc_out.shape[1] // 2

    def mixed(raw, own, got, rim, late, weight, offset, out):
        raw[:rims, :] = jnp.where(meta[0] == 0, rim[...], late[...])
        raw[pl.ds(pl.multiple_of(rims + meta[0] * half, 16), half), :] = own[...]
        raw[pl.ds(pl.multiple_of(rims + (1 - meta[0]) * half, 16), half), :] = got[...]
        for index in range(2):
            low = index * half

            def store(at, rows, value, low=low):
                out[low + rows.start : low + rows.stop, at] = value

            shifts = [(shift.at[index, back], rim_shift.at[index, back]) for back in range(taps - 1)]
            convolved(
                shifts, raw.at[low + rims : low + rims + half], raw.at[low : low + rims], weight, offset, store, taps
            )

    @pl.when(step == 0)
    def _():
        row = lax.broadcasted_iota(jnp.int32, (half, half), 0)
        col = lax.broadcasted_iota(jnp.int32, (half, half), 1)
        rim_row = lax.broadcasted_iota(jnp.int32, (rims, rims), 0)
        rim_col = lax.broadcasted_iota(jnp.int32, (rims, rims), 1) - rims
        for index in range(2):
            first = meta[1] + index * half
            start = doc_start(rows_of(half, first), docs) - first
            for back in range(1, taps):
                hit = (col == row - back) & (col >= start)
                rim_hit = (rim_col == rim_row - back) & (rim_col >= start[:rims])
                shift[index, back - 1] = jnp.where(hit, 1.0, 0.0).astype(BF16)
                rim_shift[index, back - 1] = jnp.where(rim_hit, 1.0, 0.0).astype(BF16)
        mixed(raw_s, s, got_s, rim_s, late_rim_s, sw, sbias, bc_out)
        b_turned[...] = bc_out[:, :state_width].T

    mixed(raw_x, x, got_x, rim_x, late_rim_x, w, bias, x_out)
    lanes = first_lane + step * width
    tails = mm(tail[...], head_lanes(2, heads, head_width, width, lanes))
    weighted = (x_out[...].astype(F32) * tails).astype(BF16)
    s_out[...] = mm(b_turned[...], weighted).astype(BF16)
    d_out[...] = mm(kept[...], head_lanes(3, heads, head_width, width, lanes))[:1]


def intra_kernel(
    meta, docs, x_all, bc_all, cum_all, dlt_all, gate_own, gate_got, gain,
    a_out, f_out, state, spread, gates, kept_part,
    *, head_width, first_head, group_heads,
):
    total, width = x_all.shape
    heads = cum_all.shape[1]
    count = CHUNK
    splits = total // 2 // count
    state_width = bc_all.shape[1] // 2
    state[...] = jnp.zeros_like(state)
    spread[...] = head_lanes(3, heads, head_width, width, first_head * head_width)
    mine = jnp.where(meta[0] == 0, gain[:, :heads], gain[:, heads:])
    skip = mm(jnp.concatenate(split3(jnp.broadcast_to(mine, (8, heads))), axis=1), spread[...])[:1]
    row = lax.broadcasted_iota(jnp.int32, (count, count), 0)
    col = lax.broadcasted_iota(jnp.int32, (count, count), 1)
    low_lanes = lax.broadcasted_iota(jnp.int32, (count, 2 * head_width), 1) < head_width
    zero = jnp.zeros((count, 2 * head_width), BF16)

    def spread_over(value):
        return mm(jnp.concatenate(split2(value), axis=1), spread[: 2 * heads])

    def chunk(step, before):
        first = meta[1] + step * count
        rows = pl.ds(pl.multiple_of(step * count, count), count)
        half_rows = pl.ds(pl.multiple_of(lax.rem(step, splits) * count, count), count)
        starts = doc_start(rows_of(count, first), docs)
        last_start = doc_start(first + count - 1, docs)
        here = cum_all[rows, :]
        dlt = dlt_all[:, rows]
        x = x_all[rows, :]
        end = here[count - 1 :]
        b = bc_all[rows, :state_width]
        c = bc_all[rows, state_width:]
        scores = jnp.where((col <= row) & (col >= starts - first), contract_lanes(c, b), 0.0)
        reach = spread_over(jnp.where(starts < first, jnp.exp2(here - before), 0.0))
        into = spread_over(jnp.where(starts < meta[1], jnp.exp2(here), 0.0))
        to_end = jnp.exp2(end - dlt.T)
        tail = spread_over(jnp.where(rows_of(count, first) >= last_start, to_end, 0.0))
        kept = jnp.broadcast_to(jnp.where(last_start < first, jnp.exp2(end - before), 0.0), (8, heads))
        kept = mm(jnp.concatenate(split3(kept), axis=1), spread[...])[:1]
        is_own = step // splits == meta[0]
        gate = silu(jnp.where(is_own, gate_own[half_rows, :], gate_got[half_rows, :]).astype(F32))
        gates[...] = gate
        f_out[rows, :] = gate * into
        x_part = x.astype(F32)
        old = state[...]
        kept_part[...] = mm(c, old.astype(BF16)) * reach + x_part * skip
        state[...] = old * kept + mm(b.T, (x_part * tail).astype(BF16))
        for head in range(0, group_heads, 2):
            at = slice(head * head_width, (head + 2) * head_width)
            pair = []
            for k in (first_head + head, first_head + head + 1):
                exponent = jnp.minimum(here[:, k : k + 1] - dlt[k : k + 1, :], CEILING)
                pair.append((jnp.exp2(exponent) * scores).astype(BF16))
            value = x[:, at]
            stacked = jnp.concatenate(
                [jnp.where(low_lanes, value, zero), jnp.where(low_lanes, zero, value)], axis=0
            )
            within = mm(jnp.concatenate(pair, axis=1), stacked)
            a_out[rows, at] = (within + kept_part[:, at]) * gates[:, at]
        return end

    lax.fori_loop(0, total // count, chunk, jnp.zeros((1, heads), F32))


def normed(a, f, bc, incoming, gain, squares, divisor):
    state_width = bc.shape[1] // 2
    gated = a[...] + mm(bc[:, state_width:], incoming[...]) * f[...]
    total = jnp.sum(gated * gated, axis=1, keepdims=True) if squares is None else squares[...]
    return (gated * lax.rsqrt(total / divisor + EPSILON) * gain[...]).astype(BF16)


def norm_kernel(meta, a, f, bc, incoming, gain, hidden, *, divisor):
    hidden[...] = normed(a, f, bc, incoming, gain, None, divisor)


def project_kernel(meta, *refs, ready, squared, divisor):
    a, f, bc, incoming, gain = refs[ready : ready + 5]
    w, hidden, send, keep = refs[-4:]
    width = a.shape[1]

    @pl.when(pl.program_id(0) == 0)
    def _():
        for group, part in enumerate(refs[:ready]):
            hidden[:, group * width : (group + 1) * width] = part[...]
        squares = refs[ready + 5] if squared else None
        hidden[:, ready * width :] = normed(a, f, bc, incoming, gain, squares, divisor)

    multiply(meta, hidden, w, send, keep)


def multiply(meta, hidden, w, send, keep):
    half = send.shape[0]
    there = pl.ds(pl.multiple_of((1 - meta[0]) * half, half), half)
    here = pl.ds(pl.multiple_of(meta[0] * half, half), half)
    send[...] = mm(hidden[there, :], w[...]).astype(BF16)
    keep[...] = mm(hidden[here, :], w[...])


def sum_kernel(*refs):
    out = refs[-1]
    total = refs[0][...]
    for ref in refs[1:-1]:
        if ref.shape == out.shape:
            total = total + ref[...].astype(F32)
    out[...] = total.astype(out.dtype)


def local(
    x_input, gate_input, state_proj, mix_weight, mix_bias, state_weight, state_bias,
    step_raw, decay_log, skip_gain, norm_gain, out_weight, doc_lengths,
):
    half, channels = x_input.shape
    all_heads = step_raw.shape[1]
    groups, _, state_width = state_proj.shape[1:]
    taps = mix_weight.shape[0]
    features = out_weight.shape[1]
    head_width = channels // all_heads
    heads = all_heads // 2
    width = channels // 2
    count = 2 * half
    whole_groups = groups % 2 == 0
    parts = groups // 2 if whole_groups else groups
    part_heads = heads // parts
    part_width = part_heads * head_width
    block = 2 * state_width
    sub = lax.axis_index("sub").astype(jnp.int32)
    ctx = lax.axis_index("ctx").astype(jnp.int32)
    tp = lax.axis_index("tp").astype(jnp.int32)
    tp_size = lax.axis_size("tp")
    ctx_size = lax.axis_size("ctx")
    docs = doc_lengths.astype(jnp.int32)
    meta = jnp.stack([sub, ctx * count, tp])
    params = pltpu.CompilerParams(vmem_limit_bytes=VMEM)
    fixed = lambda *shape: pl.BlockSpec(shape, lambda i, *m: (0,) * len(shape))
    shape_of = jax.ShapeDtypeStruct

    def call(body, name, grid, in_specs, out_specs, out_shape, scratch=(), prefetch=2):
        kernel = pl.pallas_call(
            body,
            grid_spec=pltpu.PrefetchScalarGridSpec(
                num_scalar_prefetch=prefetch, grid=grid, in_specs=in_specs, out_specs=out_specs,
                scratch_shapes=list(scratch),
            ),
            out_shape=out_shape,
            compiler_params=params,
            cost_estimate=pl.CostEstimate(flops=0, bytes_accessed=0, transcendentals=0),
            name=name,
        )
        return lambda *operands: kernel(
            *(pltpu.with_memory_space_constraint(v, pltpu.HBM) if any(v is p for p in pinned) else v for v in operands)
        )

    s_input = state_proj.reshape(half, groups * block)
    s_bias = state_bias.reshape(1, groups * block)
    bias = mix_bias.reshape(1, channels)
    skip = skip_gain.reshape(1, all_heads)
    gain = norm_gain.reshape(1, channels)
    rate = decay_log.reshape(1, all_heads)
    pinned = [
        meta, docs, x_input, gate_input, mix_weight, bias, state_weight, s_bias, skip, gain, rate, out_weight
    ]
    rims = 16
    cut_width = min(1024, part_width)
    cuts = part_width // cut_width
    s_width = parts * block if whole_groups else groups * block
    raw = step_raw.T
    pinned.append(raw)
    last_x, last_s = x_input[half - rims :], state_proj[half - rims :].reshape(rims, groups * block)
    early_rows = jnp.concatenate([last_x[:, :width], last_s[:, :s_width]], axis=1)
    late_rows = jnp.concatenate([last_x[:, width:], last_s[:, -s_width:]], axis=1)
    got_raw, early_rows, late_rows, x_later, gate_later = after(
        swapped(raw, "sub"), early_rows, late_rows, x_input, gate_input
    )
    rim = shifted_ring(early_rows, ("ctx", "sub"))
    late_rim = shifted_ring(late_rows, "ctx")
    got_x = swapped(x_later, "sub")
    got_s = swapped(s_input, "sub")
    got_gate = swapped(gate_later, "sub")
    mixed = (x_input, got_x, rim, late_rim, mix_weight, bias, s_input, got_s, rim, late_rim, state_weight, s_bias)

    def mix_specs(part):
        at = lambda m: m[0] * parts + part
        s_at = at if whole_groups else (lambda m: 0)
        here = lambda m: part
        rim_at = lambda m: width // block + part
        specs = []
        x_at = lambda m, i: at(m) * cuts + i
        x_here = lambda m, i: here(m) * cuts + i
        specs = []
        for rows, place in zip((half, half, rims, rims, taps, 1), (x_at, x_at, x_here, x_here, x_at, x_at)):
            specs.append(pl.BlockSpec((rows, cut_width), lambda i, m, d, place=place: (0, place(m, i))))
        for rows, place in zip((half, half, rims, rims, taps, 1), (s_at, s_at, rim_at, rim_at, s_at, s_at)):
            specs.append(pl.BlockSpec((rows, block), lambda i, m, d, place=place: (0, place(m))))
        specs[10] = pl.BlockSpec((taps, 1, 2, state_width), lambda i, m, d: (0, s_at(m), 0, 0))
        return specs

    cum, dlt, tail, kept = call(
        decay_kernel, "decay", (1,),
        [fixed(all_heads, half), fixed(all_heads, half), fixed(1, all_heads)],
        [fixed(count, heads), fixed(heads, count), fixed(count, 2 * heads), fixed(8, 3 * heads)],
        [
            shape_of((count, heads), F32), shape_of((heads, count), F32),
            shape_of((count, 2 * heads), BF16), shape_of((8, 3 * heads), BF16),
        ],
        [pltpu.VMEM((heads, count), F32)],
    )(meta, docs, raw, got_raw, rate)

    made = []
    next_meta = meta
    for part in range(parts):
        x_cat, bc, state, decay = call(
            functools.partial(
                state_kernel, taps=taps, heads=heads, head_width=head_width, first_lane=part * part_width
            ),
            "state", (cuts,),
            mix_specs(part) + [fixed(count, 2 * heads), fixed(8, 3 * heads)],
            [
                pl.BlockSpec((count, cut_width), lambda i, m, d: (0, i)), fixed(count, block),
                pl.BlockSpec((state_width, cut_width), lambda i, m, d: (0, i)),
                pl.BlockSpec((1, cut_width), lambda i, m, d: (0, i)),
            ],
            [
                shape_of((count, part_width), BF16), shape_of((count, block), BF16),
                shape_of((state_width, part_width), BF16), shape_of((1, part_width), F32),
            ],
            [
                pltpu.VMEM((rims + count, cut_width), BF16), pltpu.VMEM((rims + count, block), BF16),
                pltpu.VMEM((2, taps - 1, half, half), BF16), pltpu.VMEM((2, taps - 1, rims, rims), BF16),
                pltpu.VMEM((state_width, count), BF16),
            ],
        )(next_meta, docs, *mixed, tail, kept)
        state, next_meta = after(state, next_meta)
        pinned.append(next_meta)
        made.append([x_cat, bc, state, decay, shifted_ring(state, "ctx")])
        if part:
            made[part - 1][4], made[part][0] = after(made[part - 1][4], x_cat)
    ready = []
    for part in range(parts):
        x_cat, bc, state, decay, arriving = made[part]
        if ready:
            arriving, gate = after(arriving, ready[-1][0])
            ready[-1] = (gate, *ready[-1][1:])
        for _ in range(ctx_size // 2 - 1):
            leaving = (state.astype(F32) + decay * arriving.astype(F32)).astype(BF16)
            leaving, x_cat = after(leaving, x_cat)
            arriving = shifted_ring(leaving, "ctx")
        gated, carry_gate = call(
            functools.partial(
                intra_kernel, head_width=head_width, first_head=part * part_heads, group_heads=part_heads
            ),
            "intra", (1,),
            [
                fixed(count, part_width), fixed(count, block), fixed(count, heads), fixed(heads, count),
                pl.BlockSpec((half, part_width), lambda i, m, d, part=part: (0, m[0] * parts + part)),
                pl.BlockSpec((half, part_width), lambda i, m, d, part=part: (0, m[0] * parts + part)),
                fixed(1, all_heads),
            ],
            [fixed(count, part_width), fixed(count, part_width)],
            [shape_of((count, part_width), F32)] * 2,
            [
                pltpu.VMEM((state_width, part_width), F32), pltpu.VMEM((3 * heads, part_width), BF16),
                pltpu.VMEM((CHUNK, part_width), F32), pltpu.VMEM((CHUNK, part_width), F32),
            ],
        )(meta, docs, x_cat, bc, cum, dlt, gate_input, got_gate, skip)
        ready.append((gated, carry_gate, bc, arriving))

    divisor = HEADS // GROUPS * head_width
    gain_at = lambda part: pl.BlockSpec((1, part_width), lambda i, m: (0, m[0] * parts + part))
    hiddens = []
    for part, (gated, carry_gate, bc, arriving) in enumerate(ready[:-1]):
        hiddens.append(
            call(
                functools.partial(norm_kernel, divisor=divisor), "norm", (1,),
                [
                    fixed(count, part_width), fixed(count, part_width), fixed(count, block),
                    fixed(state_width, part_width), gain_at(part),
                ],
                fixed(count, part_width), shape_of((count, part_width), BF16),
                prefetch=1,
            )(meta, gated, carry_gate, bc, arriving, gain)
        )

    gated, carry_gate, bc, arriving = ready[-1]
    if hiddens:
        arriving, hiddens[-1] = after(arriving, hiddens[-1])
    squares = []
    if not whole_groups:
        total = gated + jnp.dot(bc[:, state_width:], arriving, preferred_element_type=F32) * carry_gate
        mine = jnp.sum(total * total, axis=1, keepdims=True)
        squares = [mine + swapped(mine, "sub")]
    out_cols = features // tp_size
    mm_cols = min(512, out_cols)
    pair = tp_size == 2
    near_blocks = out_cols // mm_cols
    row_specs = [pl.BlockSpec((half, mm_cols), lambda i, m: (0, i))] * 2

    def product(first, blocks, body, name, operands, specs, outs, out_shapes):
        cols = blocks * mm_cols
        return call(
            body, name, (blocks,),
            specs + [pl.BlockSpec((width, mm_cols), lambda i, m: (0, first(m, i)))],
            outs + row_specs,
            out_shapes + [shape_of((half, cols), BF16), shape_of((half, cols), F32)],
            prefetch=1,
        )(meta, *operands, out_weight)

    operands = [*hiddens, gated, carry_gate, bc, arriving, gain, *squares]
    specs = [fixed(*v.shape) for v in operands]
    specs[len(hiddens) + 4] = gain_at(parts - 1)
    project = functools.partial(project_kernel, ready=len(hiddens), squared=len(squares), divisor=divisor)
    hidden_spec, hidden_shape = fixed(count, width), shape_of((count, width), BF16)
    if not pair:
        every = features // mm_cols
        _, send, keep = product(lambda m, i: i, every, project, "project", operands, specs, [hidden_spec], [hidden_shape])
        summed = (keep + swapped(send, "sub").astype(F32)).astype(BF16)
        return lax.psum_scatter(summed, "tp", scatter_dimension=1, tiled=True)
    lead = max(3 * near_blocks // 4, 1)
    far_first = lambda m: (1 - m[2]) * near_blocks
    hidden, send, keep = product(
        lambda m, i: far_first(m) + i, lead, project, "project", operands, specs, [hidden_spec], [hidden_shape]
    )
    summed = (keep + swapped(send, "sub").astype(F32)).astype(BF16)
    hidden, summed = after(hidden, summed)
    far_lead = swapped(summed, "tp")
    rest = near_blocks - lead
    send, keep = product(
        lambda m, i: far_first(m) + lead + i, rest, multiply, "product", [hidden], [hidden_spec], [], []
    )
    summed = (keep + swapped(send, "sub").astype(F32)).astype(BF16)
    hidden, summed = after(hidden, summed)
    far_rest = swapped(summed, "tp")
    send, keep = product(
        lambda m, i: m[2] * near_blocks + i, near_blocks, multiply, "product", [hidden], [hidden_spec], [], [],
    )
    got = swapped(send, "sub")

    def finish(first, terms, name, dtype, old=(), weight=0):
        blocks = min(v.shape[1] for v in terms) // mm_cols
        at = lambda v: (lambda i: (0, i + (first if v.shape[1] == out_cols else 0)))
        cols = out_cols if dtype == BF16 else blocks * mm_cols
        return pl.pallas_call(
            sum_kernel, grid=(blocks,),
            in_specs=[pl.BlockSpec((half, mm_cols), at(v)) for v in terms]
            + [pl.BlockSpec(memory_space=pl.ANY)] * len(old),
            out_specs=pl.BlockSpec((half, mm_cols), lambda i: (0, i + (first if dtype == BF16 else 0))),
            out_shape=shape_of((half, cols), dtype),
            input_output_aliases={len(terms): 0} if old else {},
            compiler_params=params,
            cost_estimate=pl.CostEstimate(flops=weight, bytes_accessed=0, transcendentals=0),
            name=name,
        )(*terms, *old)

    early = finish(0, [keep, far_lead], "early", F32, weight=1 << 38)
    output = finish(0, [early, got], "lead", BF16)
    cut = lead * mm_cols
    last = (keep[:, cut:] + got[:, cut:].astype(F32) + far_rest.astype(F32)).astype(BF16)
    return lax.dynamic_update_slice(output, last, (0, cut))


def solution(mesh):
    in_specs = (
        P(("groups", "ctx", "sub"), "tp"),
        P(("groups", "ctx", "sub"), "tp"),
        P(("groups", "ctx", "sub"), "tp", None, None),
        P(None, "tp"),
        P("tp"),
        P(None, "tp", None, None),
        P("tp", None, None),
        P(("groups", "ctx", "sub"), "tp"),
        P("tp"),
        P("tp"),
        P("tp"),
        P(("tp", "sub"), None),
        P("groups"),
    )
    out_specs = P(("groups", "ctx", "sub"), "tp")
    return jax.shard_map(local, mesh=mesh, in_specs=in_specs, out_specs=out_specs, check_vma=False)
```
